32 devices in a mesh: groups: 2 (over x), expert: 16 (over z, y, core).
Axes of the slice: x: 2, y: 2, z: 4, core: 2. Of those that a mesh axis runs over, the one named last changes fastest.
Arguments:
- tokens_in: bfloat16 [4096, 1024], P(('groups', 'expert')), parts along dimension 0, may hold values from -6 to 6
- grad_out: bfloat16 [4096, 1024], P(('groups', 'expert')), parts along dimension 0, may hold values from -6 to 6
- gates: bfloat16 [4096, 8], P(('groups', 'expert')), parts along dimension 0, may hold values from 0.049804688 to 0.5
- expert_ids: int32 [4096, 8], P(('groups', 'expert')), parts along dimension 0, may hold values from 0 to 15, as said below
- replica_table: int32 [32], P('groups'), parts along dimension 0, may hold values from 0 to 15, as said below
- w_gate: bfloat16 [16, 1024, 384], P('expert'), may hold values from -0.1875 to 0.1875
- w_up: bfloat16 [16, 1024, 384], P('expert'), may hold values from -0.1875 to 0.1875
- w_down: bfloat16 [16, 384, 1024], P('expert'), may hold values from -0.3125 to 0.3125
Outputs:
- grad_tokens: bfloat16 [4096, 1024], P(('groups', 'expert')), parts along dimension 0
- grad_gates: bfloat16 [4096, 8], P(('groups', 'expert')), parts along dimension 0
- grad_w_gate: bfloat16 [32, 1024, 384], P(('groups', 'expert')), parts along dimension 0
- grad_w_up: bfloat16 [32, 1024, 384], P(('groups', 'expert')), parts along dimension 0
- grad_w_down: bfloat16 [32, 384, 1024], P(('groups', 'expert')), parts along dimension 0
The draws below stay inside these ranges and needn't reach their ends.
There are 2 independent parts, one for each index of `groups`. The reference program is written for one: setup_inputs(seed, part) draws one part's arguments, and reference() takes and returns one part's arrays. A program takes and returns all parts, laid end to end along the dimension named above; an argument that names none is the same for every part. Nothing has to cross between parts.
Inputs may be any that keep to these rules, and one draw needn't show every extreme that they name: `expert_ids`: each row names 8 different experts. `replica_table`: entry d is the expert whose weights device d holds in its replica slot.
All inputs are finite; a program needn't handle non-finite values.
Results may differ from the reference program's by a relative error of at most 0.0057.
Values may be sent and summed in bfloat16 or wider, within the bound.
A program may use at most 128 MiB of HBM per device.

```python
import math
import jax
import jax.numpy as jnp
from jax import lax

D = 1024
FF = 384
TOP = 8
TOK_DEV = 128
HOME_CAP = 80
REP_CAP = 32
SPECIALIST_COUNT = 16
TOKENS = 2048
N_EXPERT = 16


def routing_draw(key):
    order_key = jax.random.fold_in(key, 7001)
    score_key = jax.random.fold_in(key, 7002)
    table_key = jax.random.fold_in(key, 7003)
    uplift_seed_handle = jax.random.fold_in(key, 7004)
    popular = jax.random.permutation(order_key, SPECIALIST_COUNT).astype(jnp.int32)
    specialist_sorted_order = jnp.argsort(popular, stable=True).astype(jnp.int32)
    heaviest_loaded_specialist = max(SPECIALIST_COUNT // 8, 2)
    duplicate_uplift = jax.random.randint(uplift_seed_handle, (SPECIALIST_COUNT,), 0, 16384, dtype=jnp.int32)
    logit_increment = jnp.where(specialist_sorted_order < heaviest_loaded_specialist, 147456, 0).astype(jnp.int32) + duplicate_uplift
    drawn_router_logits = jax.random.randint(score_key, (TOKENS, SPECIALIST_COUNT), 0, 1048576, dtype=jnp.int32)
    specialist_logits = (drawn_router_logits + logit_increment[None, :]) * SPECIALIST_COUNT + jnp.arange(SPECIALIST_COUNT, dtype=jnp.int32)[None, :]
    chosen_ids = lax.top_k(specialist_logits, TOP)[1].astype(jnp.int32)
    shuffled = jax.random.permutation(table_key, SPECIALIST_COUNT).astype(jnp.int32) % heaviest_loaded_specialist
    placement = jnp.take(popular, shuffled).astype(jnp.int32)
    return (chosen_ids, placement)


def draw_expert_ids(key, part):
    return routing_draw(key)[0]


def draw_replica_table(key, part):
    return routing_draw(key)[1]


def level_of(stream_key, shape, split, low, top_value):
    loudness = 1.0
    for axis_at, shards_of in split:
        draws = jax.random.uniform(jax.random.fold_in(jax.random.fold_in(stream_key, 6), axis_at), (shards_of,), jnp.float32, low / len(split), top_value / len(split))
        loudness = loudness * jnp.repeat(jnp.exp(draws), shape[axis_at] // shards_of).reshape((-1,) + (1,) * (len(shape) - 1 - axis_at))
    return loudness


def bell_draw(key, extent, width, limit, shards=(), held_as=jnp.bfloat16):
    level = level_of(key, extent, shards, -0.22, 0.18) if shards else 1.0
    entries = jax.random.normal(key, extent, jnp.float32) * width * level
    return jnp.minimum(jnp.maximum(entries, -limit), limit).astype(held_as)


def setup_inputs(seed: int = 0, part: int = 0) -> dict:
    key_of = jax.random.split(jax.random.key(seed), 9)
    part_splits = jax.random.split(jax.random.fold_in(key_of[8], part), 9)
    tokens_in = bell_draw(part_splits[0], (TOKENS, D), 1.0, 6.0, ((0, 16),))
    grad_out = bell_draw(part_splits[1], (TOKENS, D), 1.0, 6.0, ((0, 16),))
    gates = jnp.clip(jnp.exp(math.log(0.5) - 2.306499 * jax.random.uniform(part_splits[2], (TOKENS, TOP), jnp.float32) ** level_of(part_splits[2], (TOKENS, TOP), ((0, 16),), -0.2, 0.2)), 0.049804688, 0.5).astype(jnp.bfloat16)
    expert_ids = draw_expert_ids(jax.random.fold_in(jax.random.fold_in(key_of[8], part), 71), part)
    replica_table = draw_replica_table(jax.random.fold_in(jax.random.fold_in(key_of[8], part), 71), part)
    w_gate = bell_draw(key_of[5], (SPECIALIST_COUNT, D, FF), D ** -0.5, 0.1875, ((0, 16),))
    w_up = bell_draw(key_of[6], (SPECIALIST_COUNT, D, FF), D ** -0.5, 0.1875, ((0, 16),))
    w_down = bell_draw(key_of[7], (SPECIALIST_COUNT, FF, D), FF ** -0.5, 0.3125, ((0, 16),))
    return {"tokens_in": tokens_in, "grad_out": grad_out, "gates": gates, "expert_ids": expert_ids, "replica_table": replica_table, "w_gate": w_gate, "w_up": w_up, "w_down": w_down}


contract_rows = (((0,), (0,)), ((), ()))
contract_cols = (((1,), (1,)), ((), ()))


def plan_routes(row_ids, replica_table, source, devices, home_cap, rep_cap):
    flat_ids = row_ids.reshape(-1).astype(jnp.int32)
    expert_axis = jnp.arange(devices, dtype=jnp.int32)
    hosted = (replica_table[None, :] == expert_axis[:, None]).astype(jnp.int32)
    copies = 1 + jnp.sum(hosted, axis=1)
    replica_order = jnp.cumsum(hosted, axis=1) - hosted
    chosen = (flat_ids[:, None] == expert_axis[None, :]).astype(jnp.int32)
    row_rank = jnp.sum((jnp.cumsum(chosen, axis=0) - chosen) * chosen, axis=1)
    row_copies = jnp.take(copies, flat_ids, axis=0)
    copy_index = (row_rank + source) % row_copies
    at_home = copy_index == 0
    matched = (jnp.take(hosted, flat_ids, axis=0) == 1) & (jnp.take(replica_order, flat_ids, axis=0) == (copy_index - 1)[:, None])
    replica_device = jnp.sum(jnp.where(matched, expert_axis[None, :], 0), axis=1)
    target = jnp.where(at_home, flat_ids, replica_device)
    bucket = target * 2 + jnp.where(at_home, 0, 1)
    bucket_hot = (bucket[:, None] == jnp.arange(2 * devices, dtype=jnp.int32)[None, :]).astype(jnp.int32)
    position = jnp.sum((jnp.cumsum(bucket_hot, axis=0) - bucket_hot) * bucket_hot, axis=1)
    slot_width = home_cap + rep_cap
    kept_rows = jnp.where(at_home, position < home_cap, position < rep_cap)
    slot_index = target * slot_width + jnp.where(at_home, position, home_cap + position)
    slot_index = jnp.where(kept_rows, slot_index, devices * slot_width)
    return slot_index.astype(jnp.int32), kept_rows


def expert_grads(rows_x, rows_dy, rows_gate, gate_w, up_w, down_w):
    pre_gate = jnp.dot(rows_x, gate_w, preferred_element_type=jnp.float32)
    pre_up = jnp.dot(rows_x, up_w, preferred_element_type=jnp.float32)
    sigmoid_gate = jax.nn.sigmoid(pre_gate)
    activated = pre_gate * sigmoid_gate
    product = activated * pre_up
    hidden = product.astype(jnp.bfloat16)
    back_hidden = lax.dot_general(rows_dy, down_w, contract_cols, preferred_element_type=jnp.float32)
    gate_grad = jnp.sum(lax.optimization_barrier(hidden).astype(jnp.float32) * back_hidden, axis=1).astype(jnp.bfloat16)
    gate_value = rows_gate.astype(jnp.float32)[:, None]
    weighted = (gate_value * product).astype(jnp.bfloat16)
    down_grad = lax.dot_general(weighted, rows_dy, contract_rows, preferred_element_type=jnp.float32)
    scaled = gate_value * back_hidden
    grad_pre_gate = (scaled * pre_up * sigmoid_gate * (1.0 + pre_gate * (1.0 - sigmoid_gate))).astype(jnp.bfloat16)
    grad_pre_up = (scaled * activated).astype(jnp.bfloat16)
    gate_w_grad = lax.dot_general(rows_x, grad_pre_gate, contract_rows, preferred_element_type=jnp.float32)
    up_w_grad = lax.dot_general(rows_x, grad_pre_up, contract_rows, preferred_element_type=jnp.float32)
    input_grad = lax.dot_general(grad_pre_gate, gate_w, contract_cols, preferred_element_type=jnp.float32)
    input_grad = input_grad + lax.dot_general(grad_pre_up, up_w, contract_cols, preferred_element_type=jnp.float32)
    return input_grad.astype(jnp.bfloat16), gate_grad, gate_w_grad, up_w_grad, down_grad


def reference(tokens_in, grad_out, gates, expert_ids, replica_table, w_gate, w_up, w_down):
    devices = N_EXPERT
    slot_width = HOME_CAP + REP_CAP
    model_width = D
    hidden_units = FF
    routed = TOK_DEV * TOP
    per_source = expert_ids.reshape(devices, routed)
    sources = jnp.arange(devices, dtype=jnp.int32)
    slot_index, kept_rows = jax.vmap(lambda row_ids, src_index: plan_routes(row_ids, replica_table, src_index, devices, HOME_CAP, REP_CAP))(per_source, sources)

    def fill_slots(slot_rows):
        empty = jnp.full((devices * slot_width + 1,), -1, jnp.int32)
        return empty.at[slot_rows].set(jnp.arange(routed, dtype=jnp.int32))[:-1]

    slot_fill = jax.vmap(fill_slots)(slot_index)
    zero_bf = jnp.zeros((), jnp.bfloat16)

    def visit(state_carry, target):
        acc_tokens, acc_gates, replica_gate, replica_up, replica_down = state_carry
        taken_slots = lax.dynamic_slice_in_dim(slot_fill, (target * slot_width).astype(jnp.int32), slot_width, 1)
        filled = taken_slots >= 0
        clipped = jnp.maximum(taken_slots, 0)
        token_row = (sources[:, None] * TOK_DEV + clipped // TOP).astype(jnp.int32)
        top_index = (clipped % TOP).astype(jnp.int32)
        rows_x = jnp.where(filled[..., None], tokens_in[token_row], zero_bf)
        rows_dy = jnp.where(filled[..., None], grad_out[token_row], zero_bf)
        rows_gate = jnp.where(filled, gates[token_row, top_index], zero_bf)
        hosted = replica_table[target]
        home_grads = expert_grads(rows_x[:, :HOME_CAP].reshape(-1, model_width), rows_dy[:, :HOME_CAP].reshape(-1, model_width),
                                  rows_gate[:, :HOME_CAP].reshape(-1), w_gate[target], w_up[target], w_down[target])
        extra_grads = expert_grads(rows_x[:, HOME_CAP:].reshape(-1, model_width), rows_dy[:, HOME_CAP:].reshape(-1, model_width),
                                   rows_gate[:, HOME_CAP:].reshape(-1), w_gate[hosted], w_up[hosted], w_down[hosted])
        back_x = jnp.concatenate([home_grads[0].reshape(devices, HOME_CAP, model_width),
                                  extra_grads[0].reshape(devices, REP_CAP, model_width)], axis=1)
        back_gate = jnp.concatenate([home_grads[1].reshape(devices, HOME_CAP), extra_grads[1].reshape(devices, REP_CAP)], axis=1)
        masked_x = jnp.where(filled[..., None], back_x.astype(jnp.float32), jnp.float32(0.0))
        acc_tokens = acc_tokens.at[token_row.reshape(-1)].add(masked_x.reshape(-1, model_width))
        masked_gate = jnp.where(filled, back_gate.astype(jnp.float32), jnp.float32(0.0))
        acc_gates = acc_gates.at[token_row.reshape(-1), top_index.reshape(-1)].add(masked_gate.reshape(-1))
        replica_gate = replica_gate.at[hosted].add(lax.optimization_barrier(extra_grads[2].astype(jnp.bfloat16)).astype(jnp.float32))
        replica_up = replica_up.at[hosted].add(lax.optimization_barrier(extra_grads[3].astype(jnp.bfloat16)).astype(jnp.float32))
        replica_down = replica_down.at[hosted].add(lax.optimization_barrier(extra_grads[4].astype(jnp.bfloat16)).astype(jnp.float32))
        return (acc_tokens, acc_gates, replica_gate, replica_up, replica_down), (home_grads[2], home_grads[3], home_grads[4])

    initial = (jnp.zeros((TOKENS, model_width), jnp.float32), jnp.zeros((TOKENS, TOP), jnp.float32),
               jnp.zeros((devices, model_width, hidden_units), jnp.float32),
               jnp.zeros((devices, model_width, hidden_units), jnp.float32),
               jnp.zeros((devices, hidden_units, model_width), jnp.float32))
    final_state, home_parts = lax.scan(visit, initial, sources)
    acc_tokens, acc_gates, replica_gate, replica_up, replica_down = final_state
    grad_tokens = acc_tokens.astype(jnp.bfloat16)
    grad_gates = acc_gates.astype(jnp.bfloat16)
    grad_w_gate = (home_parts[0] + lax.optimization_barrier(replica_gate.astype(jnp.bfloat16)).astype(jnp.float32)).astype(jnp.bfloat16)
    grad_w_up = (home_parts[1] + lax.optimization_barrier(replica_up.astype(jnp.bfloat16)).astype(jnp.float32)).astype(jnp.bfloat16)
    grad_w_down = (home_parts[2] + lax.optimization_barrier(replica_down.astype(jnp.bfloat16)).astype(jnp.float32)).astype(jnp.bfloat16)
    return (grad_tokens, grad_gates, grad_w_gate, grad_w_up, grad_w_down)
```

```python
import jax
import jax.numpy as jnp
from jax import lax
from jax.experimental import pallas as pl
from jax.experimental.pallas import tpu as pltpu
from jax.sharding import PartitionSpec as P

TOP = 8
ROWS_PER_CHUNK = 4096

contract_rows = (((0,), (0,)), ((), ()))
contract_cols = (((1,), (1,)), ((), ()))

MESH = pl.DeviceIdType.MESH
VMEM_GRANT = 58 * 2**20


def place(depth):
    me = lax.axis_index("expert")
    z, y, c = me // 4, (me // 2) % 2, me % 2
    return me, z, y, c, depth - 1


def index_of(z, y, c):
    return (z * 2 + y) * 2 + c


def greet(me, devices):
    sem = pltpu.get_barrier_semaphore()
    for peer in range(devices):
        pl.when(peer != me)(
            lambda peer=peer: pl.semaphore_signal(
                sem, inc=1, device_id={"expert": peer}, device_id_type=MESH
            )
        )
    pl.semaphore_wait(sem, devices - 1)


class Sender:
    def __init__(self, sems):
        self.sems = sems

    def send(self, group, cond, make):
        if cond is None:
            make(self.sems.at[group]).start()
        else:
            pl.when(cond)(lambda: make(self.sems.at[group]).start())

    def sent(self, group, ref):
        pltpu.make_async_copy(ref, ref, self.sems.at[group]).wait()


def remote(src, dst, recv_sem, peer):
    return lambda send_sem: pltpu.make_async_remote_copy(
        src_ref=src(), dst_ref=dst(), send_sem=send_sem, recv_sem=recv_sem(),
        device_id={"expert": peer()}, device_id_type=MESH,
    )


def landed(ref, sem):
    pltpu.make_async_copy(ref, ref, sem).wait()


TUNED_DEPTH = 4
TUNED_SHARES = (32, 32, 16, 16, 16, 16)
TUNED = [
    ("own", 0), ("own", 1), ("relay", 0, 1), ("relay", 0, -1), ("own", 3), ("relay", 0, 2),
    ("relay", 0, -2), ("cross", 0, 0), ("own", 2), ("relay", 0, 3), ("relay", 0, -3),
    ("relay", 1, -1), ("cross", 0, -3), ("relay", 1, 1), ("relay", 1, -2), ("cross", 0, 1),
    ("cross", 0, -1), ("gates", 0), ("cross", 0, 3), ("relay", 1, 2), ("cross", 0, -2),
    ("cross", 0, 2), ("cross", 3, 0), ("relay", 1, 3), ("finish", 0), ("relay", 2, 1),
    ("relay", 1, -3), ("own", 4), ("relay", 2, -1), ("relay", 3, 1), ("fwd", 0, 0),
    ("relay", 2, 2), ("own", 5), ("relay", 2, -2), ("cross", 1, 1), ("relay", 3, -1),
    ("fwd", 0, 1), ("relay", 4, -1), ("cross", 1, -2), ("relay", 3, 2), ("cross", 1, -3),
    ("cross", 1, -1), ("cross", 1, 0), ("relay", 2, 3), ("cross", 1, 2), ("sc", 0, 0),
    ("cross", 1, 3), ("relay", 2, -3), ("relay", 4, -2), ("relay", 3, -2), ("relay", 3, 3),
    ("relay", 4, 1), ("relay", 5, 1), ("sc", 0, 1), ("finish", 1), ("cross", 2, 1),
    ("relay", 5, -1), ("fwd", 1, 0), ("cross", 2, -1), ("relay", 4, 2), ("fwd", 1, 1),
    ("sc", 0, 2), ("cross", 2, 0), ("wg", 0, 1), ("relay", 5, 2), ("wg", 1, 1), ("cross", 2, 2),
    ("sc", 1, 0), ("cross", 2, -3), ("relay", 5, -2), ("cross", 2, 3), ("cross", 2, -2),
    ("wg", 0, 0), ("relay", 4, 3), ("sc", 1, 1), ("finish", 2), ("fwd", 2, 0), ("wg", 2, 1),
    ("relay", 3, -3), ("relay", 4, -3), ("cross", 3, 1), ("wg", 1, 0), ("cross", 3, -2),
    ("cross", 3, -1), ("cross", 4, -1), ("sc", 2, 0), ("cross", 5, 1), ("sc", 2, 1),
    ("cross", 3, 2), ("cross", 4, -2), ("cross", 3, 3), ("wg", 2, 0), ("cross", 4, 1),
    ("cross", 3, -3), ("sc", 1, 2), ("cross", 4, 2), ("relay", 5, -3), ("cross", 5, 0),
    ("relay", 5, 3), ("cross", 5, -2), ("cross", 5, -1), ("cross", 4, -3), ("finish", 3),
    ("cross", 4, 0), ("cross", 4, 3), ("fwd", 3, 0), ("sc", 2, 2), ("finish", 4),
    ("cross", 5, -3), ("cross", 5, 3), ("cross", 5, 2), ("fwd", 4, 0), ("sc", 3, 0), ("wg", 3, 1),
    ("finish", 5), ("wg", 3, 0), ("sc", 3, 1), ("fwd", 5, 0), ("sc", 4, 0), ("sc", 4, 1),
    ("sc", 5, 0), ("sc", 2, 3), ("sc", 3, 2), ("sc", 1, 3), ("sc", 5, 1), ("wg", 4, 0),
    ("wg", 4, 1), ("sc", 4, 2), ("ggout", 0), ("sc", 0, 3), ("sc", 5, 2), ("sc", 3, 3),
    ("sc", 4, 3), ("ggin", 0), ("sc", 5, 3), ("wg", 5, 1), ("total", 0), ("total", 2),
    ("total", 1), ("total", 4), ("total", 3), ("wg", 5, 0), ("total", 5),
]


def row_chunks(tok):
    whole = sum(TUNED_SHARES)
    sizes = [tok * share // whole for share in TUNED_SHARES]
    return [(sum(sizes[:k]), size) for k, size in enumerate(sizes)]


def step_order(depth, n):
    if depth == TUNED_DEPTH:
        return TUNED
    steps = [("own", 0), ("gates", 0)]
    for k in range(n):
        steps += [("own", k)] if k else []
        for d in range(1, depth):
            steps += [("relay", k, -d), ("relay", k, d)]
        steps += [("cross", k, d) for d in range(1 - depth, depth)]
        steps += [("finish", k), ("fwd", k, 0), ("fwd", k, 1), ("wg", k, 0), ("wg", k, 1)]
        steps += [("sc", k, p) for p in range(depth)] + [("total", k)]
    return steps + [("ggout", 0), ("ggin", 0)]


def fused_kernel(
    depth, order, home_cap, rep_cap,
    x_hbm, dy_hbm, gates_hbm, ids_hbm, table_hbm, wg_hbm, wu_hbm, wd_hbm,
    out_ref, ggo_ref, dwg_ref, dwu_ref, dwd_ref,
    buf, gbuf, gcol, ggcol, ggs, ggr, w1, wd, dadb, hgb, acc1, acc2, dx, rc, rzu, rzd, ysend, ry,
    gates_ref, ids_ref, table_ref,
    local_sems, send_sems, recv_sems, pair_sems, gate_sem, gg_sem, twin_sems, up_sems, down_sems,
    y_sems,
):
    f32, bf16 = jnp.float32, jnp.bfloat16
    devices = 4 * depth
    me, z, y, c, last = place(depth)
    tok, width = x_hbm.shape
    hidden = wd_hbm.shape[0]
    chunks = row_chunks(tok)
    lanes = gcol.shape[1]

    def local(src, dst, i):
        return pltpu.make_async_copy(src, dst, local_sems.at[i])

    own_copies = [local(x_hbm, buf.at[me, 0], 0), local(dy_hbm, buf.at[me, 1], 1)]
    weight_copies = [
        local(wg_hbm, w1.at[:, pl.ds(0, hidden)], 2),
        local(wu_hbm, w1.at[:, pl.ds(hidden, hidden)], 3),
        local(wd_hbm, wd, 4),
    ]
    plan_copies = [
        local(gates_hbm, gates_ref, 5), local(ids_hbm, ids_ref, 6), local(table_hbm, table_ref, 7),
    ]
    for copy in own_copies + plan_copies + weight_copies:
        copy.start()
    greet(me, devices)
    for copy in own_copies:
        copy.wait()

    out = Sender(send_sems)
    up = lambda: index_of(z + 1, y, c)
    down = lambda: index_of(z - 1, y, c)
    over = lambda: index_of(z, 1 - y, c)
    twin = lambda: index_of(z, y, 1 - c)
    can_up, can_down = z < last, z > 0
    half = depth // 2

    def rows_of(k):
        return pl.ds(*chunks[k])

    OWN, PASS, PAIR, CHAIN, HOME, GATE, BACK = range(7)

    def push(group, cond, b, k, peer):
        block = lambda: buf.at[b(), :, rows_of(k)]
        sem = (lambda: pair_sems.at[k]) if peer is twin else (lambda: recv_sems.at[k, b()])
        out.send(group, cond, remote(block, block, sem, peer))

    def arrived(k, b):
        landed(buf.at[b, :, rows_of(k)], recv_sems.at[k, b])

    def own(k):
        mine = lambda: me
        push(OWN, None, mine, k, over)
        push(OWN, can_up, mine, k, up)
        push(OWN, can_down, mine, k, down)
        push(OWN, None, mine, k, twin)

    def relay(k, off):
        cond = z + off >= 0 if off < 0 else z + off <= last
        more, onward = (can_up, up) if off < 0 else (can_down, down)
        b = lambda: index_of(z + off, y, c)
        pl.when(cond)(lambda: arrived(k, b()))
        if abs(off) < depth - 1:
            push(PASS, cond & more, b, k, onward)
        push(PASS, cond, b, k, over)
        push(PASS, cond, b, k, twin)

    def cross(k, off):
        b = lambda: index_of(z + off, 1 - y, c)
        cond = None if off == 0 else z + off >= 0 if off < 0 else z + off <= last
        if cond is None:
            arrived(k, b())
        else:
            pl.when(cond)(lambda: arrived(k, b()))
        push(PASS, cond, b, k, twin)

    def finish(k):
        landed(buf.at[pl.ds(0, devices // 2), :, rows_of(k)], pair_sems.at[k])

    lane = lax.broadcasted_iota(jnp.int32, (tok, lanes), 1)
    expert = lax.broadcasted_iota(jnp.int32, (devices, tok), 0)

    def send_gates():
        copies = jnp.ones((devices, tok), f32)
        for d in range(devices):
            copies = copies + jnp.where(expert == table_ref[d], 1.0, 0.0)
        dense = jnp.zeros((devices, tok), f32)
        named = jnp.zeros((devices, tok), f32)
        for k in range(ids_ref.shape[0]):
            hot = ids_ref[k : k + 1] == expert
            dense = jnp.where(hot, gates_ref[k : k + 1].astype(f32), dense)
            named = jnp.where(hot, 1.0, named)
        row = lax.broadcasted_iota(jnp.int32, (tok, tok), 0)
        col = lax.broadcasted_iota(jnp.int32, (tok, tok), 1)
        earlier = jnp.where(row < col, 1.0, 0.0).astype(bf16)
        rank = jnp.dot(named.astype(bf16), earlier, preferred_element_type=f32)
        position = jnp.floor((rank + 0.5) / copies)
        turn = rank + me.astype(f32)
        copy_index = turn - copies * jnp.floor((turn + 0.5) / copies)
        limit = jnp.where(copy_index < 0.5, float(home_cap), float(rep_cap))
        gbuf[me] = jnp.where((named > 0.5) & (position < limit), dense, 0.0).astype(bf16)
        for peer in range(devices):
            out.send(
                GATE, peer != me,
                remote(
                    lambda: gbuf.at[me], lambda: gbuf.at[me], lambda: gate_sem,
                    lambda peer=peer: peer,
                ),
            )

    def take_gates():
        landed(gbuf.at[pl.ds(0, devices - 1)], gate_sem)
        flat = gbuf[...].reshape(devices * devices, tok)
        r = lax.broadcasted_iota(jnp.int32, (devices * devices, lanes), 0)
        l = lax.broadcasted_iota(jnp.int32, (devices * devices, lanes), 1)
        pick = jnp.where(r == l * devices + me, 1.0, 0.0).astype(bf16)
        gcol[...] = lax.dot_general(flat, pick, contract_rows, preferred_element_type=f32)
        ggcol[...] = jnp.zeros_like(ggcol)

    def units(k):
        if chunks[k][1] * devices <= 256 or depth % 2:
            return [(0, depth)]
        first = jnp.where(z < half, half, 0)
        return [(first, half), (half - first, half)]

    def forward(k, u):
        if u >= len(units(k)):
            return
        r0, size = chunks[k]
        p0, planes = units(k)[u]
        nb = planes * 4
        at = pl.ds(p0 * 4, nb)
        rows = pl.ds(r0, size)
        x = buf[at, 0, rows, :].reshape(nb * size, width)
        dy = buf[at, 1, rows, :].reshape(nb * size, width)
        g = gcol[rows, :]
        spot = lane[:size]
        gate = jnp.concatenate(
            [
                jnp.sum(jnp.where(spot == p0 * 4 + j, g, 0.0), axis=1, keepdims=True)
                for j in range(nb)
            ],
            axis=0,
        )
        ab = jnp.dot(x, w1[...], preferred_element_type=f32)
        a, b = ab[:, :hidden], ab[:, hidden:]
        v = lax.dot_general(dy, wd[...], contract_cols, preferred_element_type=f32)
        sig = jax.nn.sigmoid(a)
        act = a * sig
        product = act * b
        gate_grad = jnp.sum(product.astype(bf16).astype(f32) * v, axis=1, keepdims=True)
        gate_grad = jnp.where(gate > 0, gate_grad, 0.0)
        gu = gate * v
        da = (gu * b * sig * (1.0 + a * (1.0 - sig))).astype(bf16)
        db = (gu * act).astype(bf16)
        both_grads = jnp.concatenate([da, db], axis=1)
        hgb[k % 2, at, pl.ds(0, size), :] = (gate * product).astype(bf16).reshape(nb, size, hidden)
        dadb[k % 2, at, pl.ds(0, size), :] = both_grads.reshape(nb, size, 2 * hidden)
        back = lax.dot_general(both_grads, w1[...], contract_cols, preferred_element_type=f32)
        dx[pl.ds(p0, planes), :, :, rows, :] = back.astype(bf16).reshape(
            planes, 2, 2, size, width
        )
        held = ggcol[rows, :]
        for j in range(nb):
            held = jnp.where(spot == p0 * 4 + j, gate_grad[j * size : (j + 1) * size], held)
        ggcol[rows, :] = held
        src = lambda: dx.at[pl.ds(p0, planes), :, 1 - c, rows, :]
        dst = lambda: rc.at[pl.ds(p0, planes), :, rows, :]
        out.send(PAIR, None, remote(src, dst, lambda: twin_sems.at[k, u], twin))

    def twin_sums(k):
        for u, (p0, planes) in enumerate(units(k)):
            landed(rc.at[pl.ds(p0, planes), :, rows_of(k), :], twin_sems.at[k, u])

    tile = 256 if width % 256 == 0 else 128

    def weight_tile(k, j, which):
        size = chunks[k][1]
        rows = rows_of(k)
        cols = pl.ds(j * tile, tile)
        first, final = k == 0, k == len(chunks) - 1
        if which == 0:
            x = buf[:, 0, rows, cols].reshape(devices * size, tile)
            d = dadb[k % 2, :, pl.ds(0, size), :].reshape(devices * size, 2 * hidden)
            v = lax.dot_general(x, d, contract_rows, preferred_element_type=f32)
            if not first:
                v = v + acc1[cols, :]
            if final:
                dwg_ref[cols, :] = v[:, :hidden].astype(bf16)
                dwu_ref[cols, :] = v[:, hidden:].astype(bf16)
            else:
                acc1[cols, :] = v
        else:
            dy = buf[:, 1, rows, cols].reshape(devices * size, tile)
            h = hgb[k % 2, :, pl.ds(0, size), :].reshape(devices * size, hidden)
            v = lax.dot_general(h, dy, contract_rows, preferred_element_type=f32)
            if not first:
                v = v + acc2[:, cols]
            if final:
                dwd_ref[:, cols] = v.astype(bf16)
            else:
                acc2[:, cols] = v

    def weights(k, which):
        for j in range(width // tile):
            weight_tile(k, j, which)

    def part_sum(zz, yy, rows, extra):
        total = dx[zz, yy, c, rows, :].astype(f32) + rc[zz, yy, rows, :].astype(f32)
        for ref in extra:
            total = total + ref[zz, yy, rows, :].astype(f32)
        return total

    def chain(k, p):
        rows = rows_of(k)
        for way, there, zz_of, ref, sems, has, peer in (
            (0, z <= p, lambda: z + last - p, rzu, up_sems, z > 0, up),
            (1, last - z <= p, lambda: z + p - last, rzd, down_sems, z < last, down),
        ):

            def step():
                zz = zz_of()
                pl.when(has)(lambda: landed(ref.at[zz, :, rows, :], sems.at[k, zz]))
                for yy in range(2):
                    ref[zz, yy, rows, :] = part_sum(zz, yy, rows, (ref,)).astype(bf16)

            pl.when(there)(step)
            out.send(
                CHAIN, there,
                remote(
                    lambda: ref.at[zz_of(), :, rows, :], lambda: ref.at[zz_of(), :, rows, :],
                    lambda: sems.at[k, zz_of()], peer,
                ),
            )

    def home(k):
        rows = rows_of(k)
        pl.when(z > 0)(lambda: landed(rzu.at[z, :, rows, :], up_sems.at[k, z]))
        pl.when(z < last)(lambda: landed(rzd.at[z, :, rows, :], down_sems.at[k, z]))
        ysend[rows, :] = part_sum(z, 1 - y, rows, (rzu, rzd)).astype(bf16)
        out.send(
            HOME, None,
            remote(
                lambda: ysend.at[rows, :], lambda: ry.at[rows, :], lambda: y_sems.at[k], over
            ),
        )

    def total(k):
        rows = rows_of(k)
        mine = part_sum(z, y, rows, (rzu, rzd))
        landed(ry.at[rows, :], y_sems.at[k])
        out_ref[rows, :] = (mine + ry[rows, :].astype(f32)).astype(bf16)

    def scatter_point(k, p):
        if p == 0:
            twin_sums(k)
        if p < last:
            chain(k, p)
        else:
            home(k)

    def send_gate_grads():
        turned = ggcol[...].T
        for b in range(devices):
            ggs[b] = turned[b : b + 1]
        ggr[me] = ggs[me]
        for peer in range(devices):
            out.send(
                BACK, peer != me,
                remote(
                    lambda peer=peer: ggs.at[peer], lambda: ggr.at[me], lambda: gg_sem,
                    lambda peer=peer: peer,
                ),
            )

    def take_gate_grads():
        landed(ggr.at[pl.ds(0, devices - 1)], gg_sem)
        held = ggr[...].reshape(devices, tok)
        for k in range(ids_ref.shape[0]):
            hot = ids_ref[k : k + 1] == expert
            picked = jnp.sum(jnp.where(hot, held, 0.0), axis=0, keepdims=True)
            ggo_ref[k : k + 1] = picked.astype(bf16)

    def gates_out(k):
        for copy in plan_copies:
            copy.wait()
        send_gates()

        @pl.when(z == 0)
        def _():
            rzu[...] = jnp.zeros_like(rzu)

        @pl.when(z == last)
        def _():
            rzd[...] = jnp.zeros_like(rzd)

    def ready(k):
        finish(k)
        if k == 0:
            take_gates()
            for copy in weight_copies:
                copy.wait()

    steps = dict(
        own=own, gates=gates_out, relay=relay, cross=cross, finish=ready, fwd=forward,
        wg=weights, sc=scatter_point, total=total, ggout=lambda k: send_gate_grads(),
        ggin=lambda k: take_gate_grads(),
    )
    for name, *rest in order:
        steps[name](*rest)

    def sent_blocks(zz):
        ends = (zz < last) + (zz > 0)
        passed = depth
        for off in range(1, depth):
            passed += (zz >= off) * (2 + (zz < last and off < last))
            passed += (zz + off <= last) * (2 + (zz > 0 and off < last))
        out.sent(OWN, buf.at[pl.ds(0, 2 + ends)])
        out.sent(PASS, buf.at[pl.ds(0, passed)])

    for zz in range(depth):
        pl.when(z == zz)(lambda: sent_blocks(zz))
    out.sent(PAIR, rc)
    if depth > 1:
        out.sent(CHAIN, rzu.at[pl.ds(0, depth - 1)])
    out.sent(HOME, ysend)
    out.sent(GATE, gbuf.at[pl.ds(0, devices - 1)])
    out.sent(BACK, ggs.at[pl.ds(0, devices - 1)])


def fused_grads(x, dy, gates, ids, table, gate_w, up_w, down_w, devices, home_cap, rep_cap):
    depth = devices // 4
    tok, width = x.shape
    hidden = down_w.shape[0]
    f32, bf16 = jnp.float32, jnp.bfloat16
    n = len(row_chunks(tok))
    most = max(size for _, size in row_chunks(tok))
    vmem, dma = pltpu.VMEM, pltpu.SemaphoreType.DMA
    whole = pl.BlockSpec(memory_space=pltpu.VMEM)
    hbm = pl.BlockSpec(memory_space=pltpu.HBM)
    shape = jax.ShapeDtypeStruct
    outs = pl.pallas_call(
        lambda *refs: fused_kernel(depth, step_order(depth, n), home_cap, rep_cap, *refs),
        out_shape=[
            shape((tok, width), bf16), shape(gates.shape, bf16), shape(gate_w.shape, bf16),
            shape(up_w.shape, bf16), shape(down_w.shape, bf16),
        ],
        in_specs=[hbm] * 8,
        out_specs=[whole] * 5,
        scratch_shapes=[
            vmem((devices, 2, tok, width), bf16), vmem((devices, devices, tok), bf16),
            vmem((tok, 128), f32), vmem((tok, 128), f32),
            vmem((devices, 1, tok), f32), vmem((devices, 1, tok), f32),
            vmem((width, 2 * hidden), bf16), vmem((hidden, width), bf16),
            vmem((2, devices, most, 2 * hidden), bf16), vmem((2, devices, most, hidden), bf16),
            vmem((width, 2 * hidden), f32), vmem((hidden, width), f32),
            vmem((depth, 2, 2, tok, width), bf16), vmem((depth, 2, tok, width), bf16),
            vmem((depth, 2, tok, width), bf16), vmem((depth, 2, tok, width), bf16),
            vmem((tok, width), bf16), vmem((tok, width), bf16),
            vmem(gates.shape, bf16), vmem(ids.shape, ids.dtype),
            pltpu.SMEM(table.shape, table.dtype),
            dma((8,)), dma((7,)), dma((n, devices)), dma((n,)), dma, dma,
            dma((n, 2)), dma((n, depth)), dma((n, depth)), dma((n,)),
        ],
        compiler_params=pltpu.CompilerParams(
            collective_id=0, has_side_effects=True, vmem_limit_bytes=VMEM_GRANT
        ),
    )(x, dy, gates, ids, table, gate_w, up_w, down_w)
    return store_all(outs)


def store_kernel(n, *refs):
    sems = refs[2 * n]
    copies = [
        pltpu.make_async_copy(refs[i], refs[n + i], sems.at[i]) for i in range(n)
    ]
    for copy in copies:
        copy.start()
    for copy in copies:
        copy.wait()


def store_all(arrays):
    n = len(arrays)
    return pl.pallas_call(
        lambda *refs: store_kernel(n, *refs),
        out_shape=[jax.ShapeDtypeStruct(v.shape, v.dtype) for v in arrays],
        in_specs=[pl.BlockSpec(memory_space=pltpu.VMEM)] * n,
        out_specs=[pl.BlockSpec(memory_space=pltpu.HBM)] * n,
        scratch_shapes=[pltpu.SemaphoreType.DMA((n,))],
    )(*arrays)


def keep_plan(gates, row_ids, replica_table, source, devices, home_cap, rep_cap):
    tok = row_ids.shape[0]
    experts = jnp.arange(devices, dtype=jnp.int32)
    hot = row_ids[:, :, None] == experts[None, None, :]
    named = jnp.any(hot, axis=1)
    dense_gate = jnp.sum(jnp.where(hot, gates.astype(jnp.float32)[:, :, None], 0.0), axis=1)
    copies = 1 + jnp.sum((replica_table[:, None] == experts[None, :]).astype(jnp.int32), axis=0)
    order = jnp.arange(tok, dtype=jnp.int32)
    earlier = (order[:, None] > order[None, :]).astype(jnp.bfloat16)
    rank = jnp.dot(earlier, named.astype(jnp.bfloat16), preferred_element_type=jnp.float32)
    many = copies.astype(jnp.float32)[None, :]
    position = jnp.floor((rank + 0.5) / many)
    turn = rank + source.astype(jnp.float32)
    copy_index = turn - many * jnp.floor((turn + 0.5) / many)
    limit = jnp.where(copy_index < 0.5, float(home_cap), float(rep_cap))
    kept = named & (position < limit)
    return jnp.where(kept, dense_gate, 0.0).astype(jnp.bfloat16)


def row_grads(x, dy, gate, gate_w, up_w, down_w):
    a = jnp.dot(x, gate_w, preferred_element_type=jnp.float32)
    b = jnp.dot(x, up_w, preferred_element_type=jnp.float32)
    u = lax.dot_general(dy, down_w, contract_cols, preferred_element_type=jnp.float32)
    sig = jax.nn.sigmoid(a)
    act = a * sig
    product = act * b
    hidden = product.astype(jnp.bfloat16).astype(jnp.float32)
    gate_grad = jnp.sum(hidden * u, axis=1, keepdims=True)
    gate_grad = jnp.where(gate > 0, gate_grad, 0.0)
    hg = (gate * product).astype(jnp.bfloat16)
    gu = gate * u
    da = (gu * b * sig * (1.0 + a * (1.0 - sig))).astype(jnp.bfloat16)
    db = (gu * act).astype(jnp.bfloat16)
    dx = lax.dot_general(da, gate_w, contract_cols, preferred_element_type=jnp.float32)
    dx = dx + lax.dot_general(db, up_w, contract_cols, preferred_element_type=jnp.float32)
    return gate_grad, hg, da, db, dx


def weight_grads(x, dy, hg, da, db):
    dwg = lax.dot_general(x, da, contract_rows, preferred_element_type=jnp.float32)
    dwu = lax.dot_general(x, db, contract_rows, preferred_element_type=jnp.float32)
    dwd = lax.dot_general(hg, dy, contract_rows, preferred_element_type=jnp.float32)
    return dwg, dwu, dwd


def on_device(tokens_in, grad_out, gates, expert_ids, replica_table, w_gate, w_up, w_down):
    devices = lax.axis_size("expert")
    me = lax.axis_index("expert")
    tok, width = tokens_in.shape
    home_cap = max(2, 5 * tok * TOP // (4 * devices))
    rep_cap = max(2, tok * TOP // (2 * devices))
    if devices * tok <= ROWS_PER_CHUNK and devices % 16 == 0 and devices <= 128 and tok % 128 == 0:
        outs = fused_grads(
            tokens_in, grad_out, gates.T, expert_ids.T, replica_table, w_gate[0], w_up[0], w_down[0],
            devices, home_cap, rep_cap,
        )
        return (outs[0], outs[1].T, *[g[None] for g in outs[2:]])
    kept_gate = keep_plan(gates, expert_ids, replica_table, me, devices, home_cap, rep_cap)
    lanes = -(-devices // 128) * 128
    kept_gate = jnp.pad(kept_gate, ((0, 0), (0, lanes - devices)))
    payload = jnp.concatenate([tokens_in, grad_out, kept_gate], axis=1)
    chunks = max(1, devices * tok // ROWS_PER_CHUNK)
    part = tok // chunks
    mine = jnp.arange(lanes, dtype=jnp.int32)[None, :] == me
    backs, sums = [], None
    for c in range(chunks):
        rows = lax.all_gather(payload[c * part : (c + 1) * part], "expert", axis=0, tiled=True)
        gate = jnp.sum(
            jnp.where(mine, rows[:, 2 * width :].astype(jnp.float32), 0.0),
            axis=1,
            keepdims=True,
        )
        gate_grad, hg, da, db, dx = row_grads(
            rows[:, :width], rows[:, width : 2 * width], gate, w_gate[0], w_up[0], w_down[0]
        )
        spread = jnp.where(mine, gate_grad, 0.0).astype(jnp.bfloat16)
        back = jnp.concatenate([dx.astype(jnp.bfloat16), spread], axis=1)
        backs.append(lax.psum_scatter(back, "expert", scatter_dimension=0, tiled=True))
        grads = weight_grads(rows[:, :width], rows[:, width : 2 * width], hg, da, db)
        sums = grads if sums is None else [p + q for p, q in zip(sums, grads)]
        if c + 1 < chunks:
            payload, sums = lax.optimization_barrier((payload, sums))
    back = jnp.concatenate(backs, axis=0)
    experts = jnp.arange(devices, dtype=jnp.int32)
    hot = expert_ids[:, :, None] == experts[None, None, :]
    picked = jnp.where(hot, back[:, None, width : width + devices].astype(jnp.float32), 0.0)
    grad_gates = jnp.sum(picked, axis=2).astype(jnp.bfloat16)
    return (back[:, :width], grad_gates, *[g.astype(jnp.bfloat16)[None] for g in sums])


def solution(mesh):
    return jax.shard_map(
        on_device,
        mesh=mesh,
        in_specs=(
            P(("groups", "expert"), None),
            P(("groups", "expert"), None),
            P(("groups", "expert"), None),
            P(("groups", "expert"), None),
            P("groups"),
            P("expert", None, None),
            P("expert", None, None),
            P("expert", None, None),
        ),
        out_specs=(
            P(("groups", "expert"), None),
            P(("groups", "expert"), None),
            P(("groups", "expert"), None, None),
            P(("groups", "expert"), None, None),
            P(("groups", "expert"), None, None),
        ),
        check_vma=False,
    )
```

```python
import jax
import jax.numpy as jnp
from jax import lax
from jax.experimental import pallas as pl
from jax.experimental.pallas import tpu as pltpu
from jax.sharding import PartitionSpec as P

TOP = 8
ROWS_PER_CHUNK = 4096

contract_rows = (((0,), (0,)), ((), ()))
contract_cols = (((1,), (1,)), ((), ()))

MESH = pl.DeviceIdType.MESH
VMEM_GRANT = 58 * 2**20


def place(depth):
    me = lax.axis_index("expert")
    z, y, c = me // 4, (me // 2) % 2, me % 2
    return me, z, y, c, depth - 1


def index_of(z, y, c):
    return (z * 2 + y) * 2 + c


def greet(z, y, c, last):
    sem = pltpu.get_barrier_semaphore()

    def hello(peer):
        pl.semaphore_signal(sem, inc=1, device_id={"expert": peer}, device_id_type=MESH)

    hello(index_of(z, y, 1 - c))
    hello(index_of(z, 1 - y, c))
    pl.when(z > 0)(lambda: hello(index_of(z - 1, y, c)))
    pl.when(z < last)(lambda: hello(index_of(z + 1, y, c)))
    pl.semaphore_wait(sem, 2 + (z > 0).astype(jnp.int32) + (z < last).astype(jnp.int32))


class Sender:
    def __init__(self, sems):
        self.sems = sems

    def send(self, group, cond, make):
        if cond is None:
            make(self.sems.at[group]).start()
        else:
            pl.when(cond)(lambda: make(self.sems.at[group]).start())

    def sent(self, group, ref):
        pltpu.make_async_copy(ref, ref, self.sems.at[group]).wait()


def remote(src, dst, recv_sem, peer):
    return lambda send_sem: pltpu.make_async_remote_copy(
        src_ref=src(), dst_ref=dst(), send_sem=send_sem, recv_sem=recv_sem(),
        device_id={"expert": peer()}, device_id_type=MESH,
    )


def landed(ref, sem):
    pltpu.make_async_copy(ref, ref, sem).wait()


TUNED_DEPTH = 4
TUNED_SHARES = (32, 16, 16, 16, 16, 16, 16)
PAIR_FIRST = (False, False, False, True, True, True, True)
BOTH_COLUMNS = (False, False, False, True, False, False, False)
TUNED = [
    ("own", 0), ("own", 1), ("gates", 0), ("own", 2), ("relay", 0, 1), ("relay", 0, -1),
    ("own", 3), ("relay", 1, 1), ("relay", 0, 2), ("relay", 1, -1), ("relay", 1, 2),
    ("relay", 0, -2), ("relay", 1, -2), ("relay", 0, -3), ("relay", 0, 3), ("relay", 2, -1),
    ("relay", 2, 1), ("cross", 1, 1), ("cross", 0, 0), ("cross", 1, 0), ("relay", 1, -3),
    ("relay", 1, 3), ("cross", 2, 0), ("cross", 3, 0), ("cross", 0, 1), ("relay", 2, 2),
    ("cross", 0, 2), ("cross", 0, -1), ("relay", 2, -2), ("relay", 3, -1), ("own", 4),
    ("cross", 0, -2), ("relay", 3, 1), ("cross", 0, 3), ("cross", 1, -1), ("relay", 2, 3),
    ("cross", 0, -3), ("relay", 2, -3), ("own", 5), ("cross", 3, 1), ("cross", 3, -1),
    ("cross", 1, -2), ("own", 6), ("finish", 0), ("fwd", 0, 0), ("fwd", 0, 1), ("trade", 0),
    ("cross", 1, 2), ("cross", 1, 3), ("cross", 2, -1), ("relay", 4, 1), ("relay", 5, 1),
    ("relay", 4, -1), ("wg", 0, 1), ("cross", 1, -3), ("cross", 2, 1), ("wg", 0, 0),
    ("cross", 4, 0), ("relay", 3, -2), ("relay", 5, -1), ("cross", 2, -2), ("cross", 2, 2),
    ("cross", 3, 2), ("sc", 0, 0), ("finish", 1), ("cross", 2, 3), ("cross", 2, -3),
    ("fwd", 1, 0), ("cross", 3, -2), ("relay", 3, 2), ("finish", 2), ("relay", 4, 2),
    ("relay", 4, -2), ("fwd", 2, 0), ("wg", 1, 0), ("relay", 5, 2), ("trade", 1), ("cross", 5, 0),
    ("cross", 6, 0), ("relay", 3, -3), ("relay", 5, -2), ("cross", 3, 3), ("relay", 6, 1),
    ("cross", 4, 1), ("wg", 1, 1), ("relay", 6, -1), ("sc", 0, 1), ("cross", 3, -3), ("sc", 1, 0),
    ("relay", 3, 3), ("wg", 2, 1), ("trade", 2), ("wg", 2, 0), ("relay", 4, 3), ("cross", 4, -1),
    ("relay", 4, -3), ("finish", 3), ("fwd", 3, 0), ("relay", 5, 3), ("relay", 5, -3),
    ("wg", 3, 1), ("sc", 2, 0), ("relay", 6, -2), ("relay", 6, 2), ("sc", 0, 2), ("cross", 4, -3),
    ("cross", 4, 3), ("cross", 4, -2), ("cross", 5, -1), ("sc", 1, 1), ("cross", 4, 2),
    ("cross", 5, 2), ("wg", 3, 0), ("cross", 5, 1), ("cross", 6, 1), ("cross", 5, -2),
    ("cross", 6, -1), ("relay", 6, 3), ("relay", 6, -3), ("trade", 3), ("cross", 5, 3),
    ("cross", 5, -3), ("finish", 4), ("fwd", 4, 0), ("finish", 5), ("cross", 6, -2),
    ("cross", 6, 2), ("fwd", 5, 0), ("wg", 4, 1), ("sc", 1, 2), ("cross", 6, -3), ("cross", 6, 3),
    ("trade", 4), ("sc", 3, 0), ("sc", 2, 1), ("wg", 4, 0), ("trade", 5), ("finish", 6),
    ("fwd", 6, 0), ("sc", 2, 2), ("wg", 5, 1), ("sc", 5, 0), ("sc", 4, 0), ("sc", 3, 1),
    ("trade", 6), ("sc", 5, 1), ("sc", 6, 0), ("wg", 6, 1), ("sc", 4, 1), ("sc", 0, 3),
    ("sc", 2, 3), ("sc", 3, 2), ("sc", 6, 1), ("ggout", 0), ("sc", 1, 3), ("sc", 4, 2),
    ("sc", 5, 2), ("wg", 5, 0), ("sc", 6, 2), ("total", 2), ("wg", 6, 0), ("ggin", 0),
    ("total", 0), ("sc", 5, 3), ("sc", 3, 3), ("sc", 4, 3), ("total", 1), ("total", 5),
    ("sc", 6, 3), ("total", 6), ("total", 4), ("total", 3),
]


def row_chunks(tok):
    whole = sum(TUNED_SHARES)
    sizes = [tok * share // whole for share in TUNED_SHARES]
    return [(sum(sizes[:k]), size) for k, size in enumerate(sizes)]


def step_order(depth, n):
    if depth == TUNED_DEPTH:
        return TUNED
    steps = [("own", 0), ("gates", 0)]
    for k in range(n):
        steps += [("own", k)] if k else []
        for d in range(1, depth):
            steps += [("relay", k, -d), ("relay", k, d)]
        steps += [("cross", k, d) for d in range(1 - depth, depth)]
        steps += [("finish", k), ("fwd", k, 0), ("fwd", k, 1), ("wg", k, 0), ("wg", k, 1)]
        steps += [("trade", k)] + [("sc", k, p) for p in range(depth)] + [("total", k)]
    return steps + [("ggout", 0), ("ggin", 0)]


def fused_kernel(
    depth, order, home_cap, rep_cap,
    x_hbm, dy_hbm, gates_hbm, ids_hbm, table_hbm, wg_hbm, wu_hbm, wd_hbm,
    out_hbm, ggo_hbm, dwg_hbm, dwu_hbm, dwd_hbm,
    out_ref, ggo_ref, dwg_ref, dwu_ref, dwd_ref,
    buf, gbuf, gcol, ggcol, ggs, ggr, w1, wd, dadb, hgb, acc1, acc2, dx, rc, rzu, rzd, ysend, ry, xsend, xr,
    gates_ref, ids_ref, table_ref,
    local_sems, send_sems, recv_sems, pair_sems, gate_sem, gg_sem, twin_sems, up_sems, down_sems,
    y_sems, x_sems, gate_sems,
):
    f32, bf16 = jnp.float32, jnp.bfloat16
    devices = 4 * depth
    early, wide = PAIR_FIRST, BOTH_COLUMNS
    me, z, y, c, last = place(depth)
    tok, width = x_hbm.shape
    hidden = wd_hbm.shape[0]
    chunks = row_chunks(tok)
    lanes = gcol.shape[1]

    def local(src, dst, i):
        return pltpu.make_async_copy(src, dst, local_sems.at[i])

    own_copies = [local(x_hbm, buf.at[me, 0], 0), local(dy_hbm, buf.at[me, 1], 1)]
    weight_copies = [
        local(wg_hbm, w1.at[:, pl.ds(0, hidden)], 2),
        local(wu_hbm, w1.at[:, pl.ds(hidden, hidden)], 3),
        local(wd_hbm, wd, 4),
    ]
    plan_copies = [
        local(gates_hbm, gates_ref, 5), local(ids_hbm, ids_ref, 6), local(table_hbm, table_ref, 7),
    ]
    results = [
        local(out_ref, out_hbm, 8), local(ggo_ref, ggo_hbm, 9), local(dwg_ref, dwg_hbm, 10),
        local(dwu_ref, dwu_hbm, 11), local(dwd_ref, dwd_hbm, 12),
    ]
    for copy in own_copies + plan_copies + weight_copies:
        copy.start()
    greet(z, y, c, last)
    for copy in own_copies:
        copy.wait()

    out = Sender(send_sems)
    up = lambda: index_of(z + 1, y, c)
    down = lambda: index_of(z - 1, y, c)
    over = lambda: index_of(z, 1 - y, c)
    twin = lambda: index_of(z, y, 1 - c)
    can_up, can_down = z < last, z > 0
    half = depth // 2

    def rows_of(k):
        return pl.ds(*chunks[k])

    OWN, PASS, WIDE, PAIR, CHAIN, THIN, TRADE, HOME, GATE, BACK, FLAT = range(11)

    def push(group, cond, b, k, peer):
        block = lambda: buf.at[b(), :, rows_of(k)]
        sem = (lambda: pair_sems.at[k]) if peer is twin else (lambda: recv_sems.at[k, b()])
        out.send(group, cond, remote(block, block, sem, peer))
        if k == 0 and group != OWN:
            push_gates(FLAT, cond, b, peer)

    def push_gates(group, cond, b, peer):
        sem = (lambda: gate_sem) if peer is twin else (lambda: gate_sems.at[b()])
        out.send(group, cond, remote(lambda: gbuf.at[b()], lambda: gbuf.at[b()], sem, peer))

    def arrived(k, b):
        landed(buf.at[b, :, rows_of(k)], recv_sems.at[k, b])
        if k == 0:
            landed(gbuf.at[b], gate_sems.at[b])

    def own(k):
        mine = lambda: me
        push(OWN, None, mine, k, over)
        push(OWN, can_up, mine, k, up)
        push(OWN, can_down, mine, k, down)
        push(OWN, None, mine, k, twin)

    def relay(k, off):
        cond = z + off >= 0 if off < 0 else z + off <= last
        more, onward = (can_up, up) if off < 0 else (can_down, down)
        b = lambda: index_of(z + off, y, c)
        pl.when(cond)(lambda: arrived(k, b()))
        group = WIDE if wide[k] else PASS
        if abs(off) < depth - 1:
            push(group, cond & more, b, k, onward)
        if not wide[k]:
            push(group, cond, b, k, over)
        push(group, cond, b, k, twin)

    def cross(k, off):
        b = lambda: index_of(z + off, 1 - y, c)
        cond = None if off == 0 else z + off >= 0 if off < 0 else z + off <= last
        group = WIDE if wide[k] else PASS
        if cond is None:
            arrived(k, b())
        else:
            pl.when(cond)(lambda: arrived(k, b()))
        if wide[k] and abs(off) < depth - 1:
            if off <= 0:
                push(group, can_up if cond is None else cond & can_up, b, k, up)
            if off >= 0:
                push(group, can_down if cond is None else cond & can_down, b, k, down)
        push(group, cond, b, k, twin)

    def finish(k):
        landed(buf.at[pl.ds(0, devices // 2), :, rows_of(k)], pair_sems.at[k])

    lane = lax.broadcasted_iota(jnp.int32, (tok, lanes), 1)
    expert = lax.broadcasted_iota(jnp.int32, (devices, tok), 0)

    def send_gates():
        copies = jnp.ones((devices, tok), f32)
        for d in range(devices):
            copies = copies + jnp.where(expert == table_ref[d], 1.0, 0.0)
        dense = jnp.zeros((devices, tok), f32)
        named = jnp.zeros((devices, tok), f32)
        for k in range(ids_ref.shape[0]):
            hot = ids_ref[k : k + 1] == expert
            dense = jnp.where(hot, gates_ref[k : k + 1].astype(f32), dense)
            named = jnp.where(hot, 1.0, named)
        row = lax.broadcasted_iota(jnp.int32, (tok, tok), 0)
        col = lax.broadcasted_iota(jnp.int32, (tok, tok), 1)
        earlier = jnp.where(row < col, 1.0, 0.0).astype(bf16)
        rank = jnp.dot(named.astype(bf16), earlier, preferred_element_type=f32)
        position = jnp.floor((rank + 0.5) / copies)
        turn = rank + me.astype(f32)
        copy_index = turn - copies * jnp.floor((turn + 0.5) / copies)
        limit = jnp.where(copy_index < 0.5, float(home_cap), float(rep_cap))
        gbuf[me] = jnp.where((named > 0.5) & (position < limit), dense, 0.0).astype(bf16)
        for cond, peer in ((None, over), (can_up, up), (can_down, down), (None, twin)):
            push_gates(GATE, cond, lambda: me, peer)

    def take_gates():
        landed(gbuf.at[pl.ds(0, devices // 2)], gate_sem)
        flat = gbuf[...].reshape(devices * devices, tok)
        r = lax.broadcasted_iota(jnp.int32, (devices * devices, lanes), 0)
        l = lax.broadcasted_iota(jnp.int32, (devices * devices, lanes), 1)
        pick = jnp.where(r == l * devices + me, 1.0, 0.0).astype(bf16)
        gcol[...] = lax.dot_general(flat, pick, contract_rows, preferred_element_type=f32)
        ggcol[...] = jnp.zeros_like(ggcol)

    def units(k):
        if chunks[k][1] * devices <= 256 or depth % 2:
            return [(0, depth)]
        first = jnp.where(z < half, half, 0)
        return [(first, half), (half - first, half)]

    def forward(k, u):
        if u >= len(units(k)):
            return
        r0, size = chunks[k]
        p0, planes = units(k)[u]
        nb = planes * 4
        at = pl.ds(p0 * 4, nb)
        rows = pl.ds(r0, size)
        x = buf[at, 0, rows, :].reshape(nb * size, width)
        dy = buf[at, 1, rows, :].reshape(nb * size, width)
        g = gcol[rows, :]
        spot = lane[:size]
        gate = jnp.concatenate(
            [
                jnp.sum(jnp.where(spot == p0 * 4 + j, g, 0.0), axis=1, keepdims=True)
                for j in range(nb)
            ],
            axis=0,
        )
        ab = jnp.dot(x, w1[...], preferred_element_type=f32)
        a, b = ab[:, :hidden], ab[:, hidden:]
        v = lax.dot_general(dy, wd[...], contract_cols, preferred_element_type=f32)
        sig = jax.nn.sigmoid(a)
        act = a * sig
        product = act * b
        gate_grad = jnp.sum(product.astype(bf16).astype(f32) * v, axis=1, keepdims=True)
        gate_grad = jnp.where(gate > 0, gate_grad, 0.0)
        gu = gate * v
        da = (gu * b * sig * (1.0 + a * (1.0 - sig))).astype(bf16)
        db = (gu * act).astype(bf16)
        both_grads = jnp.concatenate([da, db], axis=1)
        hgb[k % 2, at, pl.ds(0, size), :] = (gate * product).astype(bf16).reshape(nb, size, hidden)
        dadb[k % 2, at, pl.ds(0, size), :] = both_grads.reshape(nb, size, 2 * hidden)
        back = lax.dot_general(both_grads, w1[...], contract_cols, preferred_element_type=f32)
        dx[pl.ds(p0, planes), :, :, rows, :] = back.astype(bf16).reshape(
            planes, 2, 2, size, width
        )
        held = ggcol[rows, :]
        for j in range(nb):
            held = jnp.where(spot == p0 * 4 + j, gate_grad[j * size : (j + 1) * size], held)
        ggcol[rows, :] = held
        src = lambda: dx.at[pl.ds(p0, planes), :, 1 - c, rows, :]
        dst = lambda: rc.at[pl.ds(p0, planes), :, rows, :]
        out.send(PAIR, None, remote(src, dst, lambda: twin_sems.at[k, u], twin))

    def twin_sums(k):
        for u, (p0, planes) in enumerate(units(k)):
            landed(rc.at[pl.ds(p0, planes), :, rows_of(k), :], twin_sems.at[k, u])

    tile = 256 if width % 256 == 0 else 128

    def weight_tile(k, j, which):
        size = chunks[k][1]
        rows = rows_of(k)
        cols = pl.ds(j * tile, tile)
        first, final = k == 0, k == len(chunks) - 1
        if which == 0:
            x = buf[:, 0, rows, cols].reshape(devices * size, tile)
            d = dadb[k % 2, :, pl.ds(0, size), :].reshape(devices * size, 2 * hidden)
            v = lax.dot_general(x, d, contract_rows, preferred_element_type=f32)
            if not first:
                v = v + acc1[cols, :]
            if final:
                dwg_ref[cols, :] = v[:, :hidden].astype(bf16)
                dwu_ref[cols, :] = v[:, hidden:].astype(bf16)
            else:
                acc1[cols, :] = v
        else:
            dy = buf[:, 1, rows, cols].reshape(devices * size, tile)
            h = hgb[k % 2, :, pl.ds(0, size), :].reshape(devices * size, hidden)
            v = lax.dot_general(h, dy, contract_rows, preferred_element_type=f32)
            if not first:
                v = v + acc2[:, cols]
            if final:
                dwd_ref[:, cols] = v.astype(bf16)
            else:
                acc2[:, cols] = v

    def weights(k, which):
        for j in range(width // tile):
            weight_tile(k, j, which)
        if k == len(chunks) - 1:
            for copy in (results[2:4], results[4:])[which]:
                copy.start()

    def part_sum(zz, yy, rows, extra):
        total = dx[zz, yy, c, rows, :].astype(f32) + rc[zz, yy, rows, :].astype(f32)
        for ref in extra:
            total = total + ref[zz, yy, rows, :].astype(f32)
        return total

    def trade(k):
        if not early[k]:
            return
        twin_sums(k)
        rows = rows_of(k)
        for i in range(depth):
            zz = jnp.where(2 * z < depth, last - i, i)
            xsend[zz, rows, :] = part_sum(zz, 1 - y, rows, ()).astype(bf16)
            out.send(
                TRADE, None,
                remote(
                    lambda zz=zz: xsend.at[zz, rows, :], lambda zz=zz: xr.at[zz, rows, :],
                    lambda zz=zz: x_sems.at[k, zz], over,
                ),
            )

    def traded(k, zz):
        landed(xr.at[zz, rows_of(k), :], x_sems.at[k, zz])
        return part_sum(zz, y, rows_of(k), ()) + xr[zz, rows_of(k), :].astype(f32)

    def chain(k, p):
        rows = rows_of(k)
        for there, zz, ref, sems, has, peer in (
            (z <= p, z + last - p, rzu, up_sems, z > 0, up),
            (last - z <= p, z + p - last, rzd, down_sems, z < last, down),
        ):
            piece = ref.at[zz, 0, rows, :] if early[k] else ref.at[zz, :, rows, :]

            def step():
                pl.when(has)(lambda: landed(piece, sems.at[k, zz]))
                if early[k]:
                    held = ref[zz, 0, rows, :].astype(f32)
                    ref[zz, 0, rows, :] = (traded(k, zz) + held).astype(bf16)
                else:
                    for yy in range(2):
                        ref[zz, yy, rows, :] = part_sum(zz, yy, rows, (ref,)).astype(bf16)

            pl.when(there)(step)
            out.send(
                THIN if early[k] else CHAIN, there,
                remote(lambda: piece, lambda: piece, lambda: sems.at[k, zz], peer),
            )

    def home(k):
        rows = rows_of(k)
        way = 0 if early[k] else slice(None)
        pl.when(z > 0)(lambda: landed(rzu.at[z, way, rows, :], up_sems.at[k, z]))
        pl.when(z < last)(lambda: landed(rzd.at[z, way, rows, :], down_sems.at[k, z]))
        if early[k]:
            held = rzu[z, 0, rows, :].astype(f32) + rzd[z, 0, rows, :].astype(f32)
            out_ref[rows, :] = (traded(k, z) + held).astype(bf16)
            return
        ysend[rows, :] = part_sum(z, 1 - y, rows, (rzu, rzd)).astype(bf16)
        out.send(
            HOME, None,
            remote(
                lambda: ysend.at[rows, :], lambda: ry.at[rows, :], lambda: y_sems.at[k], over
            ),
        )

    def total(k):
        if early[k]:
            return
        rows = rows_of(k)
        mine = part_sum(z, y, rows, (rzu, rzd))
        landed(ry.at[rows, :], y_sems.at[k])
        out_ref[rows, :] = (mine + ry[rows, :].astype(f32)).astype(bf16)

    def scatter_point(k, p):
        if p == 0 and not early[k]:
            twin_sums(k)
        if p < depth - 1:
            chain(k, p)
        else:
            home(k)

    def send_gate_grads():
        turned = ggcol[...].T
        for b in range(devices):
            ggs[b] = turned[b : b + 1]
        ggr[me] = ggs[me]
        for peer in range(devices):
            out.send(
                BACK, peer != me,
                remote(
                    lambda peer=peer: ggs.at[peer], lambda: ggr.at[me], lambda: gg_sem,
                    lambda peer=peer: peer,
                ),
            )

    def take_gate_grads():
        landed(ggr.at[pl.ds(0, devices - 1)], gg_sem)
        held = ggr[...].reshape(devices, tok)
        for k in range(ids_ref.shape[0]):
            hot = ids_ref[k : k + 1] == expert
            picked = jnp.sum(jnp.where(hot, held, 0.0), axis=0, keepdims=True)
            ggo_ref[k : k + 1] = picked.astype(bf16)
        results[1].start()

    def gates_out(k):
        for copy in plan_copies:
            copy.wait()
        send_gates()

        @pl.when(z == 0)
        def _():
            rzu[...] = jnp.zeros_like(rzu)

        @pl.when(z == last)
        def _():
            rzd[...] = jnp.zeros_like(rzd)

    def ready(k):
        finish(k)
        if k == 0:
            take_gates()
            for copy in weight_copies:
                copy.wait()

    steps = dict(
        own=own, gates=gates_out, relay=relay, cross=cross, finish=ready, fwd=forward,
        wg=weights, trade=trade, sc=scatter_point, total=total, ggout=lambda k: send_gate_grads(),
        ggin=lambda k: take_gate_grads(),
    )
    for name, *rest in order:
        steps[name](*rest)

    results[0].start()

    def rows_in(flags, want):
        return sum(size for (_, size), flag in zip(chunks, flags) if flag == want)

    def sent_blocks(zz):
        ends = (zz < depth - 1) + (zz > 0)
        passed, widened = depth, 1 + ends
        for off in range(1, depth):
            mid = off < depth - 1
            below, above = zz >= off, zz + off < depth
            passed += below * (2 + (zz < depth - 1 and mid)) + above * (2 + (zz > 0 and mid))
            widened += 2 * below * (1 + (zz < depth - 1 and mid))
            widened += 2 * above * (1 + (zz > 0 and mid))
        out.sent(OWN, buf.at[pl.ds(0, 2 + ends)])
        out.sent(GATE, gbuf.at[pl.ds(0, 2 + ends)])
        out.sent(FLAT, gbuf.at[pl.ds(0, widened if wide[0] else passed)])
        for group, count, want in ((PASS, passed, False), (WIDE, widened, True)):
            if rows_in(wide, want):
                out.sent(group, buf.at[pl.ds(0, count), :, pl.ds(0, rows_in(wide, want))])

    for zz in range(depth):
        pl.when(z == zz)(lambda: sent_blocks(zz))
    out.sent(PAIR, rc)
    late, soon = rows_in(early, False), rows_in(early, True)
    if late:
        out.sent(HOME, ysend.at[pl.ds(0, late)])
    if soon:
        out.sent(TRADE, xsend.at[:, pl.ds(0, soon)])
    if depth > 1 and late:
        out.sent(CHAIN, rzu.at[pl.ds(0, depth - 1), :, pl.ds(0, late)])
    if depth > 1 and soon:
        out.sent(THIN, rzu.at[pl.ds(0, depth - 1), 0, pl.ds(0, soon)])
    out.sent(BACK, ggs.at[pl.ds(0, devices - 1)])
    for copy in results:
        copy.wait()


def fused_grads(x, dy, gates, ids, table, gate_w, up_w, down_w, devices, home_cap, rep_cap):
    depth = devices // 4
    tok, width = x.shape
    hidden = down_w.shape[0]
    f32, bf16 = jnp.float32, jnp.bfloat16
    n = len(row_chunks(tok))
    most = max(size for _, size in row_chunks(tok))
    vmem, dma = pltpu.VMEM, pltpu.SemaphoreType.DMA
    hbm = pl.BlockSpec(memory_space=pltpu.HBM)
    shape = jax.ShapeDtypeStruct
    outs = pl.pallas_call(
        lambda *refs: fused_kernel(depth, step_order(depth, n), home_cap, rep_cap, *refs),
        out_shape=[
            shape((tok, width), bf16), shape(gates.shape, bf16), shape(gate_w.shape, bf16),
            shape(up_w.shape, bf16), shape(down_w.shape, bf16),
        ],
        in_specs=[hbm] * 8,
        out_specs=[hbm] * 5,
        scratch_shapes=[
            vmem((tok, width), bf16), vmem(gates.shape, bf16), vmem(gate_w.shape, bf16),
            vmem(up_w.shape, bf16), vmem(down_w.shape, bf16),
            vmem((devices, 2, tok, width), bf16), vmem((devices, devices, tok), bf16),
            vmem((tok, 128), f32), vmem((tok, 128), f32),
            vmem((devices, 1, tok), f32), vmem((devices, 1, tok), f32),
            vmem((width, 2 * hidden), bf16), vmem((hidden, width), bf16),
            vmem((2, devices, most, 2 * hidden), bf16), vmem((2, devices, most, hidden), bf16),
            vmem((width, 2 * hidden), f32), vmem((hidden, width), f32),
            vmem((depth, 2, 2, tok, width), bf16), vmem((depth, 2, tok, width), bf16),
            vmem((depth, 2, tok, width), bf16), vmem((depth, 2, tok, width), bf16),
            vmem((tok, width), bf16), vmem((tok, width), bf16),
            vmem((depth, tok, width), bf16), vmem((depth, tok, width), bf16),
            vmem(gates.shape, bf16), vmem(ids.shape, ids.dtype),
            pltpu.SMEM(table.shape, table.dtype),
            dma((13,)), dma((12,)), dma((n, devices)), dma((n,)), dma, dma,
            dma((n, 2)), dma((n, depth)), dma((n, depth)), dma((n,)), dma((n, depth)), dma((devices,)),
        ],
        compiler_params=pltpu.CompilerParams(
            collective_id=0, has_side_effects=True, vmem_limit_bytes=VMEM_GRANT
        ),
    )(x, dy, gates, ids, table, gate_w, up_w, down_w)
    return store_all(outs)


def store_kernel(n, cuts, *refs):
    src, dst, held, (load_sems, store_sems) = refs[:n], refs[n : 2 * n], refs[2 * n : -2], refs[-2:]
    loads, stores = [], []
    for i in range(n):
        step = src[i].shape[0] // cuts[i]
        for j in range(cuts[i]):
            rows = pl.ds(j * step, step)
            m = len(loads)
            loads.append(
                pltpu.make_async_copy(src[i].at[rows], held[i].at[rows], load_sems.at[m])
            )
            stores.append(
                pltpu.make_async_copy(held[i].at[rows], dst[i].at[rows], store_sems.at[m])
            )
    for copy in loads:
        copy.start()
    for load, store in zip(loads, stores):
        load.wait()
        store.start()
    for copy in stores:
        copy.wait()


def store_all(arrays):
    n = len(arrays)
    cuts = [2 if v.shape[0] >= 256 and v.shape[0] % 64 == 0 else 1 for v in arrays]
    hbm = pl.BlockSpec(memory_space=pltpu.HBM)
    return pl.pallas_call(
        lambda *refs: store_kernel(n, cuts, *refs),
        out_shape=[jax.ShapeDtypeStruct(v.shape, v.dtype) for v in arrays],
        in_specs=[hbm] * n,
        out_specs=[hbm] * n,
        scratch_shapes=[pltpu.VMEM(v.shape, v.dtype) for v in arrays]
        + [pltpu.SemaphoreType.DMA((sum(cuts),))] * 2,
        compiler_params=pltpu.CompilerParams(vmem_limit_bytes=VMEM_GRANT),
    )(*arrays)


def keep_plan(gates, row_ids, replica_table, source, devices, home_cap, rep_cap):
    tok = row_ids.shape[0]
    experts = jnp.arange(devices, dtype=jnp.int32)
    hot = row_ids[:, :, None] == experts[None, None, :]
    named = jnp.any(hot, axis=1)
    dense_gate = jnp.sum(jnp.where(hot, gates.astype(jnp.float32)[:, :, None], 0.0), axis=1)
    copies = 1 + jnp.sum((replica_table[:, None] == experts[None, :]).astype(jnp.int32), axis=0)
    order = jnp.arange(tok, dtype=jnp.int32)
    earlier = (order[:, None] > order[None, :]).astype(jnp.bfloat16)
    rank = jnp.dot(earlier, named.astype(jnp.bfloat16), preferred_element_type=jnp.float32)
    many = copies.astype(jnp.float32)[None, :]
    position = jnp.floor((rank + 0.5) / many)
    turn = rank + source.astype(jnp.float32)
    copy_index = turn - many * jnp.floor((turn + 0.5) / many)
    limit = jnp.where(copy_index < 0.5, float(home_cap), float(rep_cap))
    kept = named & (position < limit)
    return jnp.where(kept, dense_gate, 0.0).astype(jnp.bfloat16)


def row_grads(x, dy, gate, gate_w, up_w, down_w):
    a = jnp.dot(x, gate_w, preferred_element_type=jnp.float32)
    b = jnp.dot(x, up_w, preferred_element_type=jnp.float32)
    u = lax.dot_general(dy, down_w, contract_cols, preferred_element_type=jnp.float32)
    sig = jax.nn.sigmoid(a)
    act = a * sig
    product = act * b
    hidden = product.astype(jnp.bfloat16).astype(jnp.float32)
    gate_grad = jnp.sum(hidden * u, axis=1, keepdims=True)
    gate_grad = jnp.where(gate > 0, gate_grad, 0.0)
    hg = (gate * product).astype(jnp.bfloat16)
    gu = gate * u
    da = (gu * b * sig * (1.0 + a * (1.0 - sig))).astype(jnp.bfloat16)
    db = (gu * act).astype(jnp.bfloat16)
    dx = lax.dot_general(da, gate_w, contract_cols, preferred_element_type=jnp.float32)
    dx = dx + lax.dot_general(db, up_w, contract_cols, preferred_element_type=jnp.float32)
    return gate_grad, hg, da, db, dx


def weight_grads(x, dy, hg, da, db):
    dwg = lax.dot_general(x, da, contract_rows, preferred_element_type=jnp.float32)
    dwu = lax.dot_general(x, db, contract_rows, preferred_element_type=jnp.float32)
    dwd = lax.dot_general(hg, dy, contract_rows, preferred_element_type=jnp.float32)
    return dwg, dwu, dwd


def on_device(tokens_in, grad_out, gates, expert_ids, replica_table, w_gate, w_up, w_down):
    devices = lax.axis_size("expert")
    me = lax.axis_index("expert")
    tok, width = tokens_in.shape
    home_cap = max(2, 5 * tok * TOP // (4 * devices))
    rep_cap = max(2, tok * TOP // (2 * devices))
    if devices * tok <= ROWS_PER_CHUNK and devices % 16 == 0 and devices <= 128 and tok % 128 == 0:
        outs = fused_grads(
            tokens_in, grad_out, gates.T, expert_ids.T, replica_table, w_gate[0], w_up[0], w_down[0],
            devices, home_cap, rep_cap,
        )
        return (outs[0], outs[1].T, *[g[None] for g in outs[2:]])
    kept_gate = keep_plan(gates, expert_ids, replica_table, me, devices, home_cap, rep_cap)
    lanes = -(-devices // 128) * 128
    kept_gate = jnp.pad(kept_gate, ((0, 0), (0, lanes - devices)))
    payload = jnp.concatenate([tokens_in, grad_out, kept_gate], axis=1)
    chunks = max(1, devices * tok // ROWS_PER_CHUNK)
    part = tok // chunks
    mine = jnp.arange(lanes, dtype=jnp.int32)[None, :] == me
    backs, sums = [], None
    for c in range(chunks):
        rows = lax.all_gather(payload[c * part : (c + 1) * part], "expert", axis=0, tiled=True)
        gate = jnp.sum(
            jnp.where(mine, rows[:, 2 * width :].astype(jnp.float32), 0.0),
            axis=1,
            keepdims=True,
        )
        gate_grad, hg, da, db, dx = row_grads(
            rows[:, :width], rows[:, width : 2 * width], gate, w_gate[0], w_up[0], w_down[0]
        )
        spread = jnp.where(mine, gate_grad, 0.0).astype(jnp.bfloat16)
        back = jnp.concatenate([dx.astype(jnp.bfloat16), spread], axis=1)
        backs.append(lax.psum_scatter(back, "expert", scatter_dimension=0, tiled=True))
        grads = weight_grads(rows[:, :width], rows[:, width : 2 * width], hg, da, db)
        sums = grads if sums is None else [p + q for p, q in zip(sums, grads)]
        if c + 1 < chunks:
            payload, sums = lax.optimization_barrier((payload, sums))
    back = jnp.concatenate(backs, axis=0)
    experts = jnp.arange(devices, dtype=jnp.int32)
    hot = expert_ids[:, :, None] == experts[None, None, :]
    picked = jnp.where(hot, back[:, None, width : width + devices].astype(jnp.float32), 0.0)
    grad_gates = jnp.sum(picked, axis=2).astype(jnp.bfloat16)
    return (back[:, :width], grad_gates, *[g.astype(jnp.bfloat16)[None] for g in sums])


def solution(mesh):
    return jax.shard_map(
        on_device,
        mesh=mesh,
        in_specs=(
            P(("groups", "expert"), None),
            P(("groups", "expert"), None),
            P(("groups", "expert"), None),
            P(("groups", "expert"), None),
            P("groups"),
            P("expert", None, None),
            P("expert", None, None),
            P("expert", None, None),
        ),
        out_specs=(
            P(("groups", "expert"), None),
            P(("groups", "expert"), None),
            P(("groups", "expert"), None, None),
            P(("groups", "expert"), None, None),
            P(("groups", "expert"), None, None),
        ),
        check_vma=False,
    )
```

```python
import jax
import jax.numpy as jnp
from jax import lax
from jax.experimental import pallas as pl
from jax.experimental.pallas import tpu as pltpu
from jax.sharding import PartitionSpec as P

TOP = 8
ROWS_PER_CHUNK = 4096

contract_rows = (((0,), (0,)), ((), ()))
contract_cols = (((1,), (1,)), ((), ()))

MESH = pl.DeviceIdType.MESH
VMEM_GRANT = 58 * 2**20


def place(depth):
    me = lax.axis_index("expert")
    z, y, c = me // 4, (me // 2) % 2, me % 2
    return me, z, y, c, depth - 1


def index_of(z, y, c):
    return (z * 2 + y) * 2 + c


def greet(z, y, c, last):
    sem = pltpu.get_barrier_semaphore()

    def hello(peer):
        pl.semaphore_signal(sem, inc=1, device_id={"expert": peer}, device_id_type=MESH)

    hello(index_of(z, y, 1 - c))
    hello(index_of(z, 1 - y, c))
    pl.when(z > 0)(lambda: hello(index_of(z - 1, y, c)))
    pl.when(z < last)(lambda: hello(index_of(z + 1, y, c)))
    pl.semaphore_wait(sem, 2 + (z > 0).astype(jnp.int32) + (z < last).astype(jnp.int32))


class Sender:
    def __init__(self, sems):
        self.sems = sems

    def send(self, group, cond, make):
        if cond is None:
            make(self.sems.at[group]).start()
        else:
            pl.when(cond)(lambda: make(self.sems.at[group]).start())

    def sent(self, group, ref):
        pltpu.make_async_copy(ref, ref, self.sems.at[group]).wait()


def remote(src, dst, recv_sem, peer):
    return lambda send_sem: pltpu.make_async_remote_copy(
        src_ref=src(), dst_ref=dst(), send_sem=send_sem, recv_sem=recv_sem(),
        device_id={"expert": peer()}, device_id_type=MESH,
    )


def landed(ref, sem):
    pltpu.make_async_copy(ref, ref, sem).wait()


TUNED_DEPTH = 4
TUNED_SHARES = (16, 32, 32, 16, 16, 16)
PAIR_FIRST = (False, False, True, True, True, True)
BOTH_COLUMNS = (False, False, False, True, False, True)
TUNED = [
    ("own", 0), ("gates", 0), ("own", 1), ("relay", 0, 1), ("relay", 0, -1), ("relay", 1, 1),
    ("relay", 0, 2), ("relay", 1, -1), ("cross", 0, 0), ("relay", 0, -2), ("cross", 1, 0),
    ("own", 2), ("cross", 1, 1), ("relay", 0, 3), ("relay", 0, -3), ("relay", 1, 2),
    ("cross", 0, 2), ("cross", 0, 1), ("relay", 1, -2), ("cross", 0, 3), ("cross", 0, -1),
    ("own", 3), ("relay", 1, 3), ("relay", 2, 1), ("cross", 0, -2), ("cross", 0, -3),
    ("relay", 1, -3), ("finish", 0), ("relay", 2, -1), ("fwd", 0, 0), ("relay", 2, -2),
    ("relay", 3, -1), ("relay", 2, 2), ("trade", 0), ("wg", 0, 0), ("cross", 1, 2),
    ("cross", 1, -1), ("cross", 1, -2), ("cross", 1, 3), ("relay", 2, 3), ("cross", 1, -3),
    ("cross", 3, 0), ("relay", 2, -3), ("own", 4), ("cross", 2, 0), ("relay", 3, 1), ("sc", 0, 0),
    ("finish", 1), ("fwd", 1, 0), ("own", 5), ("fwd", 1, 1), ("cross", 3, -1), ("wg", 0, 1),
    ("cross", 2, -1), ("relay", 4, 1), ("cross", 3, 1), ("relay", 4, -1), ("cross", 2, 1),
    ("wg", 1, 0), ("sc", 0, 1), ("cross", 2, 2), ("relay", 3, 2), ("cross", 2, -2),
    ("cross", 2, -3), ("cross", 2, 3), ("relay", 4, 2), ("cross", 3, -2), ("trade", 1),
    ("sc", 1, 0), ("wg", 1, 1), ("relay", 4, -2), ("relay", 3, -2), ("cross", 3, 2),
    ("finish", 2), ("fwd", 2, 0), ("cross", 5, 0), ("fwd", 2, 1), ("relay", 4, -3),
    ("relay", 4, 3), ("relay", 5, 1), ("relay", 5, -1), ("wg", 2, 0), ("cross", 3, 3),
    ("relay", 3, -3), ("cross", 3, -3), ("relay", 3, 3), ("wg", 2, 1), ("cross", 5, 1),
    ("cross", 5, -1), ("trade", 2), ("cross", 4, -1), ("cross", 4, 0), ("cross", 4, 1),
    ("sc", 1, 1), ("cross", 4, -3), ("cross", 4, -2), ("finish", 3), ("cross", 4, 2),
    ("cross", 4, 3), ("relay", 5, 2), ("relay", 5, -2), ("fwd", 3, 0), ("cross", 5, 2),
    ("finish", 4), ("cross", 5, -2), ("sc", 0, 2), ("fwd", 4, 0), ("sc", 2, 0), ("relay", 5, -3),
    ("relay", 5, 3), ("trade", 3), ("wg", 3, 1), ("cross", 5, 3), ("cross", 5, -3), ("sc", 1, 2),
    ("wg", 3, 0), ("trade", 4), ("finish", 5), ("fwd", 5, 0), ("sc", 2, 1), ("ggout", 0),
    ("sc", 3, 0), ("sc", 4, 0), ("trade", 5), ("sc", 2, 2), ("wg", 4, 1), ("sc", 5, 0),
    ("sc", 4, 1), ("sc", 3, 1), ("sc", 0, 3), ("wg", 5, 1), ("sc", 1, 3), ("wg", 4, 0),
    ("sc", 5, 1), ("sc", 4, 2), ("sc", 3, 2), ("total", 0), ("total", 1), ("sc", 5, 2),
    ("ggin", 0), ("sc", 4, 3), ("sc", 3, 3), ("total", 3), ("sc", 2, 3), ("wg", 5, 0),
    ("total", 2), ("sc", 5, 3), ("total", 5), ("total", 4),
]


def row_chunks(tok):
    whole = sum(TUNED_SHARES)
    sizes = [tok * share // whole for share in TUNED_SHARES]
    return [(sum(sizes[:k]), size) for k, size in enumerate(sizes)]


def unit_counts(tok, devices):
    whole = devices % 8 != 0
    return [1 if whole or size * devices <= 256 else 2 for _, size in row_chunks(tok)]


def step_order(depth, n):
    if depth == TUNED_DEPTH:
        return TUNED
    steps = [("own", 0), ("gates", 0)]
    for k in range(n):
        steps += [("own", k)] if k else []
        for d in range(1, depth):
            steps += [("relay", k, -d), ("relay", k, d)]
        steps += [("cross", k, d) for d in range(1 - depth, depth)]
        steps += [("finish", k), ("fwd", k, 0), ("fwd", k, 1), ("wg", k, 0), ("wg", k, 1)]
        steps += [("trade", k)] + [("sc", k, p) for p in range(depth)] + [("total", k)]
    return steps + [("ggout", 0), ("ggin", 0)]


def fused_kernel(
    depth, order, home_cap, rep_cap,
    x_hbm, dy_hbm, gates_hbm, ids_hbm, table_hbm, wg_hbm, wu_hbm, wd_hbm,
    out_hbm, ggo_hbm, dwg_hbm, dwu_hbm, dwd_hbm,
    out_ref, ggo_ref, dwg_ref, dwu_ref, dwd_ref,
    buf, gbuf, gcol, ggcol, ggs, ggr, w1, wd, dadb, hgb, acc1, acc2, dx, rc, rzu, rzd, ysend, ry, xsend, xr,
    gates_ref, ids_ref, table_ref,
    local_sems, send_sems, recv_sems, pair_sems, gate_sem, gg_sem, twin_sems, chain_sems,
    y_sems, x_sems, gate_sems,
):
    f32, bf16 = jnp.float32, jnp.bfloat16
    devices = 4 * depth
    early, wide = PAIR_FIRST, BOTH_COLUMNS
    counts = unit_counts(x_hbm.shape[0], devices)
    me, z, y, c, last = place(depth)
    tok, width = x_hbm.shape
    hidden = wd_hbm.shape[0]
    chunks = row_chunks(tok)
    lanes = gcol.shape[1]

    def local(src, dst, i):
        return pltpu.make_async_copy(src, dst, local_sems.at[i])

    own_copies = [local(x_hbm, buf.at[me, 0], 0), local(dy_hbm, buf.at[me, 1], 0)]
    weight_copies = [
        local(wg_hbm, w1.at[:, pl.ds(0, hidden)], 1),
        local(wu_hbm, w1.at[:, pl.ds(hidden, hidden)], 1),
        local(wd_hbm, wd, 2),
    ]
    plan_copies = [
        local(gates_hbm, gates_ref, 3), local(ids_hbm, ids_ref, 4), local(table_hbm, table_ref, 5),
    ]
    results = [
        local(out_ref, out_hbm, 6), local(ggo_ref, ggo_hbm, 7), local(dwg_ref, dwg_hbm, 8),
        local(dwu_ref, dwu_hbm, 9), local(dwd_ref, dwd_hbm, 10),
    ]
    for copy in own_copies + plan_copies + weight_copies:
        copy.start()
    greet(z, y, c, last)
    landed(buf.at[me], local_sems.at[0])

    out = Sender(send_sems)
    up = lambda: index_of(z + 1, y, c)
    down = lambda: index_of(z - 1, y, c)
    over = lambda: index_of(z, 1 - y, c)
    twin = lambda: index_of(z, y, 1 - c)
    can_up, can_down = z < last, z > 0
    half = depth // 2

    def rows_of(k):
        return pl.ds(*chunks[k])

    OWN, PASS, WIDE, PAIR, CHAIN, THIN, TRADE, HOME, GATE, BACK, FLAT = range(11)

    def push(group, cond, b, k, peer):
        block = lambda: buf.at[b(), :, rows_of(k)]
        sem = (lambda: pair_sems.at[k]) if peer is twin else (lambda: recv_sems.at[k, b() // 2])
        out.send(group, cond, remote(block, block, sem, peer))
        if k == 0 and group != OWN:
            push_gates(FLAT, cond, b, peer)

    def push_gates(group, cond, b, peer):
        sem = (lambda: gate_sem) if peer is twin else (lambda: gate_sems.at[b() // 2])
        out.send(group, cond, remote(lambda: gbuf.at[b()], lambda: gbuf.at[b()], sem, peer))

    def arrived(k, b):
        landed(buf.at[b, :, rows_of(k)], recv_sems.at[k, b // 2])
        if k == 0:
            landed(gbuf.at[b], gate_sems.at[b // 2])

    def own(k):
        mine = lambda: me
        push(OWN, None, mine, k, over)
        push(OWN, can_up, mine, k, up)
        push(OWN, can_down, mine, k, down)
        push(OWN, None, mine, k, twin)

    def relay(k, off):
        cond = z + off >= 0 if off < 0 else z + off <= last
        more, onward = (can_up, up) if off < 0 else (can_down, down)
        b = lambda: index_of(z + off, y, c)
        pl.when(cond)(lambda: arrived(k, b()))
        group = WIDE if wide[k] else PASS
        if abs(off) < depth - 1:
            push(group, cond & more, b, k, onward)
        if not wide[k]:
            push(group, cond, b, k, over)
        push(group, cond, b, k, twin)

    def cross(k, off):
        b = lambda: index_of(z + off, 1 - y, c)
        cond = None if off == 0 else z + off >= 0 if off < 0 else z + off <= last
        group = WIDE if wide[k] else PASS
        if cond is None:
            arrived(k, b())
        else:
            pl.when(cond)(lambda: arrived(k, b()))
        if wide[k] and abs(off) < depth - 1:
            if off <= 0:
                push(group, can_up if cond is None else cond & can_up, b, k, up)
            if off >= 0:
                push(group, can_down if cond is None else cond & can_down, b, k, down)
        push(group, cond, b, k, twin)

    def finish(k):
        landed(buf.at[pl.ds(0, devices // 2), :, rows_of(k)], pair_sems.at[k])

    lane = lax.broadcasted_iota(jnp.int32, (tok, lanes), 1)
    expert = lax.broadcasted_iota(jnp.int32, (devices, tok), 0)

    def send_gates():
        copies = jnp.ones((devices, tok), f32)
        for d in range(devices):
            copies = copies + jnp.where(expert == table_ref[d], 1.0, 0.0)
        dense = jnp.zeros((devices, tok), f32)
        named = jnp.zeros((devices, tok), f32)
        for k in range(ids_ref.shape[0]):
            hot = ids_ref[k : k + 1] == expert
            dense = jnp.where(hot, gates_ref[k : k + 1].astype(f32), dense)
            named = jnp.where(hot, 1.0, named)
        row = lax.broadcasted_iota(jnp.int32, (tok, tok), 0)
        col = lax.broadcasted_iota(jnp.int32, (tok, tok), 1)
        earlier = jnp.where(row < col, 1.0, 0.0).astype(bf16)
        rank = jnp.dot(named.astype(bf16), earlier, preferred_element_type=f32)
        position = jnp.floor((rank + 0.5) / copies)
        turn = rank + me.astype(f32)
        copy_index = turn - copies * jnp.floor((turn + 0.5) / copies)
        limit = jnp.where(copy_index < 0.5, float(home_cap), float(rep_cap))
        gbuf[me] = jnp.where((named > 0.5) & (position < limit), dense, 0.0).astype(bf16)
        for cond, peer in ((None, over), (can_up, up), (can_down, down), (None, twin)):
            push_gates(GATE, cond, lambda: me, peer)

    def take_gates():
        landed(gbuf.at[pl.ds(0, devices // 2)], gate_sem)
        flat = gbuf[...].reshape(devices * devices, tok)
        r = lax.broadcasted_iota(jnp.int32, (devices * devices, lanes), 0)
        l = lax.broadcasted_iota(jnp.int32, (devices * devices, lanes), 1)
        pick = jnp.where(r == l * devices + me, 1.0, 0.0).astype(bf16)
        gcol[...] = lax.dot_general(flat, pick, contract_rows, preferred_element_type=f32)
        ggcol[...] = jnp.zeros_like(ggcol)

    def units(k):
        if counts[k] == 1:
            return [(0, depth)]
        first = jnp.where(z < half, half, 0)
        return [(first, half), (half - first, half)]

    def forward(k, u):
        if u >= len(units(k)):
            return
        r0, size = chunks[k]
        p0, planes = units(k)[u]
        nb = planes * 4
        at = pl.ds(p0 * 4, nb)
        rows = pl.ds(r0, size)
        x = buf[at, 0, rows, :].reshape(nb * size, width)
        dy = buf[at, 1, rows, :].reshape(nb * size, width)
        g = gcol[rows, :]
        spot = lane[:size]
        gate = jnp.concatenate(
            [
                jnp.sum(jnp.where(spot == p0 * 4 + j, g, 0.0), axis=1, keepdims=True)
                for j in range(nb)
            ],
            axis=0,
        )
        ab = jnp.dot(x, w1[...], preferred_element_type=f32)
        a, b = ab[:, :hidden], ab[:, hidden:]
        v = lax.dot_general(dy, wd[...], contract_cols, preferred_element_type=f32)
        sig = jax.nn.sigmoid(a)
        act = a * sig
        product = act * b
        gate_grad = jnp.sum(product.astype(bf16).astype(f32) * v, axis=1, keepdims=True)
        gate_grad = jnp.where(gate > 0, gate_grad, 0.0)
        gu = gate * v
        da = (gu * b * sig * (1.0 + a * (1.0 - sig))).astype(bf16)
        db = (gu * act).astype(bf16)
        both_grads = jnp.concatenate([da, db], axis=1)
        hgb[k % 2, at, pl.ds(0, size), :] = (gate * product).astype(bf16).reshape(nb, size, hidden)
        dadb[k % 2, at, pl.ds(0, size), :] = both_grads.reshape(nb, size, 2 * hidden)
        back = lax.dot_general(both_grads, w1[...], contract_cols, preferred_element_type=f32)
        dx[pl.ds(p0, planes), :, :, rows, :] = back.astype(bf16).reshape(
            planes, 2, 2, size, width
        )
        held = ggcol[rows, :]
        for j in range(nb):
            held = jnp.where(spot == p0 * 4 + j, gate_grad[j * size : (j + 1) * size], held)
        ggcol[rows, :] = held
        src = lambda: dx.at[pl.ds(p0, planes), :, 1 - c, rows, :]
        dst = lambda: rc.at[pl.ds(p0, planes), :, rows, :]
        out.send(PAIR, None, remote(src, dst, lambda: twin_sems.at[sum(counts[:k]) + u], twin))

    def twin_sums(k):
        for u, (p0, planes) in enumerate(units(k)):
            landed(rc.at[pl.ds(p0, planes), :, rows_of(k), :], twin_sems.at[sum(counts[:k]) + u])

    tile = 256 if width % 256 == 0 else 128

    def weight_tile(k, j, which):
        size = chunks[k][1]
        rows = rows_of(k)
        cols = pl.ds(j * tile, tile)
        first, final = k == 0, k == len(chunks) - 1
        if which == 0:
            x = buf[:, 0, rows, cols].reshape(devices * size, tile)
            d = dadb[k % 2, :, pl.ds(0, size), :].reshape(devices * size, 2 * hidden)
            v = lax.dot_general(x, d, contract_rows, preferred_element_type=f32)
            if not first:
                v = v + acc1[cols, :]
            if final:
                dwg_ref[cols, :] = v[:, :hidden].astype(bf16)
                dwu_ref[cols, :] = v[:, hidden:].astype(bf16)
            else:
                acc1[cols, :] = v
        else:
            dy = buf[:, 1, rows, cols].reshape(devices * size, tile)
            h = hgb[k % 2, :, pl.ds(0, size), :].reshape(devices * size, hidden)
            v = lax.dot_general(h, dy, contract_rows, preferred_element_type=f32)
            if not first:
                v = v + acc2[:, cols]
            if final:
                dwd_ref[:, cols] = v.astype(bf16)
            else:
                acc2[:, cols] = v

    def weights(k, which):
        for j in range(width // tile):
            weight_tile(k, j, which)
        if k == len(chunks) - 1:
            for copy in (results[2:4], results[4:])[which]:
                copy.start()

    def part_sum(zz, yy, rows, extra):
        total = dx[zz, yy, c, rows, :].astype(f32) + rc[zz, yy, rows, :].astype(f32)
        for ref in extra:
            total = total + ref[zz, yy, rows, :].astype(f32)
        return total

    def trade(k):
        if not early[k]:
            return
        twin_sums(k)
        rows = rows_of(k)
        for i in range(depth):
            zz = jnp.where(2 * z < depth, last - i, i)
            xsend[zz, rows, :] = part_sum(zz, 1 - y, rows, ()).astype(bf16)
            out.send(
                TRADE, None,
                remote(
                    lambda zz=zz: xsend.at[zz, rows, :], lambda zz=zz: xr.at[zz, rows, :],
                    lambda zz=zz: x_sems.at[sum(early[:k]), zz], over,
                ),
            )

    def traded(k, zz):
        landed(xr.at[zz, rows_of(k), :], x_sems.at[sum(early[:k]), zz])
        return part_sum(zz, y, rows_of(k), ()) + xr[zz, rows_of(k), :].astype(f32)

    def chain(k, p):
        rows = rows_of(k)
        for there, zz, ref, way, has, peer in (
            (z <= p, z + last - p, rzu, 1, z > 0, up),
            (last - z <= p, z + p - last, rzd, 0, z < last, down),
        ):
            piece = ref.at[zz, 0, rows, :] if early[k] else ref.at[zz, :, rows, :]

            def step():
                pl.when(has)(lambda: landed(piece, chain_sems.at[k, zz + way]))
                if early[k]:
                    held = ref[zz, 0, rows, :].astype(f32)
                    ref[zz, 0, rows, :] = (traded(k, zz) + held).astype(bf16)
                else:
                    for yy in range(2):
                        ref[zz, yy, rows, :] = part_sum(zz, yy, rows, (ref,)).astype(bf16)

            pl.when(there)(step)
            out.send(
                THIN if early[k] else CHAIN, there,
                remote(lambda: piece, lambda: piece, lambda: chain_sems.at[k, zz + way], peer),
            )

    def home(k):
        rows = rows_of(k)
        way = 0 if early[k] else slice(None)
        pl.when(z > 0)(lambda: landed(rzu.at[z, way, rows, :], chain_sems.at[k, z + 1]))
        pl.when(z < last)(lambda: landed(rzd.at[z, way, rows, :], chain_sems.at[k, z]))
        if early[k]:
            held = rzu[z, 0, rows, :].astype(f32) + rzd[z, 0, rows, :].astype(f32)
            out_ref[rows, :] = (traded(k, z) + held).astype(bf16)
            local(out_ref.at[rows], out_hbm.at[rows], 6).start()
            return
        ysend[rows, :] = part_sum(z, 1 - y, rows, (rzu, rzd)).astype(bf16)
        out.send(
            HOME, None,
            remote(
                lambda: ysend.at[rows, :], lambda: ry.at[rows, :], lambda: y_sems.at[k - sum(early[:k])], over
            ),
        )

    def total(k):
        if early[k]:
            return
        rows = rows_of(k)
        mine = part_sum(z, y, rows, (rzu, rzd))
        landed(ry.at[rows, :], y_sems.at[k - sum(early[:k])])
        out_ref[rows, :] = (mine + ry[rows, :].astype(f32)).astype(bf16)
        local(out_ref.at[rows], out_hbm.at[rows], 6).start()

    def scatter_point(k, p):
        if p == 0 and not early[k]:
            twin_sums(k)
        if p < depth - 1:
            chain(k, p)
        else:
            home(k)

    def send_gate_grads():
        turned = ggcol[...].T
        for b in range(devices):
            ggs[b] = turned[b : b + 1]
        ggr[me] = ggs[me]
        for peer in range(devices):
            out.send(
                BACK, peer != me,
                remote(
                    lambda peer=peer: ggs.at[peer], lambda: ggr.at[me], lambda: gg_sem,
                    lambda peer=peer: peer,
                ),
            )

    def take_gate_grads():
        landed(ggr.at[pl.ds(0, devices - 1)], gg_sem)
        held = ggr[...].reshape(devices, tok)
        for k in range(ids_ref.shape[0]):
            hot = ids_ref[k : k + 1] == expert
            picked = jnp.sum(jnp.where(hot, held, 0.0), axis=0, keepdims=True)
            ggo_ref[k : k + 1] = picked.astype(bf16)
        results[1].start()

    def gates_out(k):
        for copy in plan_copies:
            copy.wait()
        send_gates()

        @pl.when(z == 0)
        def _():
            rzu[...] = jnp.zeros_like(rzu)

        @pl.when(z == last)
        def _():
            rzd[...] = jnp.zeros_like(rzd)

    def ready(k):
        finish(k)
        if k == 0:
            take_gates()
            landed(w1, local_sems.at[1])
            weight_copies[2].wait()

    steps = dict(
        own=own, gates=gates_out, relay=relay, cross=cross, finish=ready, fwd=forward,
        wg=weights, trade=trade, sc=scatter_point, total=total, ggout=lambda k: send_gate_grads(),
        ggin=lambda k: take_gate_grads(),
    )
    for name, *rest in order:
        steps[name](*rest)

    def rows_in(flags, want):
        return sum(size for (_, size), flag in zip(chunks, flags) if flag == want)

    def sent_blocks(zz):
        ends = (zz < depth - 1) + (zz > 0)
        passed, widened = depth, 1 + ends
        for off in range(1, depth):
            mid = off < depth - 1
            below, above = zz >= off, zz + off < depth
            passed += below * (2 + (zz < depth - 1 and mid)) + above * (2 + (zz > 0 and mid))
            widened += 2 * below * (1 + (zz < depth - 1 and mid))
            widened += 2 * above * (1 + (zz > 0 and mid))
        out.sent(OWN, buf.at[pl.ds(0, 2 + ends)])
        out.sent(GATE, gbuf.at[pl.ds(0, 2 + ends)])
        out.sent(FLAT, gbuf.at[pl.ds(0, widened if wide[0] else passed)])
        for group, count, want in ((PASS, passed, False), (WIDE, widened, True)):
            if rows_in(wide, want):
                out.sent(group, buf.at[pl.ds(0, count), :, pl.ds(0, rows_in(wide, want))])

    for zz in range(depth):
        pl.when(z == zz)(lambda: sent_blocks(zz))
    out.sent(PAIR, rc)
    late, soon = rows_in(early, False), rows_in(early, True)
    if late:
        out.sent(HOME, ysend.at[pl.ds(0, late)])
    if soon:
        out.sent(TRADE, xsend.at[:, pl.ds(0, soon)])
    if depth > 1 and late:
        out.sent(CHAIN, rzu.at[pl.ds(0, depth - 1), :, pl.ds(0, late)])
    if depth > 1 and soon:
        out.sent(THIN, rzu.at[pl.ds(0, depth - 1), 0, pl.ds(0, soon)])
    out.sent(BACK, ggs.at[pl.ds(0, devices - 1)])
    for copy in results:
        copy.wait()


def fused_grads(x, dy, gates, ids, table, gate_w, up_w, down_w, devices, home_cap, rep_cap):
    depth = devices // 4
    tok, width = x.shape
    hidden = down_w.shape[0]
    f32, bf16 = jnp.float32, jnp.bfloat16
    n = len(row_chunks(tok))
    most = max(size for _, size in row_chunks(tok))
    vmem, dma = pltpu.VMEM, pltpu.SemaphoreType.DMA
    hbm = pl.BlockSpec(memory_space=pltpu.HBM)
    shape = jax.ShapeDtypeStruct
    outs = pl.pallas_call(
        lambda *refs: fused_kernel(depth, step_order(depth, n), home_cap, rep_cap, *refs),
        out_shape=[
            shape((tok, width), bf16), shape(gates.shape, bf16), shape(gate_w.shape, bf16),
            shape(up_w.shape, bf16), shape(down_w.shape, bf16),
        ],
        in_specs=[hbm] * 8,
        out_specs=[hbm] * 5,
        scratch_shapes=[
            vmem((tok, width), bf16), vmem(gates.shape, bf16), vmem(gate_w.shape, bf16),
            vmem(up_w.shape, bf16), vmem(down_w.shape, bf16),
            vmem((devices, 2, tok, width), bf16), vmem((devices, devices, tok), bf16),
            vmem((tok, 128), f32), vmem((tok, 128), f32),
            vmem((devices, 1, tok), f32), vmem((devices, 1, tok), f32),
            vmem((width, 2 * hidden), bf16), vmem((hidden, width), bf16),
            vmem((2, devices, most, 2 * hidden), bf16), vmem((2, devices, most, hidden), bf16),
            vmem((width, 2 * hidden), f32), vmem((hidden, width), f32),
            vmem((depth, 2, 2, tok, width), bf16), vmem((depth, 2, tok, width), bf16),
            vmem((depth, 2, tok, width), bf16), vmem((depth, 2, tok, width), bf16),
            vmem((tok, width), bf16), vmem((tok, width), bf16),
            vmem((depth, tok, width), bf16), vmem((depth, tok, width), bf16),
            vmem(gates.shape, bf16), vmem(ids.shape, ids.dtype),
            pltpu.SMEM(table.shape, table.dtype),
            dma((12,)), dma((11,)), dma((n, devices // 2)), dma((n,)), dma, dma,
            dma((sum(unit_counts(tok, devices)),)), dma((n, depth + 1)),
            dma((max(1, n - sum(PAIR_FIRST)),)), dma((max(1, sum(PAIR_FIRST)), depth)),
            dma((devices // 2,)),
        ],
        compiler_params=pltpu.CompilerParams(
            collective_id=0, has_side_effects=True, vmem_limit_bytes=VMEM_GRANT
        ),
    )(x, dy, gates, ids, table, gate_w, up_w, down_w)
    return store_all(outs)


def store_kernel(n, cuts, *refs):
    src, dst, held, (load_sems, store_sems) = refs[:n], refs[n : 2 * n], refs[2 * n : -2], refs[-2:]
    loads, stores = [], []
    for i in range(n):
        step = src[i].shape[0] // cuts[i]
        for j in range(cuts[i]):
            rows = pl.ds(j * step, step)
            m = len(loads)
            loads.append(
                pltpu.make_async_copy(src[i].at[rows], held[i].at[rows], load_sems.at[m])
            )
            stores.append(
                pltpu.make_async_copy(held[i].at[rows], dst[i].at[rows], store_sems.at[m])
            )
    for copy in loads:
        copy.start()
    for load, store in zip(loads, stores):
        load.wait()
        store.start()
    for copy in stores:
        copy.wait()


def store_all(arrays):
    n = len(arrays)
    cuts = [4 if v.shape[0] >= 256 and v.shape[0] % 64 == 0 else 1 for v in arrays]
    hbm = pl.BlockSpec(memory_space=pltpu.HBM)
    return pl.pallas_call(
        lambda *refs: store_kernel(n, cuts, *refs),
        out_shape=[jax.ShapeDtypeStruct(v.shape, v.dtype) for v in arrays],
        in_specs=[hbm] * n,
        out_specs=[hbm] * n,
        scratch_shapes=[pltpu.VMEM(v.shape, v.dtype) for v in arrays]
        + [pltpu.SemaphoreType.DMA((sum(cuts),))] * 2,
        compiler_params=pltpu.CompilerParams(vmem_limit_bytes=VMEM_GRANT),
    )(*arrays)


def keep_plan(gates, row_ids, replica_table, source, devices, home_cap, rep_cap):
    tok = row_ids.shape[0]
    experts = jnp.arange(devices, dtype=jnp.int32)
    hot = row_ids[:, :, None] == experts[None, None, :]
    named = jnp.any(hot, axis=1)
    dense_gate = jnp.sum(jnp.where(hot, gates.astype(jnp.float32)[:, :, None], 0.0), axis=1)
    copies = 1 + jnp.sum((replica_table[:, None] == experts[None, :]).astype(jnp.int32), axis=0)
    order = jnp.arange(tok, dtype=jnp.int32)
    earlier = (order[:, None] > order[None, :]).astype(jnp.bfloat16)
    rank = jnp.dot(earlier, named.astype(jnp.bfloat16), preferred_element_type=jnp.float32)
    many = copies.astype(jnp.float32)[None, :]
    position = jnp.floor((rank + 0.5) / many)
    turn = rank + source.astype(jnp.float32)
    copy_index = turn - many * jnp.floor((turn + 0.5) / many)
    limit = jnp.where(copy_index < 0.5, float(home_cap), float(rep_cap))
    kept = named & (position < limit)
    return jnp.where(kept, dense_gate, 0.0).astype(jnp.bfloat16)


def row_grads(x, dy, gate, gate_w, up_w, down_w):
    a = jnp.dot(x, gate_w, preferred_element_type=jnp.float32)
    b = jnp.dot(x, up_w, preferred_element_type=jnp.float32)
    u = lax.dot_general(dy, down_w, contract_cols, preferred_element_type=jnp.float32)
    sig = jax.nn.sigmoid(a)
    act = a * sig
    product = act * b
    hidden = product.astype(jnp.bfloat16).astype(jnp.float32)
    gate_grad = jnp.sum(hidden * u, axis=1, keepdims=True)
    gate_grad = jnp.where(gate > 0, gate_grad, 0.0)
    hg = (gate * product).astype(jnp.bfloat16)
    gu = gate * u
    da = (gu * b * sig * (1.0 + a * (1.0 - sig))).astype(jnp.bfloat16)
    db = (gu * act).astype(jnp.bfloat16)
    dx = lax.dot_general(da, gate_w, contract_cols, preferred_element_type=jnp.float32)
    dx = dx + lax.dot_general(db, up_w, contract_cols, preferred_element_type=jnp.float32)
    return gate_grad, hg, da, db, dx


def weight_grads(x, dy, hg, da, db):
    dwg = lax.dot_general(x, da, contract_rows, preferred_element_type=jnp.float32)
    dwu = lax.dot_general(x, db, contract_rows, preferred_element_type=jnp.float32)
    dwd = lax.dot_general(hg, dy, contract_rows, preferred_element_type=jnp.float32)
    return dwg, dwu, dwd


def on_device(tokens_in, grad_out, gates, expert_ids, replica_table, w_gate, w_up, w_down):
    devices = lax.axis_size("expert")
    me = lax.axis_index("expert")
    tok, width = tokens_in.shape
    home_cap = max(2, 5 * tok * TOP // (4 * devices))
    rep_cap = max(2, tok * TOP // (2 * devices))
    if devices * tok <= ROWS_PER_CHUNK and devices % 16 == 0 and devices <= 128 and tok % 128 == 0:
        outs = fused_grads(
            tokens_in, grad_out, gates.T, expert_ids.T, replica_table, w_gate[0], w_up[0], w_down[0],
            devices, home_cap, rep_cap,
        )
        return (outs[0], outs[1].T, *[g[None] for g in outs[2:]])
    kept_gate = keep_plan(gates, expert_ids, replica_table, me, devices, home_cap, rep_cap)
    lanes = -(-devices // 128) * 128
    kept_gate = jnp.pad(kept_gate, ((0, 0), (0, lanes - devices)))
    payload = jnp.concatenate([tokens_in, grad_out, kept_gate], axis=1)
    chunks = max(1, devices * tok // ROWS_PER_CHUNK)
    part = tok // chunks
    mine = jnp.arange(lanes, dtype=jnp.int32)[None, :] == me
    backs, sums = [], None
    for c in range(chunks):
        rows = lax.all_gather(payload[c * part : (c + 1) * part], "expert", axis=0, tiled=True)
        gate = jnp.sum(
            jnp.where(mine, rows[:, 2 * width :].astype(jnp.float32), 0.0),
            axis=1,
            keepdims=True,
        )
        gate_grad, hg, da, db, dx = row_grads(
            rows[:, :width], rows[:, width : 2 * width], gate, w_gate[0], w_up[0], w_down[0]
        )
        spread = jnp.where(mine, gate_grad, 0.0).astype(jnp.bfloat16)
        back = jnp.concatenate([dx.astype(jnp.bfloat16), spread], axis=1)
        backs.append(lax.psum_scatter(back, "expert", scatter_dimension=0, tiled=True))
        grads = weight_grads(rows[:, :width], rows[:, width : 2 * width], hg, da, db)
        sums = grads if sums is None else [p + q for p, q in zip(sums, grads)]
        if c + 1 < chunks:
            payload, sums = lax.optimization_barrier((payload, sums))
    back = jnp.concatenate(backs, axis=0)
    experts = jnp.arange(devices, dtype=jnp.int32)
    hot = expert_ids[:, :, None] == experts[None, None, :]
    picked = jnp.where(hot, back[:, None, width : width + devices].astype(jnp.float32), 0.0)
    grad_gates = jnp.sum(picked, axis=2).astype(jnp.bfloat16)
    return (back[:, :width], grad_gates, *[g.astype(jnp.bfloat16)[None] for g in sums])


def solution(mesh):
    return jax.shard_map(
        on_device,
        mesh=mesh,
        in_specs=(
            P(("groups", "expert"), None),
            P(("groups", "expert"), None),
            P(("groups", "expert"), None),
            P(("groups", "expert"), None),
            P("groups"),
            P("expert", None, None),
            P("expert", None, None),
            P("expert", None, None),
        ),
        out_specs=(
            P(("groups", "expert"), None),
            P(("groups", "expert"), None),
            P(("groups", "expert"), None, None),
            P(("groups", "expert"), None, None),
            P(("groups", "expert"), None, None),
        ),
        check_vma=False,
    )
```

```python
import jax
import jax.numpy as jnp
from jax import lax
from jax.experimental import pallas as pl
from jax.experimental.pallas import tpu as pltpu
from jax.sharding import PartitionSpec as P

TOP = 8
ROWS_PER_CHUNK = 4096

contract_rows = (((0,), (0,)), ((), ()))
contract_cols = (((1,), (1,)), ((), ()))

MESH = pl.DeviceIdType.MESH
VMEM_GRANT = 58 * 2**20


def place(depth):
    me = lax.axis_index("expert")
    z, y, c = me // 4, (me // 2) % 2, me % 2
    return me, z, y, c, depth - 1


def index_of(z, y, c):
    return (z * 2 + y) * 2 + c


def greet(z, y, c, last):
    sem = pltpu.get_barrier_semaphore()

    def hello(peer):
        pl.semaphore_signal(sem, inc=1, device_id={"expert": peer}, device_id_type=MESH)

    hello(index_of(z, y, 1 - c))
    hello(index_of(z, 1 - y, c))
    pl.when(z > 0)(lambda: hello(index_of(z - 1, y, c)))
    pl.when(z < last)(lambda: hello(index_of(z + 1, y, c)))
    pl.semaphore_wait(sem, 2 + (z > 0).astype(jnp.int32) + (z < last).astype(jnp.int32))


class Sender:
    def __init__(self, sems):
        self.sems = sems

    def send(self, group, cond, make):
        if cond is None:
            make(self.sems.at[group]).start()
        else:
            pl.when(cond)(lambda: make(self.sems.at[group]).start())

    def sent(self, group, ref):
        pltpu.make_async_copy(ref, ref, self.sems.at[group]).wait()


def remote(src, dst, recv_sem, peer):
    return lambda send_sem: pltpu.make_async_remote_copy(
        src_ref=src(), dst_ref=dst(), send_sem=send_sem, recv_sem=recv_sem(),
        device_id={"expert": peer()}, device_id_type=MESH,
    )


def landed(ref, sem):
    pltpu.make_async_copy(ref, ref, sem).wait()


TUNED_DEPTH = 4
TUNED_SHARES = (16, 32, 32, 16, 16, 16)
PAIR_FIRST = (False, False, True, True, True, True)
STRAIGHT = (False, False, True, True, True, True)
BOTH_COLUMNS = (False, False, False, True, True, False)
TUNED = [
    ("own", 0), ("gates", 0), ("own", 1), ("relay", 0, -1), ("relay", 0, 1), ("own", 3),
    ("relay", 1, -1), ("relay", 0, -2), ("relay", 0, 2), ("cross", 0, 1), ("relay", 1, 1),
    ("cross", 0, -1), ("relay", 0, 3), ("own", 2), ("relay", 0, -3), ("cross", 0, 0),
    ("relay", 1, -2), ("relay", 1, 2), ("cross", 0, 2), ("cross", 0, -3), ("cross", 1, 0),
    ("cross", 0, -2), ("cross", 0, 3), ("relay", 1, -3), ("relay", 1, 3), ("relay", 2, -1),
    ("relay", 2, 1), ("cross", 1, 1), ("cross", 1, -1), ("finish", 0), ("fwd", 0, 0),
    ("wg", 0, 0), ("relay", 2, -2), ("trade", 0), ("relay", 2, 2), ("cross", 3, 0),
    ("cross", 2, 0), ("relay", 3, -1), ("wg", 0, 1), ("sc", 0, 0), ("cross", 1, -2),
    ("cross", 1, 2), ("cross", 1, -3), ("relay", 2, -3), ("cross", 1, 3), ("relay", 2, 3),
    ("own", 4), ("relay", 3, 1), ("own", 5), ("finish", 1), ("fwd", 1, 0), ("cross", 3, -1),
    ("cross", 3, 1), ("fwd", 1, 1), ("cross", 2, -1), ("cross", 2, 1), ("wg", 1, 1),
    ("relay", 5, -1), ("relay", 5, 1), ("relay", 3, 2), ("relay", 4, -1), ("sc", 0, 1),
    ("cross", 2, 2), ("cross", 2, -2), ("trade", 1), ("cross", 2, -3), ("sc", 1, 0),
    ("cross", 2, 3), ("wg", 1, 0), ("relay", 5, -2), ("cross", 3, -2), ("relay", 5, 2),
    ("cross", 3, 2), ("cross", 4, 0), ("finish", 2), ("fwd", 2, 0), ("relay", 3, -2),
    ("relay", 4, 1), ("fwd", 2, 1), ("relay", 5, 3), ("relay", 3, 3), ("relay", 5, -3),
    ("sc", 0, 2), ("wg", 2, 1), ("cross", 3, 3), ("cross", 3, -3), ("wg", 2, 0), ("cross", 4, 1),
    ("trade", 2), ("cross", 4, -1), ("cross", 5, 2), ("cross", 5, 1), ("relay", 3, -3),
    ("relay", 4, 2), ("relay", 4, -2), ("sc", 1, 1), ("finish", 3), ("cross", 5, -1),
    ("fwd", 3, 0), ("wg", 3, 0), ("cross", 5, 0), ("relay", 4, -3), ("cross", 5, 3),
    ("cross", 4, -2), ("cross", 4, 2), ("sc", 0, 3), ("cross", 5, -2), ("cross", 5, -3),
    ("sc", 2, 0), ("relay", 4, 3), ("cross", 4, 3), ("sc", 1, 2), ("sc", 2, 1), ("cross", 4, -3),
    ("trade", 3), ("finish", 4), ("fwd", 4, 0), ("wg", 3, 1), ("finish", 5), ("fwd", 5, 0),
    ("trade", 4), ("sc", 2, 2), ("sc", 2, 3), ("sc", 3, 0), ("ggout", 0), ("wg", 4, 1),
    ("total", 0), ("trade", 5), ("sc", 1, 3), ("total", 2), ("sc", 4, 0), ("wg", 4, 0),
    ("sc", 5, 0), ("sc", 4, 1), ("wg", 5, 0), ("wg", 5, 1), ("sc", 3, 1), ("sc", 3, 2),
    ("sc", 3, 3), ("total", 1), ("sc", 5, 1), ("sc", 5, 2), ("sc", 4, 2), ("sc", 4, 3),
    ("ggin", 0), ("sc", 5, 3), ("total", 4), ("total", 5), ("total", 3),
]


def row_chunks(tok):
    whole = sum(TUNED_SHARES)
    sizes = [tok * share // whole for share in TUNED_SHARES]
    return [(sum(sizes[:k]), size) for k, size in enumerate(sizes)]


def unit_counts(tok, devices):
    whole = devices % 8 != 0
    return [1 if whole or size * devices <= 256 else 2 for _, size in row_chunks(tok)]


def step_order(depth, n):
    if depth == TUNED_DEPTH:
        return TUNED
    steps = [("own", 0), ("gates", 0)]
    for k in range(n):
        steps += [("own", k)] if k else []
        for d in range(1, depth):
            steps += [("relay", k, -d), ("relay", k, d)]
        steps += [("cross", k, d) for d in range(1 - depth, depth)]
        steps += [("finish", k), ("fwd", k, 0), ("fwd", k, 1), ("wg", k, 0), ("wg", k, 1)]
        steps += [("trade", k)] + [("sc", k, p) for p in range(depth)] + [("total", k)]
    return steps + [("ggout", 0), ("ggin", 0)]


def fused_kernel(
    depth, order, home_cap, rep_cap,
    x_hbm, dy_hbm, gates_hbm, ids_hbm, table_hbm, wg_hbm, wu_hbm, wd_hbm,
    out_hbm, ggo_hbm, dwg_hbm, dwu_hbm, dwd_hbm,
    out_ref, ggo_ref, dwg_ref, dwu_ref, dwd_ref,
    buf, gbuf, gcol, ggcol, ggs, ggr, w1, wd, dadb, hgb, acc1, acc2, dx, rc, rzu, rzd, ysend, ry, xsend, xr, dsend, dr,
    gates_ref, ids_ref, table_ref,
    local_sems, send_sems, recv_sems, pair_sems, gate_sem, gg_sem, twin_sems, chain_sems,
    y_sems, x_sems, gate_sems, spread_sems,
):
    f32, bf16 = jnp.float32, jnp.bfloat16
    devices = 4 * depth
    early, wide, straight = PAIR_FIRST, BOTH_COLUMNS, STRAIGHT
    counts = unit_counts(x_hbm.shape[0], devices)
    me, z, y, c, last = place(depth)
    tok, width = x_hbm.shape
    hidden = wd_hbm.shape[0]
    chunks = row_chunks(tok)
    lanes = gcol.shape[1]

    def local(src, dst, i):
        return pltpu.make_async_copy(src, dst, local_sems.at[i])

    own_copies = [local(x_hbm, buf.at[me, 0], 0), local(dy_hbm, buf.at[me, 1], 0)]
    weight_copies = [
        local(wg_hbm, w1.at[:, pl.ds(0, hidden)], 1),
        local(wu_hbm, w1.at[:, pl.ds(hidden, hidden)], 1),
        local(wd_hbm, wd, 2),
    ]
    plan_copies = [
        local(gates_hbm, gates_ref, 3), local(ids_hbm, ids_ref, 4), local(table_hbm, table_ref, 5),
    ]
    results = [
        local(out_ref, out_hbm, 6), local(ggo_ref, ggo_hbm, 7), local(dwg_ref, dwg_hbm, 8),
        local(dwu_ref, dwu_hbm, 9), local(dwd_ref, dwd_hbm, 10),
    ]
    for copy in own_copies + plan_copies + weight_copies:
        copy.start()
    greet(z, y, c, last)
    landed(buf.at[me], local_sems.at[0])

    out = Sender(send_sems)
    up = lambda: index_of(z + 1, y, c)
    down = lambda: index_of(z - 1, y, c)
    over = lambda: index_of(z, 1 - y, c)
    twin = lambda: index_of(z, y, 1 - c)
    can_up, can_down = z < last, z > 0
    half = depth // 2

    def rows_of(k):
        return pl.ds(*chunks[k])

    OWN, PASS, WIDE, PAIR, CHAIN, THIN, TRADE, HOME, GATE, BACK, FLAT, SPREAD = range(12)

    def push(group, cond, b, k, peer):
        block = lambda: buf.at[b(), :, rows_of(k)]
        sem = (lambda: pair_sems.at[k]) if peer is twin else (lambda: recv_sems.at[k, b() // 2])
        out.send(group, cond, remote(block, block, sem, peer))
        if k == 0 and group != OWN:
            push_gates(FLAT, cond, b, peer)

    def push_gates(group, cond, b, peer):
        sem = (lambda: gate_sem) if peer is twin else (lambda: gate_sems.at[b() // 2])
        out.send(group, cond, remote(lambda: gbuf.at[b()], lambda: gbuf.at[b()], sem, peer))

    def arrived(k, b):
        landed(buf.at[b, :, rows_of(k)], recv_sems.at[k, b // 2])
        if k == 0:
            landed(gbuf.at[b], gate_sems.at[b // 2])

    def own(k):
        mine = lambda: me
        push(OWN, None, mine, k, over)
        push(OWN, can_up, mine, k, up)
        push(OWN, can_down, mine, k, down)
        push(OWN, None, mine, k, twin)

    def relay(k, off):
        cond = z + off >= 0 if off < 0 else z + off <= last
        more, onward = (can_up, up) if off < 0 else (can_down, down)
        b = lambda: index_of(z + off, y, c)
        pl.when(cond)(lambda: arrived(k, b()))
        group = WIDE if wide[k] else PASS
        if abs(off) < depth - 1:
            push(group, cond & more, b, k, onward)
        if not wide[k]:
            push(group, cond, b, k, over)
        push(group, cond, b, k, twin)

    def cross(k, off):
        b = lambda: index_of(z + off, 1 - y, c)
        cond = None if off == 0 else z + off >= 0 if off < 0 else z + off <= last
        group = WIDE if wide[k] else PASS
        if cond is None:
            arrived(k, b())
        else:
            pl.when(cond)(lambda: arrived(k, b()))
        if wide[k] and abs(off) < depth - 1:
            if off <= 0:
                push(group, can_up if cond is None else cond & can_up, b, k, up)
            if off >= 0:
                push(group, can_down if cond is None else cond & can_down, b, k, down)
        push(group, cond, b, k, twin)

    def finish(k):
        landed(buf.at[pl.ds(0, devices // 2), :, rows_of(k)], pair_sems.at[k])

    lane = lax.broadcasted_iota(jnp.int32, (tok, lanes), 1)
    expert = lax.broadcasted_iota(jnp.int32, (devices, tok), 0)

    def send_gates():
        copies = jnp.ones((devices, tok), f32)
        for d in range(devices):
            copies = copies + jnp.where(expert == table_ref[d], 1.0, 0.0)
        dense = jnp.zeros((devices, tok), f32)
        named = jnp.zeros((devices, tok), f32)
        for k in range(ids_ref.shape[0]):
            hot = ids_ref[k : k + 1] == expert
            dense = jnp.where(hot, gates_ref[k : k + 1].astype(f32), dense)
            named = jnp.where(hot, 1.0, named)
        row = lax.broadcasted_iota(jnp.int32, (tok, tok), 0)
        col = lax.broadcasted_iota(jnp.int32, (tok, tok), 1)
        earlier = jnp.where(row < col, 1.0, 0.0).astype(bf16)
        rank = jnp.dot(named.astype(bf16), earlier, preferred_element_type=f32)
        position = jnp.floor((rank + 0.5) / copies)
        turn = rank + me.astype(f32)
        copy_index = turn - copies * jnp.floor((turn + 0.5) / copies)
        limit = jnp.where(copy_index < 0.5, float(home_cap), float(rep_cap))
        gbuf[me] = jnp.where((named > 0.5) & (position < limit), dense, 0.0).astype(bf16)
        for cond, peer in ((None, over), (can_up, up), (can_down, down), (None, twin)):
            push_gates(GATE, cond, lambda: me, peer)

    def take_gates():
        landed(gbuf.at[pl.ds(0, devices // 2)], gate_sem)
        flat = gbuf[...].reshape(devices * devices, tok)
        r = lax.broadcasted_iota(jnp.int32, (devices * devices, lanes), 0)
        l = lax.broadcasted_iota(jnp.int32, (devices * devices, lanes), 1)
        pick = jnp.where(r == l * devices + me, 1.0, 0.0).astype(bf16)
        gcol[...] = lax.dot_general(flat, pick, contract_rows, preferred_element_type=f32)
        ggcol[...] = jnp.zeros_like(ggcol)

    def units(k):
        if counts[k] == 1:
            return [(0, depth)]
        first = jnp.where(z < half, half, 0)
        return [(first, half), (half - first, half)]

    def forward(k, u):
        if u >= len(units(k)):
            return
        r0, size = chunks[k]
        p0, planes = units(k)[u]
        nb = planes * 4
        at = pl.ds(p0 * 4, nb)
        rows = pl.ds(r0, size)
        x = buf[at, 0, rows, :].reshape(nb * size, width)
        dy = buf[at, 1, rows, :].reshape(nb * size, width)
        g = gcol[rows, :]
        spot = lane[:size]
        gate = jnp.concatenate(
            [
                jnp.sum(jnp.where(spot == p0 * 4 + j, g, 0.0), axis=1, keepdims=True)
                for j in range(nb)
            ],
            axis=0,
        )
        ab = jnp.dot(x, w1[...], preferred_element_type=f32)
        a, b = ab[:, :hidden], ab[:, hidden:]
        v = lax.dot_general(dy, wd[...], contract_cols, preferred_element_type=f32)
        sig = jax.nn.sigmoid(a)
        act = a * sig
        product = act * b
        gate_grad = jnp.sum(product.astype(bf16).astype(f32) * v, axis=1, keepdims=True)
        gate_grad = jnp.where(gate > 0, gate_grad, 0.0)
        gu = gate * v
        da = (gu * b * sig * (1.0 + a * (1.0 - sig))).astype(bf16)
        db = (gu * act).astype(bf16)
        both_grads = jnp.concatenate([da, db], axis=1)
        hgb[k % 2, at, pl.ds(0, size), :] = (gate * product).astype(bf16).reshape(nb, size, hidden)
        dadb[k % 2, at, pl.ds(0, size), :] = both_grads.reshape(nb, size, 2 * hidden)
        back = lax.dot_general(both_grads, w1[...], contract_cols, preferred_element_type=f32)
        dx[pl.ds(p0, planes), :, :, rows, :] = back.astype(bf16).reshape(
            planes, 2, 2, size, width
        )
        held = ggcol[rows, :]
        for j in range(nb):
            held = jnp.where(spot == p0 * 4 + j, gate_grad[j * size : (j + 1) * size], held)
        ggcol[rows, :] = held
        src = lambda: dx.at[pl.ds(p0, planes), :, 1 - c, rows, :]
        dst = lambda: rc.at[pl.ds(p0, planes), :, rows, :]
        out.send(PAIR, None, remote(src, dst, lambda: twin_sems.at[sum(counts[:k]) + u], twin))

    def twin_sums(k):
        for u, (p0, planes) in enumerate(units(k)):
            landed(rc.at[pl.ds(p0, planes), :, rows_of(k), :], twin_sems.at[sum(counts[:k]) + u])

    tile = 256 if width % 256 == 0 else 128

    def weight_tile(k, j, which):
        size = chunks[k][1]
        rows = rows_of(k)
        cols = pl.ds(j * tile, tile)
        first, final = k == 0, k == len(chunks) - 1
        if which == 0:
            x = buf[:, 0, rows, cols].reshape(devices * size, tile)
            d = dadb[k % 2, :, pl.ds(0, size), :].reshape(devices * size, 2 * hidden)
            v = lax.dot_general(x, d, contract_rows, preferred_element_type=f32)
            if not first:
                v = v + acc1[cols, :]
            if final:
                dwg_ref[cols, :] = v[:, :hidden].astype(bf16)
                dwu_ref[cols, :] = v[:, hidden:].astype(bf16)
            else:
                acc1[cols, :] = v
        else:
            dy = buf[:, 1, rows, cols].reshape(devices * size, tile)
            h = hgb[k % 2, :, pl.ds(0, size), :].reshape(devices * size, hidden)
            v = lax.dot_general(h, dy, contract_rows, preferred_element_type=f32)
            if not first:
                v = v + acc2[:, cols]
            if final:
                dwd_ref[:, cols] = v.astype(bf16)
            else:
                acc2[:, cols] = v

    def weights(k, which):
        for j in range(width // tile):
            weight_tile(k, j, which)
        if k == len(chunks) - 1:
            for copy in (results[2:4], results[4:])[which]:
                copy.start()

    def part_sum(zz, yy, rows, extra):
        total = dx[zz, yy, c, rows, :].astype(f32) + rc[zz, yy, rows, :].astype(f32)
        for ref in extra:
            total = total + ref[zz, yy, rows, :].astype(f32)
        return total

    def trade(k):
        if not early[k]:
            return
        twin_sums(k)
        rows = rows_of(k)
        for i in range(depth):
            zz = jnp.where(2 * z < depth, last - i, i)
            xsend[zz, rows, :] = part_sum(zz, 1 - y, rows, ()).astype(bf16)
            out.send(
                TRADE, None,
                remote(
                    lambda zz=zz: xsend.at[zz, rows, :], lambda zz=zz: xr.at[zz, rows, :],
                    lambda zz=zz: x_sems.at[sum(early[:k]), zz], over,
                ),
            )

    def traded(k, zz):
        landed(xr.at[zz, rows_of(k), :], x_sems.at[sum(early[:k]), zz])
        return part_sum(zz, y, rows_of(k), ()) + xr[zz, rows_of(k), :].astype(f32)

    def chain(k, p):
        rows = rows_of(k)
        for there, zz, ref, way, has, peer in (
            (z <= p, z + last - p, rzu, 1, z > 0, up),
            (last - z <= p, z + p - last, rzd, 0, z < last, down),
        ):
            piece = ref.at[zz, 0, rows, :] if early[k] else ref.at[zz, :, rows, :]

            def step():
                pl.when(has)(lambda: landed(piece, chain_sems.at[k, zz + way]))
                if early[k]:
                    held = ref[zz, 0, rows, :].astype(f32)
                    ref[zz, 0, rows, :] = (traded(k, zz) + held).astype(bf16)
                else:
                    for yy in range(2):
                        ref[zz, yy, rows, :] = part_sum(zz, yy, rows, (ref,)).astype(bf16)

            pl.when(there)(step)
            out.send(
                THIN if early[k] else CHAIN, there,
                remote(lambda: piece, lambda: piece, lambda: chain_sems.at[k, zz + way], peer),
            )

    def home(k):
        rows = rows_of(k)
        way = 0 if early[k] else slice(None)
        pl.when(z > 0)(lambda: landed(rzu.at[z, way, rows, :], chain_sems.at[k, z + 1]))
        pl.when(z < last)(lambda: landed(rzd.at[z, way, rows, :], chain_sems.at[k, z]))
        if early[k]:
            held = rzu[z, 0, rows, :].astype(f32) + rzd[z, 0, rows, :].astype(f32)
            out_ref[rows, :] = (traded(k, z) + held).astype(bf16)
            local(out_ref.at[rows], out_hbm.at[rows], 6).start()
            return
        ysend[rows, :] = part_sum(z, 1 - y, rows, (rzu, rzd)).astype(bf16)
        out.send(
            HOME, None,
            remote(
                lambda: ysend.at[rows, :], lambda: ry.at[rows, :], lambda: y_sems.at[k - sum(early[:k])], over
            ),
        )

    def total(k):
        if early[k]:
            return
        rows = rows_of(k)
        mine = part_sum(z, y, rows, (rzu, rzd))
        landed(ry.at[rows, :], y_sems.at[k - sum(early[:k])])
        out_ref[rows, :] = (mine + ry[rows, :].astype(f32)).astype(bf16)
        local(out_ref.at[rows], out_hbm.at[rows], 6).start()

    def spread(k):
        rows = rows_of(k)
        turn = sum(straight[:k])
        for i in range(depth):
            zz = jnp.where(2 * z < depth, last - i, i)

            def step():
                dsend[zz, rows, :] = traded(k, zz).astype(bf16)

            pl.when(zz != z)(step)
            out.send(
                SPREAD, zz != z,
                remote(
                    lambda: dsend.at[zz, rows, :], lambda: dr.at[z, rows, :],
                    lambda: spread_sems.at[turn, z], lambda: index_of(zz, y, c),
                ),
            )

    def collect(k):
        rows = rows_of(k)
        held = traded(k, z)
        for i in range(1, depth):
            src = (z + i) % depth
            landed(dr.at[src, rows, :], spread_sems.at[sum(straight[:k]), src])
            held = held + dr[src, rows, :].astype(f32)
        out_ref[rows, :] = held.astype(bf16)
        local(out_ref.at[rows], out_hbm.at[rows], 6).start()

    def scatter_point(k, p):
        if straight[k]:
            if p == 0:
                spread(k)
            elif p == depth - 1:
                collect(k)
            return
        if p == 0 and not early[k]:
            twin_sums(k)
        if p < depth - 1:
            chain(k, p)
        else:
            home(k)

    def send_gate_grads():
        turned = ggcol[...].T
        for b in range(devices):
            ggs[b] = turned[b : b + 1]
        ggr[me] = ggs[me]
        for peer in range(devices):
            out.send(
                BACK, peer != me,
                remote(
                    lambda peer=peer: ggs.at[peer], lambda: ggr.at[me], lambda: gg_sem,
                    lambda peer=peer: peer,
                ),
            )

    def take_gate_grads():
        landed(ggr.at[pl.ds(0, devices - 1)], gg_sem)
        held = ggr[...].reshape(devices, tok)
        for k in range(ids_ref.shape[0]):
            hot = ids_ref[k : k + 1] == expert
            picked = jnp.sum(jnp.where(hot, held, 0.0), axis=0, keepdims=True)
            ggo_ref[k : k + 1] = picked.astype(bf16)
        results[1].start()

    def gates_out(k):
        for copy in plan_copies:
            copy.wait()
        send_gates()

        @pl.when(z == 0)
        def _():
            rzu[...] = jnp.zeros_like(rzu)

        @pl.when(z == last)
        def _():
            rzd[...] = jnp.zeros_like(rzd)

    def ready(k):
        finish(k)
        if k == 0:
            take_gates()
            landed(w1, local_sems.at[1])
            weight_copies[2].wait()

    steps = dict(
        own=own, gates=gates_out, relay=relay, cross=cross, finish=ready, fwd=forward,
        wg=weights, trade=trade, sc=scatter_point, total=total, ggout=lambda k: send_gate_grads(),
        ggin=lambda k: take_gate_grads(),
    )
    for name, *rest in order:
        steps[name](*rest)

    def rows_in(flags, want):
        return sum(size for (_, size), flag in zip(chunks, flags) if flag == want)

    def sent_blocks(zz):
        ends = (zz < depth - 1) + (zz > 0)
        passed, widened = depth, 1 + ends
        for off in range(1, depth):
            mid = off < depth - 1
            below, above = zz >= off, zz + off < depth
            passed += below * (2 + (zz < depth - 1 and mid)) + above * (2 + (zz > 0 and mid))
            widened += 2 * below * (1 + (zz < depth - 1 and mid))
            widened += 2 * above * (1 + (zz > 0 and mid))
        out.sent(OWN, buf.at[pl.ds(0, 2 + ends)])
        out.sent(GATE, gbuf.at[pl.ds(0, 2 + ends)])
        out.sent(FLAT, gbuf.at[pl.ds(0, widened if wide[0] else passed)])
        for group, count, want in ((PASS, passed, False), (WIDE, widened, True)):
            if rows_in(wide, want):
                out.sent(group, buf.at[pl.ds(0, count), :, pl.ds(0, rows_in(wide, want))])

    for zz in range(depth):
        pl.when(z == zz)(lambda: sent_blocks(zz))
    out.sent(PAIR, rc)
    late, soon = rows_in(early, False), rows_in(early, True)
    direct = rows_in(straight, True)
    if late:
        out.sent(HOME, ysend.at[pl.ds(0, late)])
    if soon:
        out.sent(TRADE, xsend.at[:, pl.ds(0, soon)])
    if depth > 1 and late:
        out.sent(CHAIN, rzu.at[pl.ds(0, depth - 1), :, pl.ds(0, late)])
    if depth > 1 and soon > direct:
        out.sent(THIN, rzu.at[pl.ds(0, depth - 1), 0, pl.ds(0, soon - direct)])
    if depth > 1 and direct:
        out.sent(SPREAD, dr.at[pl.ds(0, depth - 1), pl.ds(0, direct)])
    out.sent(BACK, ggs.at[pl.ds(0, devices - 1)])
    for copy in results:
        copy.wait()


def fused_grads(x, dy, gates, ids, table, gate_w, up_w, down_w, devices, home_cap, rep_cap):
    depth = devices // 4
    tok, width = x.shape
    hidden = down_w.shape[0]
    f32, bf16 = jnp.float32, jnp.bfloat16
    n = len(row_chunks(tok))
    most = max(size for _, size in row_chunks(tok))
    vmem, dma = pltpu.VMEM, pltpu.SemaphoreType.DMA
    hbm = pl.BlockSpec(memory_space=pltpu.HBM)
    shape = jax.ShapeDtypeStruct
    outs = pl.pallas_call(
        lambda *refs: fused_kernel(depth, step_order(depth, n), home_cap, rep_cap, *refs),
        out_shape=[
            shape((tok, width), bf16), shape(gates.shape, bf16), shape(gate_w.shape, bf16),
            shape(up_w.shape, bf16), shape(down_w.shape, bf16),
        ],
        in_specs=[hbm] * 8,
        out_specs=[hbm] * 5,
        scratch_shapes=[
            vmem((tok, width), bf16), vmem(gates.shape, bf16), vmem(gate_w.shape, bf16),
            vmem(up_w.shape, bf16), vmem(down_w.shape, bf16),
            vmem((devices, 2, tok, width), bf16), vmem((devices, devices, tok), bf16),
            vmem((tok, 128), f32), vmem((tok, 128), f32),
            vmem((devices, 1, tok), f32), vmem((devices, 1, tok), f32),
            vmem((width, 2 * hidden), bf16), vmem((hidden, width), bf16),
            vmem((2, devices, most, 2 * hidden), bf16), vmem((2, devices, most, hidden), bf16),
            vmem((width, 2 * hidden), f32), vmem((hidden, width), f32),
            vmem((depth, 2, 2, tok, width), bf16), vmem((depth, 2, tok, width), bf16),
            vmem((depth, 2, tok, width), bf16), vmem((depth, 2, tok, width), bf16),
            vmem((tok, width), bf16), vmem((tok, width), bf16),
            vmem((depth, tok, width), bf16), vmem((depth, tok, width), bf16),
            vmem((depth, tok, width), bf16), vmem((depth, tok, width), bf16),
            vmem(gates.shape, bf16), vmem(ids.shape, ids.dtype),
            pltpu.SMEM(table.shape, table.dtype),
            dma((12,)), dma((12,)), dma((n, devices // 2)), dma((n,)), dma, dma,
            dma((sum(unit_counts(tok, devices)),)), dma((n, depth + 1)),
            dma((max(1, n - sum(PAIR_FIRST)),)), dma((max(1, sum(PAIR_FIRST)), depth)),
            dma((devices // 2,)), dma((max(1, sum(STRAIGHT)), depth)),
        ],
        compiler_params=pltpu.CompilerParams(
            collective_id=0, has_side_effects=True, vmem_limit_bytes=VMEM_GRANT
        ),
    )(x, dy, gates, ids, table, gate_w, up_w, down_w)
    return store_all(outs)


def store_kernel(n, cuts, *refs):
    src, dst, held, (load_sems, store_sems) = refs[:n], refs[n : 2 * n], refs[2 * n : -2], refs[-2:]
    loads, stores = [], []
    for i in range(n):
        step = src[i].shape[0] // cuts[i]
        for j in range(cuts[i]):
            rows = pl.ds(j * step, step)
            m = len(loads)
            loads.append(
                pltpu.make_async_copy(src[i].at[rows], held[i].at[rows], load_sems.at[m])
            )
            stores.append(
                pltpu.make_async_copy(held[i].at[rows], dst[i].at[rows], store_sems.at[m])
            )
    for copy in loads:
        copy.start()
    for load, store in zip(loads, stores):
        load.wait()
        store.start()
    for copy in stores:
        copy.wait()


def store_all(arrays):
    n = len(arrays)
    cuts = [4 if v.shape[0] >= 256 and v.shape[0] % 64 == 0 else 1 for v in arrays]
    hbm = pl.BlockSpec(memory_space=pltpu.HBM)
    return pl.pallas_call(
        lambda *refs: store_kernel(n, cuts, *refs),
        out_shape=[jax.ShapeDtypeStruct(v.shape, v.dtype) for v in arrays],
        in_specs=[hbm] * n,
        out_specs=[hbm] * n,
        scratch_shapes=[pltpu.VMEM(v.shape, v.dtype) for v in arrays]
        + [pltpu.SemaphoreType.DMA((sum(cuts),))] * 2,
        compiler_params=pltpu.CompilerParams(vmem_limit_bytes=VMEM_GRANT),
    )(*arrays)


def keep_plan(gates, row_ids, replica_table, source, devices, home_cap, rep_cap):
    tok = row_ids.shape[0]
    experts = jnp.arange(devices, dtype=jnp.int32)
    hot = row_ids[:, :, None] == experts[None, None, :]
    named = jnp.any(hot, axis=1)
    dense_gate = jnp.sum(jnp.where(hot, gates.astype(jnp.float32)[:, :, None], 0.0), axis=1)
    copies = 1 + jnp.sum((replica_table[:, None] == experts[None, :]).astype(jnp.int32), axis=0)
    order = jnp.arange(tok, dtype=jnp.int32)
    earlier = (order[:, None] > order[None, :]).astype(jnp.bfloat16)
    rank = jnp.dot(earlier, named.astype(jnp.bfloat16), preferred_element_type=jnp.float32)
    many = copies.astype(jnp.float32)[None, :]
    position = jnp.floor((rank + 0.5) / many)
    turn = rank + source.astype(jnp.float32)
    copy_index = turn - many * jnp.floor((turn + 0.5) / many)
    limit = jnp.where(copy_index < 0.5, float(home_cap), float(rep_cap))
    kept = named & (position < limit)
    return jnp.where(kept, dense_gate, 0.0).astype(jnp.bfloat16)


def row_grads(x, dy, gate, gate_w, up_w, down_w):
    a = jnp.dot(x, gate_w, preferred_element_type=jnp.float32)
    b = jnp.dot(x, up_w, preferred_element_type=jnp.float32)
    u = lax.dot_general(dy, down_w, contract_cols, preferred_element_type=jnp.float32)
    sig = jax.nn.sigmoid(a)
    act = a * sig
    product = act * b
    hidden = product.astype(jnp.bfloat16).astype(jnp.float32)
    gate_grad = jnp.sum(hidden * u, axis=1, keepdims=True)
    gate_grad = jnp.where(gate > 0, gate_grad, 0.0)
    hg = (gate * product).astype(jnp.bfloat16)
    gu = gate * u
    da = (gu * b * sig * (1.0 + a * (1.0 - sig))).astype(jnp.bfloat16)
    db = (gu * act).astype(jnp.bfloat16)
    dx = lax.dot_general(da, gate_w, contract_cols, preferred_element_type=jnp.float32)
    dx = dx + lax.dot_general(db, up_w, contract_cols, preferred_element_type=jnp.float32)
    return gate_grad, hg, da, db, dx


def weight_grads(x, dy, hg, da, db):
    dwg = lax.dot_general(x, da, contract_rows, preferred_element_type=jnp.float32)
    dwu = lax.dot_general(x, db, contract_rows, preferred_element_type=jnp.float32)
    dwd = lax.dot_general(hg, dy, contract_rows, preferred_element_type=jnp.float32)
    return dwg, dwu, dwd


def on_device(tokens_in, grad_out, gates, expert_ids, replica_table, w_gate, w_up, w_down):
    devices = lax.axis_size("expert")
    me = lax.axis_index("expert")
    tok, width = tokens_in.shape
    home_cap = max(2, 5 * tok * TOP // (4 * devices))
    rep_cap = max(2, tok * TOP // (2 * devices))
    if devices * tok <= ROWS_PER_CHUNK and devices % 16 == 0 and devices <= 128 and tok % 128 == 0:
        outs = fused_grads(
            tokens_in, grad_out, gates.T, expert_ids.T, replica_table, w_gate[0], w_up[0], w_down[0],
            devices, home_cap, rep_cap,
        )
        return (outs[0], outs[1].T, *[g[None] for g in outs[2:]])
    kept_gate = keep_plan(gates, expert_ids, replica_table, me, devices, home_cap, rep_cap)
    lanes = -(-devices // 128) * 128
    kept_gate = jnp.pad(kept_gate, ((0, 0), (0, lanes - devices)))
    payload = jnp.concatenate([tokens_in, grad_out, kept_gate], axis=1)
    chunks = max(1, devices * tok // ROWS_PER_CHUNK)
    part = tok // chunks
    mine = jnp.arange(lanes, dtype=jnp.int32)[None, :] == me
    backs, sums = [], None
    for c in range(chunks):
        rows = lax.all_gather(payload[c * part : (c + 1) * part], "expert", axis=0, tiled=True)
        gate = jnp.sum(
            jnp.where(mine, rows[:, 2 * width :].astype(jnp.float32), 0.0),
            axis=1,
            keepdims=True,
        )
        gate_grad, hg, da, db, dx = row_grads(
            rows[:, :width], rows[:, width : 2 * width], gate, w_gate[0], w_up[0], w_down[0]
        )
        spread = jnp.where(mine, gate_grad, 0.0).astype(jnp.bfloat16)
        back = jnp.concatenate([dx.astype(jnp.bfloat16), spread], axis=1)
        backs.append(lax.psum_scatter(back, "expert", scatter_dimension=0, tiled=True))
        grads = weight_grads(rows[:, :width], rows[:, width : 2 * width], hg, da, db)
        sums = grads if sums is None else [p + q for p, q in zip(sums, grads)]
        if c + 1 < chunks:
            payload, sums = lax.optimization_barrier((payload, sums))
    back = jnp.concatenate(backs, axis=0)
    experts = jnp.arange(devices, dtype=jnp.int32)
    hot = expert_ids[:, :, None] == experts[None, None, :]
    picked = jnp.where(hot, back[:, None, width : width + devices].astype(jnp.float32), 0.0)
    grad_gates = jnp.sum(picked, axis=2).astype(jnp.bfloat16)
    return (back[:, :width], grad_gates, *[g.astype(jnp.bfloat16)[None] for g in sums])


def solution(mesh):
    return jax.shard_map(
        on_device,
        mesh=mesh,
        in_specs=(
            P(("groups", "expert"), None),
            P(("groups", "expert"), None),
            P(("groups", "expert"), None),
            P(("groups", "expert"), None),
            P("groups"),
            P("expert", None, None),
            P("expert", None, None),
            P("expert", None, None),
        ),
        out_specs=(
            P(("groups", "expert"), None),
            P(("groups", "expert"), None),
            P(("groups", "expert"), None, None),
            P(("groups", "expert"), None, None),
            P(("groups", "expert"), None, None),
        ),
        check_vma=False,
    )
```

```python
import jax
import jax.numpy as jnp
from jax import lax
from jax.experimental import pallas as pl
from jax.experimental.pallas import tpu as pltpu
from jax.sharding import PartitionSpec as P

TOP = 8
ROWS_PER_CHUNK = 4096

contract_rows = (((0,), (0,)), ((), ()))
contract_cols = (((1,), (1,)), ((), ()))

MESH = pl.DeviceIdType.MESH
VMEM_GRANT = 58 * 2**20


def place(depth):
    me = lax.axis_index("expert")
    z, y, c = me // 4, (me // 2) % 2, me % 2
    return me, z, y, c, depth - 1


def index_of(z, y, c):
    return (z * 2 + y) * 2 + c


def greet(z, y, c, last):
    sem = pltpu.get_barrier_semaphore()

    def hello(peer):
        pl.semaphore_signal(sem, inc=1, device_id={"expert": peer}, device_id_type=MESH)

    hello(index_of(z, y, 1 - c))
    hello(index_of(z, 1 - y, c))
    pl.when(z > 0)(lambda: hello(index_of(z - 1, y, c)))
    pl.when(z < last)(lambda: hello(index_of(z + 1, y, c)))
    pl.semaphore_wait(sem, 2 + (z > 0).astype(jnp.int32) + (z < last).astype(jnp.int32))


class Sender:
    def __init__(self, sems):
        self.sems = sems

    def send(self, group, cond, make):
        if cond is None:
            make(self.sems.at[group]).start()
        else:
            pl.when(cond)(lambda: make(self.sems.at[group]).start())

    def sent(self, group, ref):
        pltpu.make_async_copy(ref, ref, self.sems.at[group]).wait()


def remote(src, dst, recv_sem, peer):
    return lambda send_sem: pltpu.make_async_remote_copy(
        src_ref=src(), dst_ref=dst(), send_sem=send_sem, recv_sem=recv_sem(),
        device_id={"expert": peer()}, device_id_type=MESH,
    )


def landed(ref, sem):
    pltpu.make_async_copy(ref, ref, sem).wait()


TUNED_DEPTH = 4
TUNED_SHARES = (32, 16, 16, 16, 16, 16, 16)
PAIR_FIRST = (False, True, True, True, True, True, True)
STRAIGHT = (False, True, True, True, True, True, True)
BOTH_COLUMNS = (False, True, False, False, False, False, True)
TUNED = [
    ("own", 0), ("gates", 0), ("own", 3), ("own", 1), ("relay", 0, 1), ("relay", 0, -1),
    ("own", 2), ("cross", 1, 0), ("cross", 0, 1), ("relay", 0, -2), ("relay", 0, 2),
    ("cross", 0, -1), ("relay", 2, 1), ("relay", 2, -1), ("cross", 1, -1), ("relay", 3, 1),
    ("relay", 0, 3), ("relay", 0, -3), ("relay", 1, -1), ("relay", 3, -1), ("cross", 1, 1),
    ("cross", 0, 0), ("relay", 1, 1), ("cross", 0, -2), ("own", 4), ("cross", 0, 2),
    ("cross", 1, 2), ("cross", 0, 3), ("cross", 2, 1), ("relay", 3, 2), ("cross", 0, -3),
    ("relay", 2, -2), ("cross", 2, -1), ("cross", 1, -2), ("relay", 1, -2), ("relay", 1, 2),
    ("relay", 3, -2), ("cross", 3, 0), ("relay", 2, 2), ("own", 5), ("finish", 0), ("fwd", 0, 0),
    ("fwd", 0, 1), ("relay", 4, 1), ("relay", 2, -3), ("cross", 1, 3), ("own", 6),
    ("cross", 2, -2), ("trade", 0), ("wg", 0, 0), ("relay", 1, 3), ("relay", 1, -3), ("sc", 0, 0),
    ("cross", 2, 2), ("cross", 3, -2), ("cross", 1, -3), ("cross", 4, 0), ("relay", 3, -3),
    ("relay", 3, 3), ("relay", 4, -1), ("relay", 2, 3), ("cross", 2, -3), ("cross", 2, 0),
    ("finish", 1), ("fwd", 1, 0), ("cross", 3, 2), ("relay", 5, -1), ("relay", 5, 1),
    ("cross", 5, 0), ("relay", 4, 2), ("wg", 0, 1), ("cross", 3, -1), ("wg", 1, 1),
    ("cross", 6, 0), ("cross", 2, 3), ("cross", 3, 1), ("relay", 4, -2), ("wg", 1, 0),
    ("relay", 6, -1), ("trade", 1), ("cross", 3, -3), ("sc", 0, 1), ("cross", 3, 3),
    ("finish", 2), ("fwd", 2, 0), ("cross", 5, -1), ("relay", 4, 3), ("relay", 5, 2),
    ("wg", 2, 0), ("relay", 6, 1), ("cross", 4, 1), ("relay", 4, -3), ("cross", 6, 1),
    ("relay", 5, -2), ("finish", 3), ("fwd", 3, 0), ("relay", 5, 3), ("cross", 6, -1),
    ("wg", 2, 1), ("wg", 3, 1), ("cross", 4, 2), ("relay", 5, -3), ("trade", 2), ("cross", 4, -3),
    ("relay", 6, 2), ("cross", 4, -1), ("cross", 4, 3), ("relay", 6, -2), ("cross", 4, -2),
    ("sc", 1, 0), ("cross", 5, 1), ("trade", 3), ("wg", 3, 0), ("sc", 1, 1), ("cross", 5, -2),
    ("cross", 6, 2), ("cross", 6, -2), ("cross", 5, 2), ("sc", 0, 2), ("relay", 6, -3),
    ("finish", 4), ("cross", 5, 3), ("cross", 5, -3), ("fwd", 4, 0), ("finish", 5), ("fwd", 5, 0),
    ("cross", 6, -3), ("wg", 4, 1), ("relay", 6, 3), ("sc", 1, 2), ("sc", 1, 3), ("sc", 2, 0),
    ("trade", 4), ("cross", 6, 3), ("sc", 2, 1), ("wg", 4, 0), ("sc", 3, 0), ("trade", 5),
    ("sc", 3, 1), ("sc", 2, 2), ("finish", 6), ("fwd", 6, 0), ("ggout", 0), ("sc", 4, 0),
    ("wg", 5, 0), ("trade", 6), ("sc", 5, 0), ("sc", 0, 3), ("sc", 4, 1), ("sc", 6, 0),
    ("wg", 6, 0), ("sc", 5, 1), ("wg", 5, 1), ("ggin", 0), ("total", 1), ("sc", 3, 2),
    ("sc", 3, 3), ("sc", 4, 2), ("sc", 5, 2), ("total", 3), ("sc", 2, 3), ("total", 0),
    ("sc", 6, 1), ("sc", 4, 3), ("sc", 6, 2), ("sc", 5, 3), ("wg", 6, 1), ("sc", 6, 3),
    ("total", 5), ("total", 6), ("total", 2), ("total", 4),
]


def row_chunks(tok):
    whole = sum(TUNED_SHARES)
    sizes = [tok * share // whole for share in TUNED_SHARES]
    return [(sum(sizes[:k]), size) for k, size in enumerate(sizes)]


def unit_counts(tok, devices):
    whole = devices % 8 != 0
    return [1 if whole or size * devices <= 256 else 2 for _, size in row_chunks(tok)]


def step_order(depth, n):
    if depth == TUNED_DEPTH:
        return TUNED
    steps = [("own", 0), ("gates", 0)]
    for k in range(n):
        steps += [("own", k)] if k else []
        for d in range(1, depth):
            steps += [("relay", k, -d), ("relay", k, d)]
        steps += [("cross", k, d) for d in range(1 - depth, depth)]
        steps += [("finish", k), ("fwd", k, 0), ("fwd", k, 1), ("wg", k, 0), ("wg", k, 1)]
        steps += [("trade", k)] + [("sc", k, p) for p in range(depth)] + [("total", k)]
    return steps + [("ggout", 0), ("ggin", 0)]


def fused_kernel(
    depth, order, home_cap, rep_cap,
    x_hbm, dy_hbm, gates_hbm, ids_hbm, table_hbm, wg_hbm, wu_hbm, wd_hbm,
    out_hbm, ggo_hbm, dwg_hbm, dwu_hbm, dwd_hbm,
    out_ref, ggo_ref, dwg_ref, dwu_ref, dwd_ref,
    buf, gbuf, gcol, ggcol, ggs, ggr, w1, wd, dadb, hgb, acc1, acc2, dx, rc, rzu, rzd, ysend, ry, xsend, xr, dsend, dr,
    gates_ref, ids_ref, table_ref,
    local_sems, send_sems, recv_sems, pair_sems, gate_sem, gg_sem, twin_sems, chain_sems,
    y_sems, x_sems, gate_sems, spread_sems,
):
    f32, bf16 = jnp.float32, jnp.bfloat16
    devices = 4 * depth
    early, wide, straight = PAIR_FIRST, BOTH_COLUMNS, STRAIGHT
    counts = unit_counts(x_hbm.shape[0], devices)
    me, z, y, c, last = place(depth)
    tok, width = x_hbm.shape
    hidden = wd_hbm.shape[0]
    chunks = row_chunks(tok)
    lanes = gcol.shape[1]

    def local(src, dst, i):
        return pltpu.make_async_copy(src, dst, local_sems.at[i])

    own_copies = [local(x_hbm, buf.at[me, 0], 0), local(dy_hbm, buf.at[me, 1], 0)]
    weight_copies = [
        local(wg_hbm, w1.at[:, pl.ds(0, hidden)], 1),
        local(wu_hbm, w1.at[:, pl.ds(hidden, hidden)], 1),
        local(wd_hbm, wd, 2),
    ]
    plan_copies = [
        local(gates_hbm, gates_ref, 3), local(ids_hbm, ids_ref, 4), local(table_hbm, table_ref, 5),
    ]
    results = [
        local(out_ref, out_hbm, 6), local(ggo_ref, ggo_hbm, 7), local(dwg_ref, dwg_hbm, 8),
        local(dwu_ref, dwu_hbm, 9), local(dwd_ref, dwd_hbm, 10),
    ]
    for copy in own_copies + plan_copies + weight_copies:
        copy.start()
    greet(z, y, c, last)
    landed(buf.at[me], local_sems.at[0])

    out = Sender(send_sems)
    up = lambda: index_of(z + 1, y, c)
    down = lambda: index_of(z - 1, y, c)
    over = lambda: index_of(z, 1 - y, c)
    twin = lambda: index_of(z, y, 1 - c)
    can_up, can_down = z < last, z > 0
    half = depth // 2

    def rows_of(k):
        return pl.ds(*chunks[k])

    OWN, PASS, WIDE, PAIR, CHAIN, THIN, TRADE, HOME, GATE, BACK, FLAT, SPREAD = range(12)

    def push(group, cond, b, k, peer):
        block = lambda: buf.at[b(), :, rows_of(k)]
        sem = (lambda: pair_sems.at[k]) if peer is twin else (lambda: recv_sems.at[k, b() // 2])
        out.send(group, cond, remote(block, block, sem, peer))
        if k == 0 and group != OWN:
            push_gates(FLAT, cond, b, peer)

    def push_gates(group, cond, b, peer):
        sem = (lambda: gate_sem) if peer is twin else (lambda: gate_sems.at[b() // 2])
        out.send(group, cond, remote(lambda: gbuf.at[b()], lambda: gbuf.at[b()], sem, peer))

    def arrived(k, b):
        landed(buf.at[b, :, rows_of(k)], recv_sems.at[k, b // 2])
        if k == 0:
            landed(gbuf.at[b], gate_sems.at[b // 2])

    def own(k):
        mine = lambda: me
        push(OWN, None, mine, k, over)
        push(OWN, can_up, mine, k, up)
        push(OWN, can_down, mine, k, down)
        push(OWN, None, mine, k, twin)

    def relay(k, off):
        cond = z + off >= 0 if off < 0 else z + off <= last
        more, onward = (can_up, up) if off < 0 else (can_down, down)
        b = lambda: index_of(z + off, y, c)
        pl.when(cond)(lambda: arrived(k, b()))
        group = WIDE if wide[k] else PASS
        if abs(off) < depth - 1:
            push(group, cond & more, b, k, onward)
        if not wide[k]:
            push(group, cond, b, k, over)
        push(group, cond, b, k, twin)

    def cross(k, off):
        b = lambda: index_of(z + off, 1 - y, c)
        cond = None if off == 0 else z + off >= 0 if off < 0 else z + off <= last
        group = WIDE if wide[k] else PASS
        if cond is None:
            arrived(k, b())
        else:
            pl.when(cond)(lambda: arrived(k, b()))
        if wide[k] and abs(off) < depth - 1:
            if off <= 0:
                push(group, can_up if cond is None else cond & can_up, b, k, up)
            if off >= 0:
                push(group, can_down if cond is None else cond & can_down, b, k, down)
        push(group, cond, b, k, twin)

    def finish(k):
        landed(buf.at[pl.ds(0, devices // 2), :, rows_of(k)], pair_sems.at[k])

    lane = lax.broadcasted_iota(jnp.int32, (tok, lanes), 1)
    expert = lax.broadcasted_iota(jnp.int32, (devices, tok), 0)

    def send_gates():
        copies = jnp.ones((devices, tok), f32)
        for d in range(devices):
            copies = copies + jnp.where(expert == table_ref[d], 1.0, 0.0)
        dense = jnp.zeros((devices, tok), f32)
        named = jnp.zeros((devices, tok), f32)
        for k in range(ids_ref.shape[0]):
            hot = ids_ref[k : k + 1] == expert
            dense = jnp.where(hot, gates_ref[k : k + 1].astype(f32), dense)
            named = jnp.where(hot, 1.0, named)
        row = lax.broadcasted_iota(jnp.int32, (tok, tok), 0)
        col = lax.broadcasted_iota(jnp.int32, (tok, tok), 1)
        earlier = jnp.where(row < col, 1.0, 0.0).astype(bf16)
        rank = jnp.dot(named.astype(bf16), earlier, preferred_element_type=f32)
        position = jnp.floor((rank + 0.5) / copies)
        turn = rank + me.astype(f32)
        copy_index = turn - copies * jnp.floor((turn + 0.5) / copies)
        limit = jnp.where(copy_index < 0.5, float(home_cap), float(rep_cap))
        gbuf[me] = jnp.where((named > 0.5) & (position < limit), dense, 0.0).astype(bf16)
        for cond, peer in ((None, over), (can_up, up), (can_down, down), (None, twin)):
            push_gates(GATE, cond, lambda: me, peer)

    def take_gates():
        landed(gbuf.at[pl.ds(0, devices // 2)], gate_sem)
        flat = gbuf[...].reshape(devices * devices, tok)
        r = lax.broadcasted_iota(jnp.int32, (devices * devices, lanes), 0)
        l = lax.broadcasted_iota(jnp.int32, (devices * devices, lanes), 1)
        pick = jnp.where(r == l * devices + me, 1.0, 0.0).astype(bf16)
        gcol[...] = lax.dot_general(flat, pick, contract_rows, preferred_element_type=f32)
        ggcol[...] = jnp.zeros_like(ggcol)

    def units(k):
        if counts[k] == 1:
            return [(0, depth)]
        first = jnp.where(z < half, half, 0)
        return [(first, half), (half - first, half)]

    def forward(k, u):
        if u >= len(units(k)):
            return
        r0, size = chunks[k]
        p0, planes = units(k)[u]
        nb = planes * 4
        at = pl.ds(p0 * 4, nb)
        rows = pl.ds(r0, size)
        x = buf[at, 0, rows, :].reshape(nb * size, width)
        dy = buf[at, 1, rows, :].reshape(nb * size, width)
        g = gcol[rows, :]
        spot = lane[:size]
        gate = jnp.concatenate(
            [
                jnp.sum(jnp.where(spot == p0 * 4 + j, g, 0.0), axis=1, keepdims=True)
                for j in range(nb)
            ],
            axis=0,
        )
        ab = jnp.dot(x, w1[...], preferred_element_type=f32)
        a, b = ab[:, :hidden], ab[:, hidden:]
        v = lax.dot_general(dy, wd[...], contract_cols, preferred_element_type=f32)
        sig = jax.nn.sigmoid(a)
        act = a * sig
        product = act * b
        gate_grad = jnp.sum(product.astype(bf16).astype(f32) * v, axis=1, keepdims=True)
        gate_grad = jnp.where(gate > 0, gate_grad, 0.0)
        gu = gate * v
        da = (gu * b * sig * (1.0 + a * (1.0 - sig))).astype(bf16)
        db = (gu * act).astype(bf16)
        both_grads = jnp.concatenate([da, db], axis=1)
        hgb[k % 2, at, pl.ds(0, size), :] = (gate * product).astype(bf16).reshape(nb, size, hidden)
        dadb[k % 2, at, pl.ds(0, size), :] = both_grads.reshape(nb, size, 2 * hidden)
        back = lax.dot_general(both_grads, w1[...], contract_cols, preferred_element_type=f32)
        dx[pl.ds(p0, planes), :, :, rows, :] = back.astype(bf16).reshape(
            planes, 2, 2, size, width
        )
        held = ggcol[rows, :]
        for j in range(nb):
            held = jnp.where(spot == p0 * 4 + j, gate_grad[j * size : (j + 1) * size], held)
        ggcol[rows, :] = held
        src = lambda: dx.at[pl.ds(p0, planes), :, 1 - c, rows, :]
        dst = lambda: rc.at[pl.ds(p0, planes), :, rows, :]
        out.send(PAIR, None, remote(src, dst, lambda: twin_sems.at[sum(counts[:k]) + u], twin))

    def twin_sums(k):
        for u, (p0, planes) in enumerate(units(k)):
            landed(rc.at[pl.ds(p0, planes), :, rows_of(k), :], twin_sems.at[sum(counts[:k]) + u])

    tile = 256 if width % 256 == 0 else 128

    def weight_tile(k, j, which):
        size = chunks[k][1]
        rows = rows_of(k)
        cols = pl.ds(j * tile, tile)
        first, final = k == 0, k == len(chunks) - 1
        if which == 0:
            x = buf[:, 0, rows, cols].reshape(devices * size, tile)
            d = dadb[k % 2, :, pl.ds(0, size), :].reshape(devices * size, 2 * hidden)
            v = lax.dot_general(x, d, contract_rows, preferred_element_type=f32)
            if not first:
                v = v + acc1[cols, :]
            if final:
                dwg_ref[cols, :] = v[:, :hidden].astype(bf16)
                dwu_ref[cols, :] = v[:, hidden:].astype(bf16)
            else:
                acc1[cols, :] = v
        else:
            dy = buf[:, 1, rows, cols].reshape(devices * size, tile)
            h = hgb[k % 2, :, pl.ds(0, size), :].reshape(devices * size, hidden)
            v = lax.dot_general(h, dy, contract_rows, preferred_element_type=f32)
            if not first:
                v = v + acc2[:, cols]
            if final:
                dwd_ref[:, cols] = v.astype(bf16)
            else:
                acc2[:, cols] = v

    def weights(k, which):
        for j in range(width // tile):
            weight_tile(k, j, which)
        if k == len(chunks) - 1:
            for copy in (results[2:4], results[4:])[which]:
                copy.start()

    def part_sum(zz, yy, rows, extra):
        total = dx[zz, yy, c, rows, :].astype(f32) + rc[zz, yy, rows, :].astype(f32)
        for ref in extra:
            total = total + ref[zz, yy, rows, :].astype(f32)
        return total

    def trade(k):
        if not early[k]:
            return
        twin_sums(k)
        rows = rows_of(k)
        for i in range(depth):
            zz = jnp.where(2 * z < depth, last - i, i)
            xsend[zz, rows, :] = part_sum(zz, 1 - y, rows, ()).astype(bf16)
            out.send(
                TRADE, None,
                remote(
                    lambda zz=zz: xsend.at[zz, rows, :], lambda zz=zz: xr.at[zz, rows, :],
                    lambda zz=zz: x_sems.at[sum(early[:k]), zz], over,
                ),
            )

    def traded(k, zz):
        landed(xr.at[zz, rows_of(k), :], x_sems.at[sum(early[:k]), zz])
        return part_sum(zz, y, rows_of(k), ()) + xr[zz, rows_of(k), :].astype(f32)

    def chain(k, p):
        rows = rows_of(k)
        for there, zz, ref, way, has, peer in (
            (z <= p, z + last - p, rzu, 1, z > 0, up),
            (last - z <= p, z + p - last, rzd, 0, z < last, down),
        ):
            piece = ref.at[zz, 0, rows, :] if early[k] else ref.at[zz, :, rows, :]

            def step():
                pl.when(has)(lambda: landed(piece, chain_sems.at[k - sum(straight[:k]), zz + way]))
                if early[k]:
                    held = ref[zz, 0, rows, :].astype(f32)
                    ref[zz, 0, rows, :] = (traded(k, zz) + held).astype(bf16)
                else:
                    for yy in range(2):
                        ref[zz, yy, rows, :] = part_sum(zz, yy, rows, (ref,)).astype(bf16)

            pl.when(there)(step)
            out.send(
                THIN if early[k] else CHAIN, there,
                remote(lambda: piece, lambda: piece, lambda: chain_sems.at[k - sum(straight[:k]), zz + way], peer),
            )

    def home(k):
        rows = rows_of(k)
        way = 0 if early[k] else slice(None)
        pl.when(z > 0)(lambda: landed(rzu.at[z, way, rows, :], chain_sems.at[k - sum(straight[:k]), z + 1]))
        pl.when(z < last)(lambda: landed(rzd.at[z, way, rows, :], chain_sems.at[k - sum(straight[:k]), z]))
        if early[k]:
            held = rzu[z, 0, rows, :].astype(f32) + rzd[z, 0, rows, :].astype(f32)
            out_ref[rows, :] = (traded(k, z) + held).astype(bf16)
            local(out_ref.at[rows], out_hbm.at[rows], 6).start()
            return
        ysend[rows, :] = part_sum(z, 1 - y, rows, (rzu, rzd)).astype(bf16)
        out.send(
            HOME, None,
            remote(
                lambda: ysend.at[rows, :], lambda: ry.at[rows, :], lambda: y_sems.at[k - sum(early[:k])], over
            ),
        )

    def total(k):
        if early[k]:
            return
        rows = rows_of(k)
        mine = part_sum(z, y, rows, (rzu, rzd))
        landed(ry.at[rows, :], y_sems.at[k - sum(early[:k])])
        out_ref[rows, :] = (mine + ry[rows, :].astype(f32)).astype(bf16)
        local(out_ref.at[rows], out_hbm.at[rows], 6).start()

    def spread(k):
        rows = rows_of(k)
        turn = sum(straight[:k])
        for i in range(depth):
            zz = jnp.where(2 * z < depth, last - i, i)

            def step():
                dsend[zz, rows, :] = traded(k, zz).astype(bf16)

            pl.when(zz != z)(step)
            out.send(
                SPREAD, zz != z,
                remote(
                    lambda: dsend.at[zz, rows, :], lambda: dr.at[z, rows, :],
                    lambda: spread_sems.at[turn, z], lambda: index_of(zz, y, c),
                ),
            )

    def collect(k):
        rows = rows_of(k)
        held = traded(k, z)
        for i in range(1, depth):
            src = (z + i) % depth
            landed(dr.at[src, rows, :], spread_sems.at[sum(straight[:k]), src])
            held = held + dr[src, rows, :].astype(f32)
        out_ref[rows, :] = held.astype(bf16)
        local(out_ref.at[rows], out_hbm.at[rows], 6).start()

    def scatter_point(k, p):
        if straight[k]:
            if p == 0:
                spread(k)
            elif p == depth - 1:
                collect(k)
            return
        if p == 0 and not early[k]:
            twin_sums(k)
        if p < depth - 1:
            chain(k, p)
        else:
            home(k)

    def send_gate_grads():
        turned = ggcol[...].T
        for b in range(devices):
            ggs[b] = turned[b : b + 1]
        ggr[me] = ggs[me]
        for peer in range(devices):
            out.send(
                BACK, peer != me,
                remote(
                    lambda peer=peer: ggs.at[peer], lambda: ggr.at[me], lambda: gg_sem,
                    lambda peer=peer: peer,
                ),
            )

    def take_gate_grads():
        landed(ggr.at[pl.ds(0, devices - 1)], gg_sem)
        held = ggr[...].reshape(devices, tok)
        for k in range(ids_ref.shape[0]):
            hot = ids_ref[k : k + 1] == expert
            picked = jnp.sum(jnp.where(hot, held, 0.0), axis=0, keepdims=True)
            ggo_ref[k : k + 1] = picked.astype(bf16)
        results[1].start()

    def gates_out(k):
        for copy in plan_copies:
            copy.wait()
        send_gates()

        @pl.when(z == 0)
        def _():
            rzu[...] = jnp.zeros_like(rzu)

        @pl.when(z == last)
        def _():
            rzd[...] = jnp.zeros_like(rzd)

    def ready(k):
        finish(k)
        if k == 0:
            take_gates()
            landed(w1, local_sems.at[1])
            weight_copies[2].wait()

    steps = dict(
        own=own, gates=gates_out, relay=relay, cross=cross, finish=ready, fwd=forward,
        wg=weights, trade=trade, sc=scatter_point, total=total, ggout=lambda k: send_gate_grads(),
        ggin=lambda k: take_gate_grads(),
    )
    for name, *rest in order:
        steps[name](*rest)

    def rows_in(flags, want):
        return sum(size for (_, size), flag in zip(chunks, flags) if flag == want)

    def sent_blocks(zz):
        ends = (zz < depth - 1) + (zz > 0)
        passed, widened = depth, 1 + ends
        for off in range(1, depth):
            mid = off < depth - 1
            below, above = zz >= off, zz + off < depth
            passed += below * (2 + (zz < depth - 1 and mid)) + above * (2 + (zz > 0 and mid))
            widened += 2 * below * (1 + (zz < depth - 1 and mid))
            widened += 2 * above * (1 + (zz > 0 and mid))
        out.sent(OWN, buf.at[pl.ds(0, 2 + ends)])
        out.sent(GATE, gbuf.at[pl.ds(0, 2 + ends)])
        out.sent(FLAT, gbuf.at[pl.ds(0, widened if wide[0] else passed)])
        for group, count, want in ((PASS, passed, False), (WIDE, widened, True)):
            if rows_in(wide, want):
                out.sent(group, buf.at[pl.ds(0, count), :, pl.ds(0, rows_in(wide, want))])

    for zz in range(depth):
        pl.when(z == zz)(lambda: sent_blocks(zz))
    out.sent(PAIR, rc)
    late, soon = rows_in(early, False), rows_in(early, True)
    direct = rows_in(straight, True)
    if late:
        out.sent(HOME, ysend.at[pl.ds(0, late)])
    if soon:
        out.sent(TRADE, xsend.at[:, pl.ds(0, soon)])
    if depth > 1 and late:
        out.sent(CHAIN, rzu.at[pl.ds(0, depth - 1), :, pl.ds(0, late)])
    if depth > 1 and soon > direct:
        out.sent(THIN, rzu.at[pl.ds(0, depth - 1), 0, pl.ds(0, soon - direct)])
    if depth > 1 and direct:
        out.sent(SPREAD, dr.at[pl.ds(0, depth - 1), pl.ds(0, direct)])
    out.sent(BACK, ggs.at[pl.ds(0, devices - 1)])
    for copy in results:
        copy.wait()


def fused_grads(x, dy, gates, ids, table, gate_w, up_w, down_w, devices, home_cap, rep_cap):
    depth = devices // 4
    tok, width = x.shape
    hidden = down_w.shape[0]
    f32, bf16 = jnp.float32, jnp.bfloat16
    n = len(row_chunks(tok))
    most = max(size for _, size in row_chunks(tok))
    vmem, dma = pltpu.VMEM, pltpu.SemaphoreType.DMA
    hbm = pl.BlockSpec(memory_space=pltpu.HBM)
    shape = jax.ShapeDtypeStruct
    outs = pl.pallas_call(
        lambda *refs: fused_kernel(depth, step_order(depth, n), home_cap, rep_cap, *refs),
        out_shape=[
            shape((tok, width), bf16), shape(gates.shape, bf16), shape(gate_w.shape, bf16),
            shape(up_w.shape, bf16), shape(down_w.shape, bf16),
        ],
        in_specs=[hbm] * 8,
        out_specs=[hbm] * 5,
        scratch_shapes=[
            vmem((tok, width), bf16), vmem(gates.shape, bf16), vmem(gate_w.shape, bf16),
            vmem(up_w.shape, bf16), vmem(down_w.shape, bf16),
            vmem((devices, 2, tok, width), bf16), vmem((devices, devices, tok), bf16),
            vmem((tok, 128), f32), vmem((tok, 128), f32),
            vmem((devices, 1, tok), f32), vmem((devices, 1, tok), f32),
            vmem((width, 2 * hidden), bf16), vmem((hidden, width), bf16),
            vmem((2, devices, most, 2 * hidden), bf16), vmem((2, devices, most, hidden), bf16),
            vmem((width, 2 * hidden), f32), vmem((hidden, width), f32),
            vmem((depth, 2, 2, tok, width), bf16), vmem((depth, 2, tok, width), bf16),
            vmem((depth, 2, tok, width), bf16), vmem((depth, 2, tok, width), bf16),
            vmem((tok, width), bf16), vmem((tok, width), bf16),
            vmem((depth, tok, width), bf16), vmem((depth, tok, width), bf16),
            vmem((depth, tok, width), bf16), vmem((depth, tok, width), bf16),
            vmem(gates.shape, bf16), vmem(ids.shape, ids.dtype),
            pltpu.SMEM(table.shape, table.dtype),
            dma((12,)), dma((12,)), dma((n, devices // 2)), dma((n,)), dma, dma,
            dma((sum(unit_counts(tok, devices)),)), dma((max(1, n - sum(STRAIGHT)), depth + 1)),
            dma((max(1, n - sum(PAIR_FIRST)),)), dma((max(1, sum(PAIR_FIRST)), depth)),
            dma((devices // 2,)), dma((max(1, sum(STRAIGHT)), depth)),
        ],
        compiler_params=pltpu.CompilerParams(
            collective_id=0, has_side_effects=True, vmem_limit_bytes=VMEM_GRANT
        ),
    )(x, dy, gates, ids, table, gate_w, up_w, down_w)
    return store_all(outs)


def store_kernel(n, cuts, *refs):
    src, dst, held, (load_sems, store_sems) = refs[:n], refs[n : 2 * n], refs[2 * n : -2], refs[-2:]
    loads, stores = [], []
    for i in range(n):
        step = src[i].shape[0] // cuts[i]
        for j in range(cuts[i]):
            rows = pl.ds(j * step, step)
            m = len(loads)
            loads.append(
                pltpu.make_async_copy(src[i].at[rows], held[i].at[rows], load_sems.at[m])
            )
            stores.append(
                pltpu.make_async_copy(held[i].at[rows], dst[i].at[rows], store_sems.at[m])
            )
    for copy in loads:
        copy.start()
    for load, store in zip(loads, stores):
        load.wait()
        store.start()
    for copy in stores:
        copy.wait()


def store_all(arrays):
    n = len(arrays)
    cuts = [4 if v.shape[0] >= 256 and v.shape[0] % 64 == 0 else 1 for v in arrays]
    hbm = pl.BlockSpec(memory_space=pltpu.HBM)
    return pl.pallas_call(
        lambda *refs: store_kernel(n, cuts, *refs),
        out_shape=[jax.ShapeDtypeStruct(v.shape, v.dtype) for v in arrays],
        in_specs=[hbm] * n,
        out_specs=[hbm] * n,
        scratch_shapes=[pltpu.VMEM(v.shape, v.dtype) for v in arrays]
        + [pltpu.SemaphoreType.DMA((sum(cuts),))] * 2,
        compiler_params=pltpu.CompilerParams(vmem_limit_bytes=VMEM_GRANT),
    )(*arrays)


def keep_plan(gates, row_ids, replica_table, source, devices, home_cap, rep_cap):
    tok = row_ids.shape[0]
    experts = jnp.arange(devices, dtype=jnp.int32)
    hot = row_ids[:, :, None] == experts[None, None, :]
    named = jnp.any(hot, axis=1)
    dense_gate = jnp.sum(jnp.where(hot, gates.astype(jnp.float32)[:, :, None], 0.0), axis=1)
    copies = 1 + jnp.sum((replica_table[:, None] == experts[None, :]).astype(jnp.int32), axis=0)
    order = jnp.arange(tok, dtype=jnp.int32)
    earlier = (order[:, None] > order[None, :]).astype(jnp.bfloat16)
    rank = jnp.dot(earlier, named.astype(jnp.bfloat16), preferred_element_type=jnp.float32)
    many = copies.astype(jnp.float32)[None, :]
    position = jnp.floor((rank + 0.5) / many)
    turn = rank + source.astype(jnp.float32)
    copy_index = turn - many * jnp.floor((turn + 0.5) / many)
    limit = jnp.where(copy_index < 0.5, float(home_cap), float(rep_cap))
    kept = named & (position < limit)
    return jnp.where(kept, dense_gate, 0.0).astype(jnp.bfloat16)


def row_grads(x, dy, gate, gate_w, up_w, down_w):
    a = jnp.dot(x, gate_w, preferred_element_type=jnp.float32)
    b = jnp.dot(x, up_w, preferred_element_type=jnp.float32)
    u = lax.dot_general(dy, down_w, contract_cols, preferred_element_type=jnp.float32)
    sig = jax.nn.sigmoid(a)
    act = a * sig
    product = act * b
    hidden = product.astype(jnp.bfloat16).astype(jnp.float32)
    gate_grad = jnp.sum(hidden * u, axis=1, keepdims=True)
    gate_grad = jnp.where(gate > 0, gate_grad, 0.0)
    hg = (gate * product).astype(jnp.bfloat16)
    gu = gate * u
    da = (gu * b * sig * (1.0 + a * (1.0 - sig))).astype(jnp.bfloat16)
    db = (gu * act).astype(jnp.bfloat16)
    dx = lax.dot_general(da, gate_w, contract_cols, preferred_element_type=jnp.float32)
    dx = dx + lax.dot_general(db, up_w, contract_cols, preferred_element_type=jnp.float32)
    return gate_grad, hg, da, db, dx


def weight_grads(x, dy, hg, da, db):
    dwg = lax.dot_general(x, da, contract_rows, preferred_element_type=jnp.float32)
    dwu = lax.dot_general(x, db, contract_rows, preferred_element_type=jnp.float32)
    dwd = lax.dot_general(hg, dy, contract_rows, preferred_element_type=jnp.float32)
    return dwg, dwu, dwd


def on_device(tokens_in, grad_out, gates, expert_ids, replica_table, w_gate, w_up, w_down):
    devices = lax.axis_size("expert")
    me = lax.axis_index("expert")
    tok, width = tokens_in.shape
    home_cap = max(2, 5 * tok * TOP // (4 * devices))
    rep_cap = max(2, tok * TOP // (2 * devices))
    if devices * tok <= ROWS_PER_CHUNK and devices % 16 == 0 and devices <= 128 and tok % 128 == 0:
        outs = fused_grads(
            tokens_in, grad_out, gates.T, expert_ids.T, replica_table, w_gate[0], w_up[0], w_down[0],
            devices, home_cap, rep_cap,
        )
        return (outs[0], outs[1].T, *[g[None] for g in outs[2:]])
    kept_gate = keep_plan(gates, expert_ids, replica_table, me, devices, home_cap, rep_cap)
    lanes = -(-devices // 128) * 128
    kept_gate = jnp.pad(kept_gate, ((0, 0), (0, lanes - devices)))
    payload = jnp.concatenate([tokens_in, grad_out, kept_gate], axis=1)
    chunks = max(1, devices * tok // ROWS_PER_CHUNK)
    part = tok // chunks
    mine = jnp.arange(lanes, dtype=jnp.int32)[None, :] == me
    backs, sums = [], None
    for c in range(chunks):
        rows = lax.all_gather(payload[c * part : (c + 1) * part], "expert", axis=0, tiled=True)
        gate = jnp.sum(
            jnp.where(mine, rows[:, 2 * width :].astype(jnp.float32), 0.0),
            axis=1,
            keepdims=True,
        )
        gate_grad, hg, da, db, dx = row_grads(
            rows[:, :width], rows[:, width : 2 * width], gate, w_gate[0], w_up[0], w_down[0]
        )
        spread = jnp.where(mine, gate_grad, 0.0).astype(jnp.bfloat16)
        back = jnp.concatenate([dx.astype(jnp.bfloat16), spread], axis=1)
        backs.append(lax.psum_scatter(back, "expert", scatter_dimension=0, tiled=True))
        grads = weight_grads(rows[:, :width], rows[:, width : 2 * width], hg, da, db)
        sums = grads if sums is None else [p + q for p, q in zip(sums, grads)]
        if c + 1 < chunks:
            payload, sums = lax.optimization_barrier((payload, sums))
    back = jnp.concatenate(backs, axis=0)
    experts = jnp.arange(devices, dtype=jnp.int32)
    hot = expert_ids[:, :, None] == experts[None, None, :]
    picked = jnp.where(hot, back[:, None, width : width + devices].astype(jnp.float32), 0.0)
    grad_gates = jnp.sum(picked, axis=2).astype(jnp.bfloat16)
    return (back[:, :width], grad_gates, *[g.astype(jnp.bfloat16)[None] for g in sums])


def solution(mesh):
    return jax.shard_map(
        on_device,
        mesh=mesh,
        in_specs=(
            P(("groups", "expert"), None),
            P(("groups", "expert"), None),
            P(("groups", "expert"), None),
            P(("groups", "expert"), None),
            P("groups"),
            P("expert", None, None),
            P("expert", None, None),
            P("expert", None, None),
        ),
        out_specs=(
            P(("groups", "expert"), None),
            P(("groups", "expert"), None),
            P(("groups", "expert"), None, None),
            P(("groups", "expert"), None, None),
            P(("groups", "expert"), None, None),
        ),
        check_vma=False,
    )
```

```python
import jax
import jax.numpy as jnp
from jax import lax
from jax.experimental import pallas as pl
from jax.experimental.pallas import tpu as pltpu
from jax.sharding import PartitionSpec as P

TOP = 8
ROWS_PER_CHUNK = 4096

contract_rows = (((0,), (0,)), ((), ()))
contract_cols = (((1,), (1,)), ((), ()))

MESH = pl.DeviceIdType.MESH
VMEM_GRANT = 58 * 2**20


def place(depth):
    me = lax.axis_index("expert")
    z, y, c = me // 4, (me // 2) % 2, me % 2
    return me, z, y, c, depth - 1


def index_of(z, y, c):
    return (z * 2 + y) * 2 + c


def greet(z, y, c, last):
    sem = pltpu.get_barrier_semaphore()

    def hello(peer):
        pl.semaphore_signal(sem, inc=1, device_id={"expert": peer}, device_id_type=MESH)

    hello(index_of(z, y, 1 - c))
    hello(index_of(z, 1 - y, c))
    pl.when(z > 0)(lambda: hello(index_of(z - 1, y, c)))
    pl.when(z < last)(lambda: hello(index_of(z + 1, y, c)))
    pl.semaphore_wait(sem, 2 + (z > 0).astype(jnp.int32) + (z < last).astype(jnp.int32))


class Sender:
    def __init__(self, sems):
        self.sems = sems

    def send(self, group, cond, make):
        if cond is None:
            make(self.sems.at[group]).start()
        else:
            pl.when(cond)(lambda: make(self.sems.at[group]).start())

    def sent(self, group, ref):
        pltpu.make_async_copy(ref, ref, self.sems.at[group]).wait()


def remote(src, dst, recv_sem, peer):
    return lambda send_sem: pltpu.make_async_remote_copy(
        src_ref=src(), dst_ref=dst(), send_sem=send_sem, recv_sem=recv_sem(),
        device_id={"expert": peer()}, device_id_type=MESH,
    )


def landed(ref, sem):
    pltpu.make_async_copy(ref, ref, sem).wait()


TUNED_DEPTH = 4
TUNED_SHARES = (32, 16, 16, 16, 16, 16, 16)
PAIR_FIRST = (False, True, True, True, True, True, True)
STRAIGHT = (False, True, True, True, True, True, True)
BOTH_COLUMNS = (False, True, False, False, False, False, True)
TUNED = [
    ("own", 0), ("gates", 0), ("own", 3), ("own", 1), ("relay", 0, 1), ("relay", 0, -1),
    ("own", 2), ("cross", 1, 0), ("cross", 0, 1), ("relay", 0, -2), ("relay", 0, 2),
    ("cross", 0, -1), ("relay", 2, 1), ("relay", 2, -1), ("cross", 1, -1), ("relay", 3, 1),
    ("relay", 0, 3), ("relay", 0, -3), ("relay", 1, -1), ("relay", 3, -1), ("cross", 1, 1),
    ("cross", 0, 0), ("relay", 1, 1), ("cross", 0, -2), ("own", 4), ("cross", 0, 2),
    ("cross", 1, 2), ("cross", 0, 3), ("cross", 2, 1), ("relay", 3, 2), ("cross", 0, -3),
    ("relay", 2, -2), ("cross", 2, -1), ("cross", 1, -2), ("relay", 1, -2), ("relay", 1, 2),
    ("relay", 3, -2), ("cross", 3, 0), ("relay", 2, 2), ("own", 5), ("finish", 0), ("fwd", 0, 0),
    ("fwd", 0, 1), ("relay", 4, 1), ("relay", 2, -3), ("cross", 1, 3), ("own", 6),
    ("cross", 2, -2), ("trade", 0), ("wg", 0, 0), ("relay", 1, 3), ("relay", 1, -3), ("sc", 0, 0),
    ("cross", 2, 2), ("cross", 3, -2), ("cross", 1, -3), ("cross", 4, 0), ("relay", 3, -3),
    ("relay", 3, 3), ("relay", 4, -1), ("relay", 2, 3), ("cross", 2, -3), ("cross", 2, 0),
    ("finish", 1), ("fwd", 1, 0), ("cross", 3, 2), ("relay", 5, -1), ("relay", 5, 1),
    ("cross", 5, 0), ("relay", 4, 2), ("wg", 0, 1), ("cross", 3, -1), ("wg", 1, 1),
    ("cross", 6, 0), ("cross", 2, 3), ("cross", 3, 1), ("relay", 4, -2), ("wg", 1, 0),
    ("relay", 6, -1), ("trade", 1), ("cross", 3, -3), ("sc", 0, 1), ("cross", 3, 3),
    ("finish", 2), ("fwd", 2, 0), ("cross", 5, -1), ("relay", 4, 3), ("relay", 5, 2),
    ("wg", 2, 0), ("relay", 6, 1), ("cross", 4, 1), ("relay", 4, -3), ("cross", 6, 1),
    ("relay", 5, -2), ("finish", 3), ("fwd", 3, 0), ("relay", 5, 3), ("cross", 6, -1),
    ("wg", 2, 1), ("wg", 3, 1), ("cross", 4, 2), ("relay", 5, -3), ("trade", 2), ("cross", 4, -3),
    ("relay", 6, 2), ("cross", 4, -1), ("cross", 4, 3), ("relay", 6, -2), ("cross", 4, -2),
    ("sc", 1, 0), ("cross", 5, 1), ("trade", 3), ("wg", 3, 0), ("sc", 1, 1), ("cross", 5, -2),
    ("cross", 6, 2), ("cross", 6, -2), ("cross", 5, 2), ("sc", 0, 2), ("relay", 6, -3),
    ("finish", 4), ("cross", 5, 3), ("cross", 5, -3), ("fwd", 4, 0), ("finish", 5), ("fwd", 5, 0),
    ("cross", 6, -3), ("wg", 4, 1), ("relay", 6, 3), ("sc", 1, 2), ("sc", 1, 3), ("sc", 2, 0),
    ("trade", 4), ("cross", 6, 3), ("sc", 2, 1), ("wg", 4, 0), ("sc", 3, 0), ("trade", 5),
    ("sc", 3, 1), ("sc", 2, 2), ("finish", 6), ("fwd", 6, 0), ("ggout", 0), ("sc", 4, 0),
    ("wg", 5, 0), ("trade", 6), ("sc", 5, 0), ("sc", 0, 3), ("sc", 4, 1), ("sc", 6, 0),
    ("wg", 6, 0), ("sc", 5, 1), ("wg", 5, 1), ("ggin", 0), ("total", 1), ("sc", 3, 2),
    ("sc", 3, 3), ("sc", 4, 2), ("sc", 5, 2), ("total", 3), ("sc", 2, 3), ("total", 0),
    ("sc", 6, 1), ("sc", 4, 3), ("sc", 6, 2), ("sc", 5, 3), ("wg", 6, 1), ("sc", 6, 3),
    ("total", 5), ("total", 6), ("total", 2), ("total", 4),
]


def row_chunks(tok):
    whole = sum(TUNED_SHARES)
    sizes = [tok * share // whole for share in TUNED_SHARES]
    return [(sum(sizes[:k]), size) for k, size in enumerate(sizes)]


def unit_counts(tok, devices):
    whole = devices % 8 != 0
    return [1 if whole or size * devices <= 256 else 2 for _, size in row_chunks(tok)]


def step_order(depth, n):
    if depth == TUNED_DEPTH:
        return TUNED
    steps = [("own", 0), ("gates", 0)]
    for k in range(n):
        steps += [("own", k)] if k else []
        for d in range(1, depth):
            steps += [("relay", k, -d), ("relay", k, d)]
        steps += [("cross", k, d) for d in range(1 - depth, depth)]
        steps += [("finish", k), ("fwd", k, 0), ("fwd", k, 1), ("wg", k, 0), ("wg", k, 1)]
        steps += [("trade", k)] + [("sc", k, p) for p in range(depth)] + [("total", k)]
    return steps + [("ggout", 0), ("ggin", 0)]


def fused_kernel(
    depth, order, home_cap, rep_cap,
    x_hbm, dy_hbm, gates_hbm, ids_hbm, table_hbm, wg_hbm, wu_hbm, wd_hbm,
    out_hbm, ggo_hbm, dwg_hbm, dwu_hbm, dwd_hbm,
    out_ref, ggo_ref, dwg_ref, dwu_ref, dwd_ref,
    buf, gbuf, gcol, ggcol, ggs, ggr, w1, wd, dadb, hgb, acc1, acc2, dx, rc, rzu, rzd, ysend, ry, xsend, xr, dsend, dr,
    gates_ref, ids_ref, table_ref,
    local_sems, send_sems, recv_sems, pair_sems, gate_sem, gg_sem, twin_sems, chain_sems,
    y_sems, x_sems, gate_sems, spread_sems,
):
    f32, bf16 = jnp.float32, jnp.bfloat16
    devices = 4 * depth
    early, wide, straight = PAIR_FIRST, BOTH_COLUMNS, STRAIGHT
    counts = unit_counts(x_hbm.shape[0], devices)
    me, z, y, c, last = place(depth)
    tok, width = x_hbm.shape
    hidden = wd_hbm.shape[0]
    chunks = row_chunks(tok)
    lanes = gcol.shape[1]

    def local(src, dst, i):
        return pltpu.make_async_copy(src, dst, local_sems.at[i])

    own_copies = [local(x_hbm, buf.at[me, 0], 0), local(dy_hbm, buf.at[me, 1], 0)]
    weight_copies = [
        local(wg_hbm, w1.at[:, pl.ds(0, hidden)], 1),
        local(wu_hbm, w1.at[:, pl.ds(hidden, hidden)], 1),
        local(wd_hbm, wd, 2),
    ]
    plan_copies = [
        local(gates_hbm, gates_ref, 3), local(ids_hbm, ids_ref, 4), local(table_hbm, table_ref, 5),
    ]
    results = [
        local(out_ref, out_hbm, 6), local(ggo_ref, ggo_hbm, 7), local(dwg_ref, dwg_hbm, 8),
        local(dwu_ref, dwu_hbm, 9), local(dwd_ref, dwd_hbm, 10),
    ]
    for copy in own_copies + plan_copies + weight_copies:
        copy.start()
    greet(z, y, c, last)
    landed(buf.at[me], local_sems.at[0])

    out = Sender(send_sems)
    up = lambda: index_of(z + 1, y, c)
    down = lambda: index_of(z - 1, y, c)
    over = lambda: index_of(z, 1 - y, c)
    twin = lambda: index_of(z, y, 1 - c)
    can_up, can_down = z < last, z > 0
    half = depth // 2

    def rows_of(k):
        return pl.ds(*chunks[k])

    OWN, PASS, WIDE, PAIR, CHAIN, THIN, TRADE, HOME, GATE, BACK, FLAT, SPREAD = range(12)

    def push(group, cond, b, k, peer):
        block = lambda: buf.at[b(), :, rows_of(k)]
        sem = (lambda: pair_sems.at[k]) if peer is twin else (lambda: recv_sems.at[k, b() // 2])
        out.send(group, cond, remote(block, block, sem, peer))
        if k == 0 and group != OWN:
            push_gates(FLAT, cond, b, peer)

    def push_gates(group, cond, b, peer):
        sem = (lambda: gate_sem) if peer is twin else (lambda: gate_sems.at[b() // 2])
        out.send(group, cond, remote(lambda: gbuf.at[b()], lambda: gbuf.at[b()], sem, peer))

    def arrived(k, b):
        landed(buf.at[b, :, rows_of(k)], recv_sems.at[k, b // 2])
        if k == 0:
            landed(gbuf.at[b], gate_sems.at[b // 2])

    def own(k):
        mine = lambda: me
        push(OWN, None, mine, k, over)
        push(OWN, can_up, mine, k, up)
        push(OWN, can_down, mine, k, down)
        push(OWN, None, mine, k, twin)

    def relay(k, off):
        cond = z + off >= 0 if off < 0 else z + off <= last
        more, onward = (can_up, up) if off < 0 else (can_down, down)
        b = lambda: index_of(z + off, y, c)
        pl.when(cond)(lambda: arrived(k, b()))
        group = WIDE if wide[k] else PASS
        if abs(off) < depth - 1:
            push(group, cond & more, b, k, onward)
        if not wide[k]:
            push(group, cond, b, k, over)
        push(group, cond, b, k, twin)

    def cross(k, off):
        b = lambda: index_of(z + off, 1 - y, c)
        cond = None if off == 0 else z + off >= 0 if off < 0 else z + off <= last
        group = WIDE if wide[k] else PASS
        if cond is None:
            arrived(k, b())
        else:
            pl.when(cond)(lambda: arrived(k, b()))
        if wide[k] and abs(off) < depth - 1:
            if off <= 0:
                push(group, can_up if cond is None else cond & can_up, b, k, up)
            if off >= 0:
                push(group, can_down if cond is None else cond & can_down, b, k, down)
        push(group, cond, b, k, twin)

    def finish(k):
        landed(buf.at[pl.ds(0, devices // 2), :, rows_of(k)], pair_sems.at[k])

    lane = lax.broadcasted_iota(jnp.int32, (tok, lanes), 1)
    expert = lax.broadcasted_iota(jnp.int32, (devices, tok), 0)

    def send_gates():
        copies = jnp.ones((devices, tok), f32)
        for d in range(devices):
            copies = copies + jnp.where(expert == table_ref[d], 1.0, 0.0)
        dense = jnp.zeros((devices, tok), f32)
        named = jnp.zeros((devices, tok), f32)
        for k in range(ids_ref.shape[0]):
            hot = ids_ref[k : k + 1] == expert
            dense = jnp.where(hot, gates_ref[k : k + 1].astype(f32), dense)
            named = jnp.where(hot, 1.0, named)
        row = lax.broadcasted_iota(jnp.int32, (tok, tok), 0)
        col = lax.broadcasted_iota(jnp.int32, (tok, tok), 1)
        earlier = jnp.where(row < col, 1.0, 0.0).astype(bf16)
        rank = jnp.dot(named.astype(bf16), earlier, preferred_element_type=f32)
        position = jnp.floor((rank + 0.5) / copies)
        turn = rank + me.astype(f32)
        copy_index = turn - copies * jnp.floor((turn + 0.5) / copies)
        limit = jnp.where(copy_index < 0.5, float(home_cap), float(rep_cap))
        gbuf[me] = jnp.where((named > 0.5) & (position < limit), dense, 0.0).astype(bf16)
        for cond, peer in ((None, over), (can_up, up), (can_down, down), (None, twin)):
            push_gates(GATE, cond, lambda: me, peer)

    def take_gates():
        landed(gbuf.at[pl.ds(0, devices // 2)], gate_sem)
        flat = gbuf[...].reshape(devices * devices, tok)
        r = lax.broadcasted_iota(jnp.int32, (devices * devices, lanes), 0)
        l = lax.broadcasted_iota(jnp.int32, (devices * devices, lanes), 1)
        pick = jnp.where(r == l * devices + me, 1.0, 0.0).astype(bf16)
        gcol[...] = lax.dot_general(flat, pick, contract_rows, preferred_element_type=f32)
        ggcol[...] = jnp.zeros_like(ggcol)

    def units(k):
        if counts[k] == 1:
            return [(0, depth)]
        first = jnp.where(z < half, half, 0)
        return [(first, half), (half - first, half)]

    def forward(k, u):
        if u >= len(units(k)):
            return
        r0, size = chunks[k]
        p0, planes = units(k)[u]
        nb = planes * 4
        at = pl.ds(p0 * 4, nb)
        rows = pl.ds(r0, size)
        x = buf[at, 0, rows, :].reshape(nb * size, width)
        dy = buf[at, 1, rows, :].reshape(nb * size, width)
        g = gcol[rows, :]
        spot = lane[:size]
        gate = jnp.concatenate(
            [
                jnp.sum(jnp.where(spot == p0 * 4 + j, g, 0.0), axis=1, keepdims=True)
                for j in range(nb)
            ],
            axis=0,
        )
        ab = jnp.dot(x, w1[...], preferred_element_type=f32)
        a, b = ab[:, :hidden], ab[:, hidden:]
        v = lax.dot_general(dy, wd[...], contract_cols, preferred_element_type=f32)
        sig = jax.nn.sigmoid(a)
        act = a * sig
        product = act * b
        gate_grad = jnp.sum(product.astype(bf16).astype(f32) * v, axis=1, keepdims=True)
        gate_grad = jnp.where(gate > 0, gate_grad, 0.0)
        gu = gate * v
        da = (gu * b * sig * (1.0 + a * (1.0 - sig))).astype(bf16)
        db = (gu * act).astype(bf16)
        both_grads = jnp.concatenate([da, db], axis=1)
        hgb[k % 2, at, pl.ds(0, size), :] = (gate * product).astype(bf16).reshape(nb, size, hidden)
        dadb[k % 2, at, pl.ds(0, size), :] = both_grads.reshape(nb, size, 2 * hidden)
        back = lax.dot_general(both_grads, w1[...], contract_cols, preferred_element_type=f32)
        dx[pl.ds(p0, planes), :, :, rows, :] = back.astype(bf16).reshape(
            planes, 2, 2, size, width
        )
        held = ggcol[rows, :]
        for j in range(nb):
            held = jnp.where(spot == p0 * 4 + j, gate_grad[j * size : (j + 1) * size], held)
        ggcol[rows, :] = held
        for j, (q0, span) in enumerate(twin_parts(k)):
            if counts[k] == 1 or j == u:
                src = lambda: dx.at[pl.ds(q0, span), :, 1 - c, rows, :]
                dst = lambda: rc.at[pl.ds(q0, span), :, rows, :]
                out.send(PAIR, None, remote(src, dst, lambda: twin_sems.at[k, j], twin))

    def twin_parts(k):
        if depth % 2:
            return [(0, depth)]
        first = jnp.where(z < half, half, 0)
        return [(first, half), (half - first, half)]

    def twin_sum(k, j):
        q0, span = twin_parts(k)[j]
        landed(rc.at[pl.ds(q0, span), :, rows_of(k), :], twin_sems.at[k, j])

    def twin_sums(k):
        for j in range(len(twin_parts(k))):
            twin_sum(k, j)

    tile = 256 if width % 256 == 0 else 128

    def weight_tile(k, j, which):
        size = chunks[k][1]
        rows = rows_of(k)
        cols = pl.ds(j * tile, tile)
        first, final = k == 0, k == len(chunks) - 1
        if which == 0:
            x = buf[:, 0, rows, cols].reshape(devices * size, tile)
            d = dadb[k % 2, :, pl.ds(0, size), :].reshape(devices * size, 2 * hidden)
            v = lax.dot_general(x, d, contract_rows, preferred_element_type=f32)
            if not first:
                v = v + acc1[cols, :]
            if final:
                dwg_ref[cols, :] = v[:, :hidden].astype(bf16)
                dwu_ref[cols, :] = v[:, hidden:].astype(bf16)
            else:
                acc1[cols, :] = v
        else:
            dy = buf[:, 1, rows, cols].reshape(devices * size, tile)
            h = hgb[k % 2, :, pl.ds(0, size), :].reshape(devices * size, hidden)
            v = lax.dot_general(h, dy, contract_rows, preferred_element_type=f32)
            if not first:
                v = v + acc2[:, cols]
            if final:
                dwd_ref[:, cols] = v.astype(bf16)
            else:
                acc2[:, cols] = v

    def weights(k, which):
        for j in range(width // tile):
            weight_tile(k, j, which)
        if k == len(chunks) - 1:
            for copy in (results[2:4], results[4:])[which]:
                copy.start()

    def part_sum(zz, yy, rows, extra):
        total = dx[zz, yy, c, rows, :].astype(f32) + rc[zz, yy, rows, :].astype(f32)
        for ref in extra:
            total = total + ref[zz, yy, rows, :].astype(f32)
        return total

    def trade(k):
        if not early[k]:
            return
        rows = rows_of(k)
        parts = len(twin_parts(k))
        for i in range(depth):
            if i * parts % depth == 0:
                twin_sum(k, i * parts // depth)
            zz = jnp.where(2 * z < depth, last - i, i)
            xsend[zz, rows, :] = part_sum(zz, 1 - y, rows, ()).astype(bf16)
            out.send(
                TRADE, None,
                remote(
                    lambda zz=zz: xsend.at[zz, rows, :], lambda zz=zz: xr.at[zz, rows, :],
                    lambda zz=zz: x_sems.at[sum(early[:k]), zz], over,
                ),
            )

    def traded(k, zz):
        landed(xr.at[zz, rows_of(k), :], x_sems.at[sum(early[:k]), zz])
        return part_sum(zz, y, rows_of(k), ()) + xr[zz, rows_of(k), :].astype(f32)

    def chain(k, p):
        rows = rows_of(k)
        for there, zz, ref, way, has, peer in (
            (z <= p, z + last - p, rzu, 1, z > 0, up),
            (last - z <= p, z + p - last, rzd, 0, z < last, down),
        ):
            piece = ref.at[zz, 0, rows, :] if early[k] else ref.at[zz, :, rows, :]

            def step():
                pl.when(has)(lambda: landed(piece, chain_sems.at[k - sum(straight[:k]), zz + way]))
                if early[k]:
                    held = ref[zz, 0, rows, :].astype(f32)
                    ref[zz, 0, rows, :] = (traded(k, zz) + held).astype(bf16)
                else:
                    for yy in range(2):
                        ref[zz, yy, rows, :] = part_sum(zz, yy, rows, (ref,)).astype(bf16)

            pl.when(there)(step)
            out.send(
                THIN if early[k] else CHAIN, there,
                remote(lambda: piece, lambda: piece, lambda: chain_sems.at[k - sum(straight[:k]), zz + way], peer),
            )

    def home(k):
        rows = rows_of(k)
        way = 0 if early[k] else slice(None)
        pl.when(z > 0)(lambda: landed(rzu.at[z, way, rows, :], chain_sems.at[k - sum(straight[:k]), z + 1]))
        pl.when(z < last)(lambda: landed(rzd.at[z, way, rows, :], chain_sems.at[k - sum(straight[:k]), z]))
        if early[k]:
            held = rzu[z, 0, rows, :].astype(f32) + rzd[z, 0, rows, :].astype(f32)
            out_ref[rows, :] = (traded(k, z) + held).astype(bf16)
            local(out_ref.at[rows], out_hbm.at[rows], 6).start()
            return
        ysend[rows, :] = part_sum(z, 1 - y, rows, (rzu, rzd)).astype(bf16)
        out.send(
            HOME, None,
            remote(
                lambda: ysend.at[rows, :], lambda: ry.at[rows, :], lambda: y_sems.at[k - sum(early[:k])], over
            ),
        )

    def total(k):
        if early[k]:
            return
        rows = rows_of(k)
        mine = part_sum(z, y, rows, (rzu, rzd))
        landed(ry.at[rows, :], y_sems.at[k - sum(early[:k])])
        out_ref[rows, :] = (mine + ry[rows, :].astype(f32)).astype(bf16)
        local(out_ref.at[rows], out_hbm.at[rows], 6).start()

    def spread(k):
        rows = rows_of(k)
        turn = sum(straight[:k])
        for i in range(depth):
            zz = jnp.where(2 * z < depth, last - i, i)

            def step():
                dsend[zz, rows, :] = traded(k, zz).astype(bf16)

            pl.when(zz != z)(step)
            out.send(
                SPREAD, zz != z,
                remote(
                    lambda: dsend.at[zz, rows, :], lambda: dr.at[z, rows, :],
                    lambda: spread_sems.at[turn, z], lambda: index_of(zz, y, c),
                ),
            )

    def collect(k):
        rows = rows_of(k)
        held = traded(k, z)
        for i in range(1, depth):
            src = (z + i) % depth
            landed(dr.at[src, rows, :], spread_sems.at[sum(straight[:k]), src])
            held = held + dr[src, rows, :].astype(f32)
        out_ref[rows, :] = held.astype(bf16)
        local(out_ref.at[rows], out_hbm.at[rows], 6).start()

    def scatter_point(k, p):
        if straight[k]:
            if p == 0:
                spread(k)
            elif p == depth - 1:
                collect(k)
            return
        if p == 0 and not early[k]:
            twin_sums(k)
        if p < depth - 1:
            chain(k, p)
        else:
            home(k)

    def send_gate_grads():
        turned = ggcol[...].T
        for b in range(devices):
            ggs[b] = turned[b : b + 1]
        ggr[me] = ggs[me]
        for peer in range(devices):
            out.send(
                BACK, peer != me,
                remote(
                    lambda peer=peer: ggs.at[peer], lambda: ggr.at[me], lambda: gg_sem,
                    lambda peer=peer: peer,
                ),
            )

    def take_gate_grads():
        landed(ggr.at[pl.ds(0, devices - 1)], gg_sem)
        held = ggr[...].reshape(devices, tok)
        for k in range(ids_ref.shape[0]):
            hot = ids_ref[k : k + 1] == expert
            picked = jnp.sum(jnp.where(hot, held, 0.0), axis=0, keepdims=True)
            ggo_ref[k : k + 1] = picked.astype(bf16)
        results[1].start()

    def gates_out(k):
        for copy in plan_copies:
            copy.wait()
        send_gates()

        @pl.when(z == 0)
        def _():
            rzu[...] = jnp.zeros_like(rzu)

        @pl.when(z == last)
        def _():
            rzd[...] = jnp.zeros_like(rzd)

    def ready(k):
        finish(k)
        if k == 0:
            take_gates()
            landed(w1, local_sems.at[1])
            weight_copies[2].wait()

    steps = dict(
        own=own, gates=gates_out, relay=relay, cross=cross, finish=ready, fwd=forward,
        wg=weights, trade=trade, sc=scatter_point, total=total, ggout=lambda k: send_gate_grads(),
        ggin=lambda k: take_gate_grads(),
    )
    for name, *rest in order:
        steps[name](*rest)

    def rows_in(flags, want):
        return sum(size for (_, size), flag in zip(chunks, flags) if flag == want)

    def sent_blocks(zz):
        ends = (zz < depth - 1) + (zz > 0)
        passed, widened = depth, 1 + ends
        for off in range(1, depth):
            mid = off < depth - 1
            below, above = zz >= off, zz + off < depth
            passed += below * (2 + (zz < depth - 1 and mid)) + above * (2 + (zz > 0 and mid))
            widened += 2 * below * (1 + (zz < depth - 1 and mid))
            widened += 2 * above * (1 + (zz > 0 and mid))
        out.sent(OWN, buf.at[pl.ds(0, 2 + ends)])
        out.sent(GATE, gbuf.at[pl.ds(0, 2 + ends)])
        out.sent(FLAT, gbuf.at[pl.ds(0, widened if wide[0] else passed)])
        for group, count, want in ((PASS, passed, False), (WIDE, widened, True)):
            if rows_in(wide, want):
                out.sent(group, buf.at[pl.ds(0, count), :, pl.ds(0, rows_in(wide, want))])

    for zz in range(depth):
        pl.when(z == zz)(lambda: sent_blocks(zz))
    out.sent(PAIR, rc)
    late, soon = rows_in(early, False), rows_in(early, True)
    direct = rows_in(straight, True)
    if late:
        out.sent(HOME, ysend.at[pl.ds(0, late)])
    if soon:
        out.sent(TRADE, xsend.at[:, pl.ds(0, soon)])
    if depth > 1 and late:
        out.sent(CHAIN, rzu.at[pl.ds(0, depth - 1), :, pl.ds(0, late)])
    if depth > 1 and soon > direct:
        out.sent(THIN, rzu.at[pl.ds(0, depth - 1), 0, pl.ds(0, soon - direct)])
    if depth > 1 and direct:
        out.sent(SPREAD, dr.at[pl.ds(0, depth - 1), pl.ds(0, direct)])
    out.sent(BACK, ggs.at[pl.ds(0, devices - 1)])
    for copy in results:
        copy.wait()


def fused_grads(x, dy, gates, ids, table, gate_w, up_w, down_w, devices, home_cap, rep_cap):
    depth = devices // 4
    tok, width = x.shape
    hidden = down_w.shape[0]
    f32, bf16 = jnp.float32, jnp.bfloat16
    n = len(row_chunks(tok))
    most = max(size for _, size in row_chunks(tok))
    vmem, dma = pltpu.VMEM, pltpu.SemaphoreType.DMA
    hbm = pl.BlockSpec(memory_space=pltpu.HBM)
    shape = jax.ShapeDtypeStruct
    outs = pl.pallas_call(
        lambda *refs: fused_kernel(depth, step_order(depth, n), home_cap, rep_cap, *refs),
        out_shape=[
            shape((tok, width), bf16), shape(gates.shape, bf16), shape(gate_w.shape, bf16),
            shape(up_w.shape, bf16), shape(down_w.shape, bf16),
        ],
        in_specs=[hbm] * 8,
        out_specs=[hbm] * 5,
        scratch_shapes=[
            vmem((tok, width), bf16), vmem(gates.shape, bf16), vmem(gate_w.shape, bf16),
            vmem(up_w.shape, bf16), vmem(down_w.shape, bf16),
            vmem((devices, 2, tok, width), bf16), vmem((devices, devices, tok), bf16),
            vmem((tok, 128), f32), vmem((tok, 128), f32),
            vmem((devices, 1, tok), f32), vmem((devices, 1, tok), f32),
            vmem((width, 2 * hidden), bf16), vmem((hidden, width), bf16),
            vmem((2, devices, most, 2 * hidden), bf16), vmem((2, devices, most, hidden), bf16),
            vmem((width, 2 * hidden), f32), vmem((hidden, width), f32),
            vmem((depth, 2, 2, tok, width), bf16), vmem((depth, 2, tok, width), bf16),
            vmem((depth, 2, tok, width), bf16), vmem((depth, 2, tok, width), bf16),
            vmem((tok, width), bf16), vmem((tok, width), bf16),
            vmem((depth, tok, width), bf16), vmem((depth, tok, width), bf16),
            vmem((depth, tok, width), bf16), vmem((depth, tok, width), bf16),
            vmem(gates.shape, bf16), vmem(ids.shape, ids.dtype),
            pltpu.SMEM(table.shape, table.dtype),
            dma((12,)), dma((12,)), dma((n, devices // 2)), dma((n,)), dma, dma,
            dma((n, 2)), dma((max(1, n - sum(STRAIGHT)), depth + 1)),
            dma((max(1, n - sum(PAIR_FIRST)),)), dma((max(1, sum(PAIR_FIRST)), depth)),
            dma((devices // 2,)), dma((max(1, sum(STRAIGHT)), depth)),
        ],
        compiler_params=pltpu.CompilerParams(
            collective_id=0, has_side_effects=True, vmem_limit_bytes=VMEM_GRANT
        ),
    )(x, dy, gates, ids, table, gate_w, up_w, down_w)
    return store_all(outs)


def store_kernel(n, cuts, *refs):
    src, dst, held, (load_sems, store_sems) = refs[:n], refs[n : 2 * n], refs[2 * n : -2], refs[-2:]
    loads, stores = [], []
    for i in range(n):
        step = src[i].shape[0] // cuts[i]
        for j in range(cuts[i]):
            rows = pl.ds(j * step, step)
            m = len(loads)
            loads.append(
                pltpu.make_async_copy(src[i].at[rows], held[i].at[rows], load_sems.at[m])
            )
            stores.append(
                pltpu.make_async_copy(held[i].at[rows], dst[i].at[rows], store_sems.at[m])
            )
    for copy in loads:
        copy.start()
    for load, store in zip(loads, stores):
        load.wait()
        store.start()
    for copy in stores:
        copy.wait()


def store_all(arrays):
    n = len(arrays)
    cuts = [4 if v.shape[0] >= 256 and v.shape[0] % 64 == 0 else 1 for v in arrays]
    hbm = pl.BlockSpec(memory_space=pltpu.HBM)
    return pl.pallas_call(
        lambda *refs: store_kernel(n, cuts, *refs),
        out_shape=[jax.ShapeDtypeStruct(v.shape, v.dtype) for v in arrays],
        in_specs=[hbm] * n,
        out_specs=[hbm] * n,
        scratch_shapes=[pltpu.VMEM(v.shape, v.dtype) for v in arrays]
        + [pltpu.SemaphoreType.DMA((sum(cuts),))] * 2,
        compiler_params=pltpu.CompilerParams(vmem_limit_bytes=VMEM_GRANT),
    )(*arrays)


def keep_plan(gates, row_ids, replica_table, source, devices, home_cap, rep_cap):
    tok = row_ids.shape[0]
    experts = jnp.arange(devices, dtype=jnp.int32)
    hot = row_ids[:, :, None] == experts[None, None, :]
    named = jnp.any(hot, axis=1)
    dense_gate = jnp.sum(jnp.where(hot, gates.astype(jnp.float32)[:, :, None], 0.0), axis=1)
    copies = 1 + jnp.sum((replica_table[:, None] == experts[None, :]).astype(jnp.int32), axis=0)
    order = jnp.arange(tok, dtype=jnp.int32)
    earlier = (order[:, None] > order[None, :]).astype(jnp.bfloat16)
    rank = jnp.dot(earlier, named.astype(jnp.bfloat16), preferred_element_type=jnp.float32)
    many = copies.astype(jnp.float32)[None, :]
    position = jnp.floor((rank + 0.5) / many)
    turn = rank + source.astype(jnp.float32)
    copy_index = turn - many * jnp.floor((turn + 0.5) / many)
    limit = jnp.where(copy_index < 0.5, float(home_cap), float(rep_cap))
    kept = named & (position < limit)
    return jnp.where(kept, dense_gate, 0.0).astype(jnp.bfloat16)


def row_grads(x, dy, gate, gate_w, up_w, down_w):
    a = jnp.dot(x, gate_w, preferred_element_type=jnp.float32)
    b = jnp.dot(x, up_w, preferred_element_type=jnp.float32)
    u = lax.dot_general(dy, down_w, contract_cols, preferred_element_type=jnp.float32)
    sig = jax.nn.sigmoid(a)
    act = a * sig
    product = act * b
    hidden = product.astype(jnp.bfloat16).astype(jnp.float32)
    gate_grad = jnp.sum(hidden * u, axis=1, keepdims=True)
    gate_grad = jnp.where(gate > 0, gate_grad, 0.0)
    hg = (gate * product).astype(jnp.bfloat16)
    gu = gate * u
    da = (gu * b * sig * (1.0 + a * (1.0 - sig))).astype(jnp.bfloat16)
    db = (gu * act).astype(jnp.bfloat16)
    dx = lax.dot_general(da, gate_w, contract_cols, preferred_element_type=jnp.float32)
    dx = dx + lax.dot_general(db, up_w, contract_cols, preferred_element_type=jnp.float32)
    return gate_grad, hg, da, db, dx


def weight_grads(x, dy, hg, da, db):
    dwg = lax.dot_general(x, da, contract_rows, preferred_element_type=jnp.float32)
    dwu = lax.dot_general(x, db, contract_rows, preferred_element_type=jnp.float32)
    dwd = lax.dot_general(hg, dy, contract_rows, preferred_element_type=jnp.float32)
    return dwg, dwu, dwd


def on_device(tokens_in, grad_out, gates, expert_ids, replica_table, w_gate, w_up, w_down):
    devices = lax.axis_size("expert")
    me = lax.axis_index("expert")
    tok, width = tokens_in.shape
    home_cap = max(2, 5 * tok * TOP // (4 * devices))
    rep_cap = max(2, tok * TOP // (2 * devices))
    if devices * tok <= ROWS_PER_CHUNK and devices % 16 == 0 and devices <= 128 and tok % 128 == 0:
        outs = fused_grads(
            tokens_in, grad_out, gates.T, expert_ids.T, replica_table, w_gate[0], w_up[0], w_down[0],
            devices, home_cap, rep_cap,
        )
        return (outs[0], outs[1].T, *[g[None] for g in outs[2:]])
    kept_gate = keep_plan(gates, expert_ids, replica_table, me, devices, home_cap, rep_cap)
    lanes = -(-devices // 128) * 128
    kept_gate = jnp.pad(kept_gate, ((0, 0), (0, lanes - devices)))
    payload = jnp.concatenate([tokens_in, grad_out, kept_gate], axis=1)
    chunks = max(1, devices * tok // ROWS_PER_CHUNK)
    part = tok // chunks
    mine = jnp.arange(lanes, dtype=jnp.int32)[None, :] == me
    backs, sums = [], None
    for c in range(chunks):
        rows = lax.all_gather(payload[c * part : (c + 1) * part], "expert", axis=0, tiled=True)
        gate = jnp.sum(
            jnp.where(mine, rows[:, 2 * width :].astype(jnp.float32), 0.0),
            axis=1,
            keepdims=True,
        )
        gate_grad, hg, da, db, dx = row_grads(
            rows[:, :width], rows[:, width : 2 * width], gate, w_gate[0], w_up[0], w_down[0]
        )
        spread = jnp.where(mine, gate_grad, 0.0).astype(jnp.bfloat16)
        back = jnp.concatenate([dx.astype(jnp.bfloat16), spread], axis=1)
        backs.append(lax.psum_scatter(back, "expert", scatter_dimension=0, tiled=True))
        grads = weight_grads(rows[:, :width], rows[:, width : 2 * width], hg, da, db)
        sums = grads if sums is None else [p + q for p, q in zip(sums, grads)]
        if c + 1 < chunks:
            payload, sums = lax.optimization_barrier((payload, sums))
    back = jnp.concatenate(backs, axis=0)
    experts = jnp.arange(devices, dtype=jnp.int32)
    hot = expert_ids[:, :, None] == experts[None, None, :]
    picked = jnp.where(hot, back[:, None, width : width + devices].astype(jnp.float32), 0.0)
    grad_gates = jnp.sum(picked, axis=2).astype(jnp.bfloat16)
    return (back[:, :width], grad_gates, *[g.astype(jnp.bfloat16)[None] for g in sums])


def solution(mesh):
    return jax.shard_map(
        on_device,
        mesh=mesh,
        in_specs=(
            P(("groups", "expert"), None),
            P(("groups", "expert"), None),
            P(("groups", "expert"), None),
            P(("groups", "expert"), None),
            P("groups"),
            P("expert", None, None),
            P("expert", None, None),
            P("expert", None, None),
        ),
        out_specs=(
            P(("groups", "expert"), None),
            P(("groups", "expert"), None),
            P(("groups", "expert"), None, None),
            P(("groups", "expert"), None, None),
            P(("groups", "expert"), None, None),
        ),
        check_vma=False,
    )
```
